512 devices in a mesh: kp: 32 (over x, y, core), ka: 16 (over z).
Axes of the slice: x: 4, y: 4, z: 16, core: 2. Of those that a mesh axis runs over, the one named last changes fastest.
Arguments:
- band_form: bfloat16 [64, 24, 2048], P('ka'), may hold values from -0.71875 to 0.71875
- interp_coef: bfloat16 [64, 128, 128], P('ka'), may hold values from -0.5 to 0.5
- screen: bfloat16 [64, 2048, 32], P('ka', 'kp'), may hold values from -0.3984375 to 0.3984375
- coulomb: float32 [2048], replicated, may hold values from 0.3 to 3
- shift_map: int32 [64, 2048], replicated, may hold values from 0 to 2047, each once within a row
- grid_order: int32 [64], replicated, may hold values from 0 to 63, each once
- energies: float32 [8192], P('ka'), may hold values from 0.18101934 to 0.543058
- initial: float32 [8192, 64], P('ka'), may hold values from -6 to 6
Outputs:
- kernel: bfloat16 [8192, 8192], P('ka', 'kp')
- subspace: float32 [8192, 64], P('ka')
The draws below stay inside these ranges and needn't reach their ends.
All inputs are finite; a program needn't handle non-finite values.
Results may differ from the reference program's by a relative error of at most 0.02.
Values may be sent and summed in bfloat16 or wider, within the bound.
No kernel may reach another device: no remote copies, remote signals or barrier semaphores. Data moves between devices by JAX's collectives and lax.ppermute only.
A program may use at most 64 MiB of HBM per device.

```python
import math
import jax
import jax.numpy as jnp
from jax import lax

NV = 8
NC = 16
NG = 2048
NE = 32
NVEC = 64
STEPS = 2
GRID_Y = 8
NB = 24
NVC = 128
NK = 64
NQ = 64
N = 8192


def shard_levels(stream_key, extent, split, low, largest):
    loudness = 1.0
    for axis_at, parts in split:
        draws = jax.random.uniform(jax.random.fold_in(jax.random.fold_in(stream_key, 6), axis_at), (parts,), jnp.float32, low / len(split), largest / len(split))
        loudness = loudness * jnp.repeat(jnp.exp(draws), extent[axis_at] // parts).reshape((-1,) + (1,) * (len(extent) - 1 - axis_at))
    return loudness


def centred(rng, dims, scale, bound, split=(), held_as=jnp.bfloat16):
    level = shard_levels(rng, dims, split, -0.22, 0.18) if split else 1.0
    entries = jax.random.normal(rng, dims, jnp.float32) * scale * level
    return jnp.minimum(jnp.maximum(entries, -bound), bound).astype(held_as)


def setup_inputs(seed: int = 0) -> dict:
    arg_keys = jax.random.split(jax.random.key(seed), 9)
    return {
        "band_form": centred(arg_keys[0], (NK, NB, NG), (0.12 * (2048 // NG) ** 0.125), 0.71875, ((0, 16),)),
        "interp_coef": centred(arg_keys[1], (NK, NVC, NVC), NVC ** -0.5, 0.5, ((0, 16),)),
        "screen": centred(arg_keys[2], (NQ, NG, NE), 0.0625, 0.3984375, ((0, 16), (1, 32))),
        "coulomb": jnp.clip(jnp.exp(jax.random.uniform(arg_keys[3], (NG,), jnp.float32, math.log(0.3), math.log(3.0))), 0.3, 3.0),
        "shift_map": jax.vmap(lambda own: jax.random.permutation(own, NG))(jax.random.split(arg_keys[4], NQ)).reshape((NQ, NG)).astype(jnp.int32),
        "grid_order": jax.random.permutation(arg_keys[5], NK).astype(jnp.int32),
        "energies": jnp.clip(0.18101934 + 0.36203864 * jax.random.uniform(arg_keys[6], (N,), jnp.float32) ** shard_levels(arg_keys[6], (N,), ((0, 16),), -0.2, 0.2), 0.18101934, 0.543058),
        "initial": centred(arg_keys[7], (N, NVEC), 1.0, 6.0, ((0, 16),), jnp.float32),
    }


def pair_block(near_form, mapped, near_coef, far_coef, screen_cols, coulomb):
    valence = (near_form[:NV, None, :].astype(jnp.float32) * mapped[None, :NV, :].astype(jnp.float32)).reshape(NV * NV, -1).astype(jnp.bfloat16)
    conduction = (near_form[NV:, None, :].astype(jnp.float32) * mapped[None, NV:, :].astype(jnp.float32)).reshape(NC * NC, -1).astype(jnp.bfloat16)
    scaled = (coulomb[None, :] * valence.astype(jnp.float32)).astype(jnp.bfloat16)
    direct = jnp.dot(conduction.astype(jnp.float32), scaled.T.astype(jnp.float32), preferred_element_type=jnp.float32)
    left = jnp.dot(conduction.astype(jnp.float32), screen_cols.astype(jnp.float32), preferred_element_type=jnp.float32)
    right = jnp.dot(valence.astype(jnp.float32), screen_cols.astype(jnp.float32), preferred_element_type=jnp.float32)
    direct = direct + jnp.dot(left.astype(jnp.float32), right.T.astype(jnp.float32), precision=lax.Precision.HIGHEST, preferred_element_type=jnp.float32)
    block = direct.reshape(NC, NC, NV, NV).transpose(2, 0, 3, 1).reshape(NV * NC, NV * NC).astype(jnp.bfloat16)
    half = jnp.dot(block.astype(jnp.float32), far_coef.astype(jnp.float32), preferred_element_type=jnp.float32).astype(jnp.bfloat16)
    return jnp.dot(near_coef.T.astype(jnp.float32), half.astype(jnp.float32), preferred_element_type=jnp.float32).astype(jnp.bfloat16)

def reference(band_form, interp_coef, screen, coulomb, shift_map, grid_order, energies, initial):
    grid_x = NK // GRID_Y
    cell_x = grid_order // GRID_Y
    cell_y = grid_order % GRID_Y
    pairs = NV * NC

    def kernel_row(point):
        transfers = ((cell_x[point] - cell_x) % grid_x * GRID_Y + (cell_y[point] - cell_y) % GRID_Y).astype(jnp.int32)
        maps = jnp.take(shift_map, transfers, axis=0)
        mapped = jnp.take_along_axis(band_form, maps[:, None, :], axis=2)
        columns = jnp.take(screen, transfers, axis=0)
        blocks = jax.vmap(pair_block, in_axes=(None, 0, None, 0, 0, None))(band_form[point], mapped, interp_coef[point], interp_coef, columns, coulomb)
        return blocks.transpose(1, 0, 2).reshape(pairs, NK * pairs)
    kernel = lax.map(kernel_row, jnp.arange(NK, dtype=jnp.int32)).reshape(NK * pairs, NK * pairs)
    vectors = initial
    for repeat in range(STEPS):
        images = energies[:, None] * vectors + jnp.dot(kernel.astype(jnp.float32), vectors.astype(jnp.bfloat16).astype(jnp.float32), preferred_element_type=jnp.float32)
        correlation = jnp.dot(images.T.astype(jnp.float32), images.astype(jnp.float32), precision=lax.Precision.HIGHEST, preferred_element_type=jnp.float32) / (NK * pairs)
        factor = jnp.linalg.cholesky(correlation)
        vectors = jax.scipy.linalg.solve_triangular(factor, images.T, lower=True).T
    return (kernel, vectors)
```

```python
import jax
import jax.numpy as jnp
from jax import lax
from jax.experimental import pallas as pl
from jax.experimental.pallas import tpu as pltpu
from jax.sharding import PartitionSpec as P

NV, NC = 8, 16
GRID_Y = 8
GRID_X = 8
BF, F32 = jnp.bfloat16, jnp.float32
HIGH = lax.Precision.HIGHEST
VM = pl.BlockSpec(memory_space=pltpu.VMEM)
SM = pl.BlockSpec(memory_space=pltpu.SMEM)


def pick_kernel(t_ref, g_ref, o_ref, rolled):
    def roll_one(h, _):
        x = g_ref[h, 0:64, :].astype(F32)
        rolled[0, h] = x.astype(BF)
        for s in range(1, 4):
            rolled[s, h] = pltpu.roll(x, 32 * s, 1).astype(BF)
        return 0

    lax.fori_loop(0, 16, roll_one, 0)
    lane_block = lax.broadcasted_iota(jnp.int32, (64, 128), 1) // 32

    def dest(d, _):
        for j in range(2):
            acc = None
            for i in range(4):
                q = t_ref[(2 * d + j) * 4 + i]
                tile = rolled[(i - q) & 3, q >> 2].astype(F32)
                acc = tile if acc is None else jnp.where(lane_block == i, tile, acc)
            o_ref[d, 64 * j : 64 * j + 64, :] = acc.astype(BF)
        half = d & 1
        plane = d >> 1
        o_ref[d, 128:152, :] = g_ref[plane, pl.ds(pl.multiple_of(64 + 24 * half, 8), 24), :]
        o_ref[d, 152:160, :] = g_ref[plane, pl.ds(pl.multiple_of(112 + 8 * half, 8), 8), :]
        o_ref[d, 160:168, :] = g_ref[plane, 128:136, :]
        return 0

    lax.fori_loop(0, 32, dest, 0)


def pick(gathered, table):
    return pl.pallas_call(
        pick_kernel,
        out_shape=jax.ShapeDtypeStruct((32, 168, 128), BF),
        in_specs=[pl.BlockSpec(memory_space=pltpu.SMEM), pl.BlockSpec(memory_space=pltpu.VMEM)],
        out_specs=pl.BlockSpec(memory_space=pltpu.VMEM),
        scratch_shapes=[pltpu.VMEM((4, 16, 64, 128), BF)],
        name="pick",
    )(table, gathered)


def pair_kernel(t_ref, r_ref, near_ref, coef_ref, coul_ref, map_ref, o_ref, y_ref, far, farc, cond, val, scaled, expand):
    step = pl.program_id(0)
    j = step // 4
    i = step % 4

    @pl.when(step == 0)
    def _():
        lane = lax.broadcasted_iota(jnp.int32, (24, 128), 1)
        for m in range(16):
            lo = r_ref[2 * m, 128:152, :].astype(F32)
            hi = r_ref[2 * m + 1, 128:152, :].astype(F32)
            far[0, m] = jnp.where(lane < 64, lo, pltpu.roll(hi, 64, 1))
            far[1, m] = jnp.where(lane < 64, pltpu.roll(lo, 64, 1), hi)
        rows = r_ref[:, 152:160, :].reshape(256, 128)
        out_row = lax.broadcasted_iota(jnp.int32, (128, 256), 0)
        in_row = lax.broadcasted_iota(jnp.int32, (128, 256), 1)
        for k in range(2):
            sel = (in_row == (out_row // 4) * 8 + k * 4 + out_row % 4).astype(F32).astype(BF)
            farc[k] = jnp.dot(sel, rows, preferred_element_type=F32).astype(BF)
        row = lax.broadcasted_iota(jnp.int32, (64, 1024), 0)
        col = lax.broadcasted_iota(jnp.int32, (64, 1024), 1)
        expand[...] = (row == col // 16).astype(F32).astype(BF)

    def gather_chunk(m, _):
        idx = map_ref[0, pl.ds(m, 1), :]
        low = jnp.broadcast_to(idx & 127, (24, 128))
        high = jnp.broadcast_to(idx >> 7, (24, 128))
        acc = jnp.take_along_axis(far[j, 0], low, axis=1)
        for s in range(1, 16):
            acc = jnp.where(high == s, jnp.take_along_axis(far[j, s], low, axis=1), acc)
        cs = pl.ds(pl.multiple_of(m * 128, 128), 128)
        a = near_ref[i, :, cs].astype(F32)
        coul = coul_ref[pl.ds(m, 1), :]
        for c in range(NC):
            cond[c * 16 : c * 16 + 16, cs] = (a[8 + c : 9 + c, :] * acc[8:24, :]).astype(BF)
        for v in range(0, NV, 2):
            x = jnp.concatenate([a[v : v + 1, :] * acc[0:8, :], a[v + 1 : v + 2, :] * acc[0:8, :]], axis=0).astype(BF)
            val[v * 8 : v * 8 + 16, cs] = x
            scaled[v * 8 : v * 8 + 16, cs] = (coul * x.astype(F32)).astype(BF)
        return 0

    lax.fori_loop(0, 16, gather_chunk, 0)
    nt = (((1,), (1,)), ((), ()))
    cols = r_ref[:, pl.ds(pl.multiple_of(64 * j, 64), 64), :].reshape(2048, 128)
    left = jnp.dot(cond[...], cols, preferred_element_type=F32)
    right = jnp.dot(val[...], cols, preferred_element_type=F32)
    left = jnp.where(lax.broadcasted_iota(jnp.int32, (256, 128), 1) // 32 == i, left, 0.0)
    direct = lax.dot_general(cond[...], scaled[...], nt, preferred_element_type=F32)
    direct += lax.dot_general(left, right, nt, precision=lax.Precision.HIGHEST, preferred_element_type=F32)
    spread = jnp.dot(direct.astype(BF), expand[...], preferred_element_type=F32)
    r16 = lax.broadcasted_iota(jnp.int32, (256, 1024), 0) % 16
    c16 = lax.broadcasted_iota(jnp.int32, (256, 1024), 1) % 16
    spread = jnp.where(r16 == c16, spread, 0.0).astype(BF)
    group = (lax.broadcasted_iota(jnp.int32, (16, 256), 0) == lax.broadcasted_iota(jnp.int32, (16, 256), 1) // 16).astype(F32).astype(BF)
    wide = jnp.dot(group, spread, preferred_element_type=F32).astype(BF)
    block = jnp.concatenate([wide[:, v * 128 : v * 128 + 128] for v in range(NV)], axis=0)
    half = jnp.dot(block, farc[j], preferred_element_type=F32).astype(BF)
    tn = (((0,), (0,)), ((), ()))
    out = lax.dot_general(coef_ref[i], half, tn, preferred_element_type=F32).astype(BF)
    o_ref[pl.ds(pl.multiple_of(i * 128, 128), 128), pl.ds(pl.multiple_of(j * 128, 128), 128)] = out

    @pl.when(step == 7)
    def _():
        odd = t_ref[8] == 1
        both = r_ref[:, 160:168, :].reshape(256, 128).astype(F32)
        lane = lax.broadcasted_iota(jnp.int32, (256, 128), 1)
        other = pltpu.roll(both, 64, 1)
        first = jnp.where(lane < 64, jnp.where(odd, other, both), 0.0).astype(BF)
        second = jnp.where(lane < 64, 0.0, jnp.where(odd, both, other)).astype(BF)
        y = jnp.dot(o_ref[0:256, :], first, preferred_element_type=F32)
        y_ref[...] = y + jnp.dot(o_ref[256:512, :], second, preferred_element_type=F32)


def pair_blocks(table, received, near, coef, coulomb, shift_map):
    grid_spec = pltpu.PrefetchScalarGridSpec(
        num_scalar_prefetch=1,
        grid=(8,),
        in_specs=[
            pl.BlockSpec((32, 168, 128), lambda p, t: (0, 0, 0)),
            pl.BlockSpec((4, 24, 2048), lambda p, t: (0, 0, 0)),
            pl.BlockSpec((4, 128, 128), lambda p, t: (0, 0, 0)),
            pl.BlockSpec((16, 128), lambda p, t: (0, 0)),
            pl.BlockSpec((1, 16, 128), lambda p, t: (t[p], 0, 0)),
        ],
        out_specs=(pl.BlockSpec((512, 256), lambda p, t: (0, 0)), pl.BlockSpec((256, 128), lambda p, t: (0, 0))),
        scratch_shapes=[
            pltpu.VMEM((2, 16, 24, 128), F32),
            pltpu.VMEM((2, 128, 128), BF),
            pltpu.VMEM((256, 2048), BF),
            pltpu.VMEM((64, 2048), BF),
            pltpu.VMEM((64, 2048), BF),
            pltpu.VMEM((64, 1024), BF),
        ],
    )
    return pl.pallas_call(
        pair_kernel,
        grid_spec=grid_spec,
        out_shape=(jax.ShapeDtypeStruct((512, 256), BF), jax.ShapeDtypeStruct((256, 128), F32)),
        name="pairs",
    )(table, received, near, coef, coulomb, shift_map)


def split_kernel(x_ref, o_ref):
    lane = lax.broadcasted_iota(jnp.int32, (8, 128), 1)
    for m in range(16):
        x = x_ref[m]
        high = x.astype(BF).astype(F32)
        low = x - high
        o_ref[2 * m] = jnp.where(lane < 64, high, pltpu.roll(low, 64, 1)).astype(BF)
        o_ref[2 * m + 1] = jnp.where(lane < 64, pltpu.roll(high, 64, 1), low).astype(BF)


def split_parts(x):
    return pl.pallas_call(
        split_kernel,
        out_shape=jax.ShapeDtypeStruct((32, 8, 128), BF),
        in_specs=[VM],
        out_specs=VM,
        name="split",
    )(x)


TN = (((0,), (0,)), ((), ()))
NT = (((1,), (1,)), ((), ()))


def fold_rows(square):
    lane = lax.broadcasted_iota(jnp.int32, (32, 128), 1)
    return jnp.where(lane < 64, square[0:32], pltpu.roll(square[32:64], 64, 1))


def second_kernel(k_ref, x_ref, o_ref):
    x = x_ref[...].reshape(256, 128)
    lane = lax.broadcasted_iota(jnp.int32, (256, 128), 1)
    low = jnp.dot(k_ref[0:256, :], x, preferred_element_type=F32)
    high = jnp.dot(k_ref[256:512, :], x, preferred_element_type=F32)
    low = low + pltpu.roll(low, 64, 1)
    high = high + pltpu.roll(high, 64, 1)
    y = jnp.where(lane < 64, low, high)
    corr = lax.dot_general(x, x, TN, preferred_element_type=F32)
    corr = corr + pltpu.roll(corr, 64, 1)
    corr = fold_rows(corr[0:64] + corr[64:128])
    o_ref[:, 0:8, :] = y.reshape(32, 8, 128)
    o_ref[:, 8:9, :] = corr.reshape(32, 1, 128)


def second_product(kernel, x):
    return pl.pallas_call(
        second_kernel,
        out_shape=jax.ShapeDtypeStruct((32, 9, 128), F32),
        in_specs=[VM, VM],
        out_specs=VM,
        name="second",
    )(kernel, x)


def inverse_factor(packed, scale):
    lane = lax.broadcasted_iota(jnp.int32, (64, 128), 1)
    row = lax.broadcasted_iota(jnp.int32, (64, 128), 0)
    full = jnp.concatenate([packed, pltpu.roll(packed, 64, 1)], axis=0) * scale
    work = jnp.where(lane < 64, full, (lane - 64 == row).astype(F32))
    done = []
    tiles = [work[8 * t : 8 * t + 8] for t in range(8)]
    for j in range(64):
        t0 = j // 8
        top = jnp.broadcast_to(tiles[t0][:, j : j + 1], (8, 128))
        pivot = top[j % 8 : j % 8 + 1, :]
        r = lax.rsqrt(pivot)
        r = r * (1.5 - 0.5 * pivot * r * r)
        line = tiles[t0][j % 8 : j % 8 + 1, :] * r
        done.append(line)
        scaled = line * r
        for t in range(t0, 8):
            column = top if t == t0 else jnp.broadcast_to(tiles[t][:, j : j + 1], (8, 128))
            tiles[t] = tiles[t] - column * scaled
    return jnp.concatenate(done, axis=0)


def apply_inverse(x, inv):
    lane = lax.broadcasted_iota(jnp.int32, (64, 128), 1)
    upper = jnp.where(lane < 64, pltpu.roll(inv, 64, 1), 0.0)
    lower = jnp.where(lane < 64, 0.0, inv)
    both = jnp.concatenate([upper, lower], axis=0)
    return lax.dot_general(x, both, NT, precision=HIGH, preferred_element_type=F32)


def middle_kernel(g_ref, image_ref, corr_ref, *, scale):
    packed = g_ref[:, 8:9, :].reshape(32, 128)
    inv = inverse_factor(packed, scale)
    image = apply_inverse(g_ref[:, 0:8, :].reshape(256, 128), inv)
    image_ref[...] = image
    corr = lax.dot_general(image, image, TN, precision=HIGH, preferred_element_type=F32)
    corr = corr[0:64] + pltpu.roll(corr[64:128], 64, 1)
    corr_ref[...] = fold_rows(corr)


def middle(g, scale):
    return pl.pallas_call(
        lambda *refs: middle_kernel(*refs, scale=scale),
        out_shape=(jax.ShapeDtypeStruct((256, 128), F32), jax.ShapeDtypeStruct((32, 128), F32)),
        in_specs=[VM],
        out_specs=(VM, VM),
        name="middle",
    )(g)


def last_kernel(image_ref, corr_ref, o_ref, *, scale):
    packed = corr_ref[0]
    for m in range(1, 16):
        packed = packed + corr_ref[m]
    inv = inverse_factor(packed, scale)
    vectors = apply_inverse(image_ref[...], inv)
    o_ref[0:256, :] = vectors[:, 0:64]
    o_ref[256:512, :] = pltpu.roll(vectors, 64, 1)[:, 0:64]


def last(image, corr, scale):
    return pl.pallas_call(
        lambda *refs: last_kernel(*refs, scale=scale),
        out_shape=jax.ShapeDtypeStruct((512, 64), F32),
        in_specs=[VM, VM],
        out_specs=VM,
        name="last",
    )(image, corr)


def halves_in_lanes(rows, start):
    low = lax.dynamic_slice_in_dim(rows, start, 8, 0)
    high = lax.dynamic_slice_in_dim(rows, start + 256, 8, 0)
    return jnp.concatenate([low, high], axis=1)


def on_device(band_form, interp_coef, screen, coulomb, shift_map, grid_order, energies, initial):
    plane = lax.axis_index("ka")
    col = lax.axis_index("kp")
    cells_x, cells_y = grid_order // GRID_Y, grid_order % GRID_Y
    near_x = lax.dynamic_slice_in_dim(cells_x, 4 * plane, 4)
    near_y = lax.dynamic_slice_in_dim(cells_y, 4 * plane, 4)
    table = (near_x[None, :] - cells_x[:, None]) % GRID_X * GRID_Y + (near_y[None, :] - cells_y[:, None]) % GRID_Y
    table = table.reshape(256)

    columns = screen.transpose(1, 0, 2).reshape(64, 128)
    forms = lax.dynamic_slice_in_dim(band_form, 64 * col, 64, 2).reshape(2, 2, 24, 64).transpose(0, 2, 1, 3).reshape(48, 128)
    coefs = lax.dynamic_slice_in_dim(interp_coef, 4 * col, 4, 1).reshape(16, 128)
    starts = halves_in_lanes(initial, 8 * col)
    diagonal = halves_in_lanes(jnp.broadcast_to(energies[:, None], (512, 64)), 8 * col)
    piece = jnp.concatenate([columns, forms, coefs, starts.astype(BF)], axis=0)
    gathered = lax.all_gather(piece, "ka", axis=0, tiled=False)
    received = lax.all_to_all(pick(gathered, table), "kp", 0, 0, tiled=True)

    own = lax.dynamic_slice_in_dim(table, 8 * col, 8)
    scalars = jnp.concatenate([own, jnp.broadcast_to(col % 2, (8,)).astype(jnp.int32)])
    kernel, product = pair_blocks(
        scalars, received, band_form, interp_coef, coulomb.reshape(16, 128), shift_map.reshape(64, 16, 128)
    )
    product = lax.all_to_all(product.reshape(32, 8, 128), "kp", 0, 0, tiled=True)
    image = jnp.sum(product, axis=0) + diagonal * starts
    far = lax.all_to_all(split_parts(lax.all_gather(image, "ka", axis=0, tiled=False)), "kp", 0, 0, tiled=True)

    sums = jnp.sum(lax.all_to_all(second_product(kernel, far), "kp", 0, 0, tiled=True), axis=0)
    sums = sums + jnp.concatenate([diagonal * image, jnp.zeros((1, 128), F32)], axis=0)
    everyone = lax.all_to_all(jnp.broadcast_to(sums[None], (32, 9, 128)), "kp", 0, 0, tiled=True)
    scale = 1.0 / 8192
    image, corr = middle(everyone, scale)
    vectors = last(image, lax.all_gather(corr, "ka", axis=0, tiled=False), scale)
    return (kernel, vectors)


def solution(mesh):
    return jax.shard_map(
        on_device,
        mesh=mesh,
        in_specs=(
            P("ka", None, None),
            P("ka", None, None),
            P("ka", "kp", None),
            P(),
            P(),
            P(),
            P("ka"),
            P("ka", None),
        ),
        out_specs=(P("ka", "kp"), P("ka", None)),
        check_vma=False,
    )
```

```python
import jax
import jax.numpy as jnp
from jax import lax
from jax.experimental import pallas as pl
from jax.experimental.pallas import tpu as pltpu
from jax.sharding import PartitionSpec as P

NV, NC = 8, 16
GRID_Y = 8
GRID_X = 8
BF, F32 = jnp.bfloat16, jnp.float32
HIGH = lax.Precision.HIGHEST
VM = pl.BlockSpec(memory_space=pltpu.VMEM)
SM = pl.BlockSpec(memory_space=pltpu.SMEM)


def pick_kernel(t_ref, g_ref, o_ref, rolled):
    def roll_one(h, _):
        x = g_ref[h, 0:64, :].astype(F32)
        rolled[0, h] = x.astype(BF)
        for s in range(1, 4):
            rolled[s, h] = pltpu.roll(x, 32 * s, 1).astype(BF)
        return 0

    lax.fori_loop(0, 16, roll_one, 0)
    lane_block = lax.broadcasted_iota(jnp.int32, (64, 128), 1) // 32

    def dest(d, _):
        for j in range(2):
            acc = None
            for i in range(4):
                q = t_ref[(2 * d + j) * 4 + i]
                tile = rolled[(i - q) & 3, q >> 2].astype(F32)
                acc = tile if acc is None else jnp.where(lane_block == i, tile, acc)
            o_ref[d, 64 * j : 64 * j + 64, :] = acc.astype(BF)
        half = d & 1
        plane = d >> 1
        o_ref[d, 128:152, :] = g_ref[plane, pl.ds(pl.multiple_of(64 + 24 * half, 8), 24), :]
        o_ref[d, 152:160, :] = g_ref[plane, pl.ds(pl.multiple_of(112 + 8 * half, 8), 8), :]
        o_ref[d, 160:168, :] = g_ref[plane, 128:136, :]
        return 0

    lax.fori_loop(0, 32, dest, 0)


def pick(gathered, table):
    return pl.pallas_call(
        pick_kernel,
        out_shape=jax.ShapeDtypeStruct((32, 168, 128), BF),
        in_specs=[pl.BlockSpec(memory_space=pltpu.SMEM), pl.BlockSpec(memory_space=pltpu.VMEM)],
        out_specs=pl.BlockSpec(memory_space=pltpu.VMEM),
        scratch_shapes=[pltpu.VMEM((4, 16, 64, 128), BF)],
        name="pick",
    )(table, gathered)


def pair_kernel(t_ref, r_ref, near_ref, coef_ref, coul_ref, map_ref, o_ref, y_ref, far, farc, cond, val, scaled, expand):
    step = pl.program_id(0)
    j = step // 4
    i = step % 4

    @pl.when(step == 0)
    def _():
        lane = lax.broadcasted_iota(jnp.int32, (24, 128), 1)
        for m in range(16):
            lo = r_ref[2 * m, 128:152, :].astype(F32)
            hi = r_ref[2 * m + 1, 128:152, :].astype(F32)
            far[0, m] = jnp.where(lane < 64, lo, pltpu.roll(hi, 64, 1))
            far[1, m] = jnp.where(lane < 64, pltpu.roll(lo, 64, 1), hi)
        rows = r_ref[:, 152:160, :].reshape(256, 128)
        out_row = lax.broadcasted_iota(jnp.int32, (128, 256), 0)
        in_row = lax.broadcasted_iota(jnp.int32, (128, 256), 1)
        for k in range(2):
            sel = (in_row == (out_row // 4) * 8 + k * 4 + out_row % 4).astype(F32).astype(BF)
            farc[k] = jnp.dot(sel, rows, preferred_element_type=F32).astype(BF)
        row = lax.broadcasted_iota(jnp.int32, (64, 1024), 0)
        col = lax.broadcasted_iota(jnp.int32, (64, 1024), 1)
        expand[...] = (row == col // 16).astype(F32).astype(BF)

    def gather_chunk(m, _):
        idx = map_ref[0, pl.ds(m, 1), :]
        low = jnp.broadcast_to(idx & 127, (24, 128))
        high = jnp.broadcast_to(idx >> 7, (24, 128))
        acc = jnp.take_along_axis(far[j, 0], low, axis=1)
        for s in range(1, 16):
            acc = jnp.where(high == s, jnp.take_along_axis(far[j, s], low, axis=1), acc)
        cs = pl.ds(pl.multiple_of(m * 128, 128), 128)
        a = near_ref[i, :, cs].astype(F32)
        coul = coul_ref[pl.ds(m, 1), :]
        for c in range(NC):
            cond[c * 16 : c * 16 + 16, cs] = (a[8 + c : 9 + c, :] * acc[8:24, :]).astype(BF)
        for v in range(0, NV, 2):
            x = jnp.concatenate([a[v : v + 1, :] * acc[0:8, :], a[v + 1 : v + 2, :] * acc[0:8, :]], axis=0).astype(BF)
            val[v * 8 : v * 8 + 16, cs] = x
            scaled[v * 8 : v * 8 + 16, cs] = (coul * x.astype(F32)).astype(BF)
        return 0

    lax.fori_loop(0, 16, gather_chunk, 0, unroll=4)
    nt = (((1,), (1,)), ((), ()))
    cols = r_ref[:, pl.ds(pl.multiple_of(64 * j, 64), 64), :].reshape(2048, 128)
    left = jnp.dot(cond[...], cols, preferred_element_type=F32)
    right = jnp.dot(val[...], cols, preferred_element_type=F32)
    left = jnp.where(lax.broadcasted_iota(jnp.int32, (256, 128), 1) // 32 == i, left, 0.0)
    direct = lax.dot_general(cond[...], scaled[...], nt, preferred_element_type=F32)
    direct += lax.dot_general(left, right, nt, precision=lax.Precision.HIGHEST, preferred_element_type=F32)
    spread = jnp.dot(direct.astype(BF), expand[...], preferred_element_type=F32)
    r16 = lax.broadcasted_iota(jnp.int32, (256, 1024), 0) % 16
    c16 = lax.broadcasted_iota(jnp.int32, (256, 1024), 1) % 16
    spread = jnp.where(r16 == c16, spread, 0.0).astype(BF)
    group = (lax.broadcasted_iota(jnp.int32, (16, 256), 0) == lax.broadcasted_iota(jnp.int32, (16, 256), 1) // 16).astype(F32).astype(BF)
    wide = jnp.dot(group, spread, preferred_element_type=F32).astype(BF)
    block = jnp.concatenate([wide[:, v * 128 : v * 128 + 128] for v in range(NV)], axis=0)
    half = jnp.dot(block, farc[j], preferred_element_type=F32).astype(BF)
    tn = (((0,), (0,)), ((), ()))
    out = lax.dot_general(coef_ref[i], half, tn, preferred_element_type=F32).astype(BF)
    o_ref[pl.ds(pl.multiple_of(i * 128, 128), 128), pl.ds(pl.multiple_of(j * 128, 128), 128)] = out

    @pl.when(step == 7)
    def _():
        odd = t_ref[8] == 1
        both = r_ref[:, 160:168, :].reshape(256, 128).astype(F32)
        lane = lax.broadcasted_iota(jnp.int32, (256, 128), 1)
        other = pltpu.roll(both, 64, 1)
        first = jnp.where(lane < 64, jnp.where(odd, other, both), 0.0).astype(BF)
        second = jnp.where(lane < 64, 0.0, jnp.where(odd, both, other)).astype(BF)
        y = jnp.dot(o_ref[0:256, :], first, preferred_element_type=F32)
        y_ref[...] = y + jnp.dot(o_ref[256:512, :], second, preferred_element_type=F32)


def pair_blocks(table, received, near, coef, coulomb, shift_map):
    grid_spec = pltpu.PrefetchScalarGridSpec(
        num_scalar_prefetch=1,
        grid=(8,),
        in_specs=[
            VM,
            VM,
            VM,
            VM,
            pl.BlockSpec((1, 16, 128), lambda p, t: (t[p], 0, 0)),
        ],
        out_specs=(pl.BlockSpec((512, 256), lambda p, t: (0, 0)), pl.BlockSpec((256, 128), lambda p, t: (0, 0))),
        scratch_shapes=[
            pltpu.VMEM((2, 16, 24, 128), F32),
            pltpu.VMEM((2, 128, 128), BF),
            pltpu.VMEM((256, 2048), BF),
            pltpu.VMEM((64, 2048), BF),
            pltpu.VMEM((64, 2048), BF),
            pltpu.VMEM((64, 1024), BF),
        ],
    )
    return pl.pallas_call(
        pair_kernel,
        grid_spec=grid_spec,
        out_shape=(jax.ShapeDtypeStruct((512, 256), BF), jax.ShapeDtypeStruct((256, 128), F32)),
        name="pairs",
    )(table, received, near, coef, coulomb, shift_map)


def split_kernel(x_ref, o_ref):
    lane = lax.broadcasted_iota(jnp.int32, (8, 128), 1)
    for m in range(16):
        x = x_ref[m]
        high = x.astype(BF).astype(F32)
        low = x - high
        o_ref[2 * m] = jnp.where(lane < 64, high, pltpu.roll(low, 64, 1)).astype(BF)
        o_ref[2 * m + 1] = jnp.where(lane < 64, pltpu.roll(high, 64, 1), low).astype(BF)


def split_parts(x):
    return pl.pallas_call(
        split_kernel,
        out_shape=jax.ShapeDtypeStruct((32, 8, 128), BF),
        in_specs=[VM],
        out_specs=VM,
        name="split",
    )(x)


TN = (((0,), (0,)), ((), ()))
NT = (((1,), (1,)), ((), ()))


def fold_rows(square):
    lane = lax.broadcasted_iota(jnp.int32, (32, 128), 1)
    return jnp.where(lane < 64, square[0:32], pltpu.roll(square[32:64], 64, 1))


def second_kernel(k_ref, x_ref, o_ref):
    x = x_ref[...].reshape(256, 128)
    lane = lax.broadcasted_iota(jnp.int32, (256, 128), 1)
    low = jnp.dot(k_ref[0:256, :], x, preferred_element_type=F32)
    high = jnp.dot(k_ref[256:512, :], x, preferred_element_type=F32)
    low = low + pltpu.roll(low, 64, 1)
    high = high + pltpu.roll(high, 64, 1)
    y = jnp.where(lane < 64, low, high)
    corr = lax.dot_general(x, x, TN, preferred_element_type=F32)
    corr = corr + pltpu.roll(corr, 64, 1)
    corr = fold_rows(corr[0:64] + corr[64:128])
    o_ref[:, 0:8, :] = y.reshape(32, 8, 128)
    o_ref[:, 8:9, :] = corr.reshape(32, 1, 128)


def second_product(kernel, x):
    return pl.pallas_call(
        second_kernel,
        out_shape=jax.ShapeDtypeStruct((32, 9, 128), F32),
        in_specs=[VM, VM],
        out_specs=VM,
        name="second",
    )(kernel, x)


def inverse_factor(packed, scale):
    lane = lax.broadcasted_iota(jnp.int32, (64, 128), 1)
    row = lax.broadcasted_iota(jnp.int32, (64, 128), 0)
    full = jnp.concatenate([packed, pltpu.roll(packed, 64, 1)], axis=0) * scale
    work = jnp.where(lane < 64, full, (lane - 64 == row).astype(F32))
    done = []
    tiles = [work[8 * t : 8 * t + 8] for t in range(8)]
    for j in range(64):
        t0 = j // 8
        top = jnp.broadcast_to(tiles[t0][:, j : j + 1], (8, 128))
        pivot = top[j % 8 : j % 8 + 1, :]
        r = lax.rsqrt(pivot)
        r = r * (1.5 - 0.5 * pivot * r * r)
        line = tiles[t0][j % 8 : j % 8 + 1, :] * r
        done.append(line)
        scaled = line * r
        for t in range(t0, 8):
            column = top if t == t0 else jnp.broadcast_to(tiles[t][:, j : j + 1], (8, 128))
            tiles[t] = tiles[t] - column * scaled
    return jnp.concatenate(done, axis=0)


def lane_halves(inv):
    lane = lax.broadcasted_iota(jnp.int32, (64, 128), 1)
    return jnp.where(lane < 64, pltpu.roll(inv, 64, 1), 0.0), jnp.where(lane < 64, 0.0, inv)


def apply_inverse(x, inv):
    both = jnp.concatenate(lane_halves(inv), axis=0)
    return lax.dot_general(x, both, NT, precision=HIGH, preferred_element_type=F32)


def middle_kernel(g_ref, image_ref, corr_ref, *, scale):
    packed = g_ref[:, 8:9, :].reshape(32, 128)
    inv = inverse_factor(packed, scale)
    image = apply_inverse(g_ref[:, 0:8, :].reshape(256, 128), inv)
    image_ref[...] = image
    corr = lax.dot_general(image, image, TN, precision=HIGH, preferred_element_type=F32)
    corr = corr[0:64] + pltpu.roll(corr[64:128], 64, 1)
    corr_ref[...] = fold_rows(corr)


def middle(g, scale):
    return pl.pallas_call(
        lambda *refs: middle_kernel(*refs, scale=scale),
        out_shape=(jax.ShapeDtypeStruct((256, 128), F32), jax.ShapeDtypeStruct((32, 128), F32)),
        in_specs=[VM],
        out_specs=(VM, VM),
        name="middle",
    )(g)


def last_kernel(image_ref, corr_ref, o_ref, *, scale):
    packed = corr_ref[0]
    for m in range(1, 16):
        packed = packed + corr_ref[m]
    inv = inverse_factor(packed, scale)
    upper, lower = lane_halves(inv)
    image = image_ref[...]
    o_ref[:, 0:256] = lax.dot_general(upper, image, NT, precision=HIGH, preferred_element_type=F32)
    o_ref[:, 256:512] = lax.dot_general(lower, image, NT, precision=HIGH, preferred_element_type=F32)


def last(image, corr, scale):
    return pl.pallas_call(
        lambda *refs: last_kernel(*refs, scale=scale),
        out_shape=jax.ShapeDtypeStruct((64, 512), F32),
        in_specs=[VM, VM],
        out_specs=VM,
        name="last",
    )(image, corr).T


def to_all(x, axis):
    size = lax.axis_size(axis)
    return lax.all_to_all(jnp.broadcast_to(x[None], (size, *x.shape)), axis, 0, 0, tiled=True)


def halves_in_lanes(rows, start):
    low = lax.dynamic_slice_in_dim(rows, start, 8, 0)
    high = lax.dynamic_slice_in_dim(rows, start + 256, 8, 0)
    return jnp.concatenate([low, high], axis=1)


def on_device(band_form, interp_coef, screen, coulomb, shift_map, grid_order, energies, initial):
    plane = lax.axis_index("ka")
    col = lax.axis_index("kp")
    cells_x, cells_y = grid_order // GRID_Y, grid_order % GRID_Y
    near_x = lax.dynamic_slice_in_dim(cells_x, 4 * plane, 4)
    near_y = lax.dynamic_slice_in_dim(cells_y, 4 * plane, 4)
    table = (near_x[None, :] - cells_x[:, None]) % GRID_X * GRID_Y + (near_y[None, :] - cells_y[:, None]) % GRID_Y
    table = table.reshape(256)

    columns = screen.transpose(1, 0, 2).reshape(64, 128)
    forms = lax.dynamic_slice_in_dim(band_form, 64 * col, 64, 2).reshape(2, 2, 24, 64).transpose(0, 2, 1, 3).reshape(48, 128)
    coefs = lax.dynamic_slice_in_dim(interp_coef, 4 * col, 4, 1).reshape(16, 128)
    starts = halves_in_lanes(initial, 8 * col)
    diagonal = halves_in_lanes(jnp.broadcast_to(energies[:, None], (512, 64)), 8 * col)
    piece = jnp.concatenate([columns, forms, coefs, starts.astype(BF)], axis=0)
    gathered = lax.all_gather(piece, "ka", axis=0, tiled=False)
    received = lax.all_to_all(pick(gathered, table), "kp", 0, 0, tiled=True)

    own = lax.dynamic_slice_in_dim(table, 8 * col, 8)
    scalars = jnp.concatenate([own, jnp.broadcast_to(col % 2, (8,)).astype(jnp.int32)])
    kernel, product = pair_blocks(
        scalars, received, band_form, interp_coef, coulomb.reshape(16, 128), shift_map.reshape(64, 16, 128)
    )
    product = lax.all_to_all(product.reshape(32, 8, 128), "kp", 0, 0, tiled=True)
    image = jnp.sum(product, axis=0) + diagonal * starts
    far = lax.all_to_all(split_parts(to_all(image, "ka")), "kp", 0, 0, tiled=True)

    sums = jnp.sum(lax.all_to_all(second_product(kernel, far), "kp", 0, 0, tiled=True), axis=0)
    sums = sums + jnp.concatenate([diagonal * image, jnp.zeros((1, 128), F32)], axis=0)
    everyone = to_all(sums, "kp")
    scale = 1.0 / 8192
    image, corr = middle(everyone, scale)
    vectors = last(image, to_all(corr, "ka"), scale)
    return (kernel, vectors)


def solution(mesh):
    return jax.shard_map(
        on_device,
        mesh=mesh,
        in_specs=(
            P("ka", None, None),
            P("ka", None, None),
            P("ka", "kp", None),
            P(),
            P(),
            P(),
            P("ka"),
            P("ka", None),
        ),
        out_specs=(P("ka", "kp"), P("ka", None)),
        check_vma=False,
    )
```

```python
import jax
import jax.numpy as jnp
from jax import lax
from jax.experimental import pallas as pl
from jax.experimental.pallas import tpu as pltpu
from jax.sharding import PartitionSpec as P

NV, NC = 8, 16
GRID_Y = 8
GRID_X = 8
BF, F32 = jnp.bfloat16, jnp.float32
HIGH = lax.Precision.HIGHEST
VM = pl.BlockSpec(memory_space=pltpu.VMEM)
SM = pl.BlockSpec(memory_space=pltpu.SMEM)


def pick_kernel(t_ref, g_ref, o_ref, rolled):
    def roll_one(h, _):
        x = g_ref[h, 0:64, :].astype(F32)
        rolled[0, h] = x.astype(BF)
        for s in range(1, 4):
            rolled[s, h] = pltpu.roll(x, 32 * s, 1).astype(BF)
        return 0

    lax.fori_loop(0, 16, roll_one, 0)
    lane_block = lax.broadcasted_iota(jnp.int32, (64, 128), 1) // 32

    def dest(d, _):
        for j in range(2):
            acc = None
            for i in range(4):
                q = t_ref[(2 * d + j) * 4 + i]
                tile = rolled[(i - q) & 3, q >> 2].astype(F32)
                acc = tile if acc is None else jnp.where(lane_block == i, tile, acc)
            o_ref[d, 64 * j : 64 * j + 64, :] = acc.astype(BF)
        half = d & 1
        plane = d >> 1
        o_ref[d, 128:152, :] = g_ref[plane, pl.ds(pl.multiple_of(64 + 24 * half, 8), 24), :]
        o_ref[d, 152:160, :] = g_ref[plane, pl.ds(pl.multiple_of(112 + 8 * half, 8), 8), :]
        o_ref[d, 160:168, :] = g_ref[plane, 128:136, :]
        return 0

    lax.fori_loop(0, 32, dest, 0)


def pick(gathered, table):
    return pl.pallas_call(
        pick_kernel,
        out_shape=jax.ShapeDtypeStruct((32, 168, 128), BF),
        in_specs=[pl.BlockSpec(memory_space=pltpu.SMEM), pl.BlockSpec(memory_space=pltpu.VMEM)],
        out_specs=pl.BlockSpec(memory_space=pltpu.VMEM),
        scratch_shapes=[pltpu.VMEM((4, 16, 64, 128), BF)],
        name="pick",
    )(table, gathered)


NT = (((1,), (1,)), ((), ()))
TN = (((0,), (0,)), ((), ()))


def prepare_kernel(form_ref, o_ref):
    for c in range(NC):
        o_ref[0, c] = jnp.broadcast_to(form_ref[0, 8 + c : 9 + c, :].astype(F32), (16, 2048)).astype(BF)


def prepare(near):
    return pl.pallas_call(
        prepare_kernel,
        grid=(4,),
        in_specs=[pl.BlockSpec((1, 24, 2048), lambda i: (i, 0, 0))],
        out_specs=pl.BlockSpec((1, 16, 16, 2048), lambda i: (i, 0, 0, 0)),
        out_shape=jax.ShapeDtypeStruct((4, 16, 16, 2048), BF),
        name="prepare",
    )(near)


def pair_kernel(t_ref, r_ref, near_ref, wide_ref, coef_ref, coul_ref, map_ref, o_ref, send_ref, far, farc, nearc, cols, cond, val, scaled, acc, right, kt):
    lane24 = lax.broadcasted_iota(jnp.int32, (24, 128), 1)
    for m in range(16):
        lo = r_ref[2 * m, 128:152, :].astype(F32)
        hi = r_ref[2 * m + 1, 128:152, :].astype(F32)
        at = (slice(24 * (m // 2), 24 * (m // 2) + 24), slice(128 * (m % 2), 128 * (m % 2) + 128))
        far[(0, *at)] = jnp.where(lane24 < 64, lo, pltpu.roll(hi, 64, 1)).astype(BF)
        far[(1, *at)] = jnp.where(lane24 < 64, pltpu.roll(lo, 64, 1), hi).astype(BF)
    rows = r_ref[:, 152:160, :].reshape(256, 128)
    out_row = lax.broadcasted_iota(jnp.int32, (128, 256), 0)
    in_row = lax.broadcasted_iota(jnp.int32, (128, 256), 1)
    for k in range(2):
        sel = (in_row == (out_row // 4) * 8 + k * 4 + out_row % 4).astype(F32).astype(BF)
        farc[k] = jnp.dot(sel, rows, preferred_element_type=F32).astype(BF)
        cols[k] = r_ref[:, 64 * k : 64 * k + 64, :].reshape(2048, 128).astype(F32).T.astype(BF)
    old = lax.broadcasted_iota(jnp.int32, (128, 128), 1)
    new = lax.broadcasted_iota(jnp.int32, (128, 128), 0)
    order = (old == (new % 8) * 16 + new // 8).astype(F32).astype(BF)
    for i in range(4):
        nearc[i] = lax.dot_general(coef_ref[i], order, (((0,), (1,)), ((), ())), preferred_element_type=F32).astype(BF)

    place = lax.broadcasted_iota(jnp.int32, (256, 128), 0).astype(F32).astype(BF)
    one, zero = jnp.ones((), BF), jnp.zeros((), BF)
    granule = lax.broadcasted_iota(jnp.int32, (8, 128), 1) // 16

    def finish(p):
        j = p // 4
        i = p % 4
        r_hi = right[...].astype(BF)
        r_lo = (right[...] - r_hi.astype(F32)).astype(BF)
        left = acc[64:96, :]
        l_hi = left.astype(BF)
        l_lo = (left - l_hi.astype(F32)).astype(BF)
        low = jnp.dot(r_lo, l_hi, preferred_element_type=F32) + jnp.dot(r_hi, l_lo, preferred_element_type=F32)
        direct = acc[0:64, :] + (jnp.dot(r_hi, l_hi, preferred_element_type=F32) + low)
        tiles = []
        for half in range(2):
            t = [direct[8 * v : 8 * v + 8, 128 * half : 128 * half + 128] for v in range(8)]
            for s in (1, 2, 4):
                upper = (granule & s) != 0
                n = list(t)
                for v in range(8):
                    if not v & s:
                        a, b = t[v], t[v | s]
                        n[v] = jnp.where(upper, pltpu.roll(b, 16 * s, 1), a)
                        n[v | s] = jnp.where(upper, b, pltpu.roll(a, 128 - 16 * s, 1))
                t = n
            tiles += t
        block = jnp.concatenate(tiles, axis=0).astype(BF)
        half = jnp.dot(block, farc[j], preferred_element_type=F32).astype(BF)
        out = jnp.dot(nearc[i], half, preferred_element_type=F32)
        at_i = pl.ds(pl.multiple_of(i * 128, 128), 128)
        at_j = pl.ds(pl.multiple_of(j * 128, 128), 128)
        o_ref[at_i, at_j] = out.astype(BF)
        kt[at_j, at_i] = out.T.astype(BF)

    def pair(p, _):
        finish(jnp.maximum(p - 1, 0))
        j = p // 4
        i = p % 4
        index = map_ref[t_ref[p]]
        for m in range(16):
            cs = slice(128 * m, 128 * m + 128)
            if m % 2 == 0:
                pick_low = [
                    jnp.where(place == (index[n : n + 1, :] & 255).astype(F32).astype(BF), one, zero) for n in (m, m + 1)
                ]
                both = jnp.dot(far[j], jnp.concatenate(pick_low, axis=1), preferred_element_type=F32)
            high = jnp.broadcast_to(index[m : m + 1, :] >> 8, (24, 128))
            ls = slice(128 * (m % 2), 128 * (m % 2) + 128)
            got = both[0:24, ls]
            for s in range(1, 8):
                got = jnp.where(high == s, both[24 * s : 24 * s + 24, ls], got)
            a = near_ref[i, :, cs].astype(F32)
            m_c = got[8:24, :].astype(BF)
            for c in range(NC):
                cond[16 * c : 16 * c + 16, cs] = wide_ref[i, c, :, cs] * m_c
            a_v = a[0:8, :]
            coul = coul_ref[m : m + 1, :]
            for v in range(0, NV, 2):
                x = jnp.concatenate([a_v * got[v : v + 1, :], a_v * got[v + 1 : v + 2, :]], axis=0).astype(BF)
                val[8 * v : 8 * v + 16, cs] = x
                scaled[8 * v : 8 * v + 16, cs] = (coul * x.astype(F32)).astype(BF)
        own = cols[j, pl.ds(pl.multiple_of(32 * i, 32), 32), :]
        acc[0:64, :] = lax.dot_general(scaled[...], cond[...], NT, preferred_element_type=F32)
        acc[64:96, :] = lax.dot_general(own, cond[...], NT, preferred_element_type=F32)
        right[...] = lax.dot_general(val[...], own, NT, preferred_element_type=F32)
        return 0

    lax.fori_loop(0, 8, pair, 0)
    finish(7)

    odd = t_ref[8] == 1
    both = r_ref[:, 160:168, :].reshape(256, 128).astype(F32)
    lane = lax.broadcasted_iota(jnp.int32, (256, 128), 1)
    other = pltpu.roll(both, 64, 1)
    first = jnp.where(lane < 64, jnp.where(odd, other, both), 0.0).astype(BF)
    second = jnp.where(lane < 64, 0.0, jnp.where(odd, both, other)).astype(BF)
    y = jnp.dot(o_ref[0:256, :], first, preferred_element_type=F32)
    y = y + jnp.dot(o_ref[256:512, :], second, preferred_element_type=F32)
    y_hi = y.astype(BF)
    send_ref[:, 0:8, :] = y_hi.reshape(32, 8, 128)
    send_ref[:, 8:16, :] = (y - y_hi.astype(F32)).astype(BF).reshape(32, 8, 128)
    for b in range(4):
        send_ref[:, 16 + 8 * b : 24 + 8 * b, :] = kt[:, 128 * b : 128 * b + 128].reshape(32, 8, 128)


def pair_blocks(table, received, near, wide, coef, coulomb, shift_map):
    return pl.pallas_call(
        pair_kernel,
        in_specs=[SM, VM, VM, VM, VM, VM, VM],
        out_specs=(VM, VM),
        out_shape=(jax.ShapeDtypeStruct((512, 256), BF), jax.ShapeDtypeStruct((32, 48, 128), BF)),
        scratch_shapes=[
            pltpu.VMEM((2, 192, 256), BF),
            pltpu.VMEM((2, 128, 128), BF),
            pltpu.VMEM((4, 128, 128), BF),
            pltpu.VMEM((2, 128, 2048), BF),
            pltpu.VMEM((256, 2048), BF),
            pltpu.VMEM((64, 2048), BF),
            pltpu.VMEM((64, 2048), BF),
            pltpu.VMEM((96, 256), F32),
            pltpu.VMEM((64, 32), F32),
            pltpu.VMEM((256, 512), BF),
        ],
        name="pairs",
    )(table, received, near, wide, coef, coulomb, shift_map)


def fold_rows(square):
    lane = lax.broadcasted_iota(jnp.int32, (32, 128), 1)
    return jnp.where(lane < 64, square[0:32], pltpu.roll(square[32:64], 64, 1))


def second_kernel(r_ref, x_ref, o_ref):
    lane = lax.broadcasted_iota(jnp.int32, (8, 128), 1)
    parts = []
    for m in range(16):
        x = x_ref[m]
        high = x.astype(BF).astype(F32)
        low = x - high
        parts.append(jnp.where(lane < 64, high, pltpu.roll(low, 64, 1)))
        parts.append(jnp.where(lane < 64, pltpu.roll(high, 64, 1), low))
    x = jnp.concatenate(parts, axis=0)
    xt = x.T.astype(BF)
    sums = []
    for b in range(4):
        g = jnp.dot(xt, r_ref[:, 16 + 8 * b : 24 + 8 * b, :].reshape(256, 128), preferred_element_type=F32)
        sums.append(g[0:64] + g[64:128])
    for b in range(2):
        y = jnp.concatenate([sums[b], sums[b + 2]], axis=0).T
        o_ref[16 * b : 16 * b + 16, 0:8, :] = y.reshape(16, 8, 128)
    corr = jnp.dot(xt, x.astype(BF), preferred_element_type=F32)
    corr = corr + pltpu.roll(corr, 64, 1)
    corr = fold_rows(corr[0:64] + corr[64:128])
    o_ref[:, 8:9, :] = corr.reshape(32, 1, 128)


def second_product(received, x):
    return pl.pallas_call(
        second_kernel,
        out_shape=jax.ShapeDtypeStruct((32, 9, 128), F32),
        in_specs=[VM, VM],
        out_specs=VM,
        name="second",
    )(received, x)


def inverse_factor(packed, scale):
    lane = lax.broadcasted_iota(jnp.int32, (64, 128), 1)
    row = lax.broadcasted_iota(jnp.int32, (64, 128), 0)
    full = jnp.concatenate([packed, pltpu.roll(packed, 64, 1)], axis=0) * scale
    work = jnp.where(lane < 64, full, (lane - 64 == row).astype(F32))
    done = []
    tiles = [work[8 * t : 8 * t + 8] for t in range(8)]
    for j in range(64):
        t0 = j // 8
        top = jnp.broadcast_to(tiles[t0][:, j : j + 1], (8, 128))
        pivot = top[j % 8 : j % 8 + 1, :]
        r = lax.rsqrt(pivot)
        r = r * (1.5 - 0.5 * pivot * r * r)
        line = tiles[t0][j % 8 : j % 8 + 1, :] * r
        done.append(line)
        scaled = line * r
        for t in range(t0, 8):
            column = top if t == t0 else jnp.broadcast_to(tiles[t][:, j : j + 1], (8, 128))
            tiles[t] = tiles[t] - column * scaled
    return jnp.concatenate(done, axis=0)


def lane_halves(inv):
    lane = lax.broadcasted_iota(jnp.int32, (64, 128), 1)
    return jnp.where(lane < 64, pltpu.roll(inv, 64, 1), 0.0), jnp.where(lane < 64, 0.0, inv)


def apply_inverse(x, inv):
    both = jnp.concatenate(lane_halves(inv), axis=0)
    return lax.dot_general(x, both, NT, precision=HIGH, preferred_element_type=F32)


def middle_kernel(g_ref, image_ref, corr_ref, *, scale):
    packed = g_ref[:, 8:9, :].reshape(32, 128)
    inv = inverse_factor(packed, scale)
    image = apply_inverse(g_ref[:, 0:8, :].reshape(256, 128), inv)
    image_ref[...] = image
    corr = lax.dot_general(image, image, TN, precision=HIGH, preferred_element_type=F32)
    corr = corr[0:64] + pltpu.roll(corr[64:128], 64, 1)
    corr = fold_rows(corr)
    for m in range(16):
        corr_ref[m] = corr


def middle(g, scale):
    return pl.pallas_call(
        lambda *refs: middle_kernel(*refs, scale=scale),
        out_shape=(jax.ShapeDtypeStruct((256, 128), F32), jax.ShapeDtypeStruct((16, 32, 128), F32)),
        in_specs=[VM],
        out_specs=(VM, VM),
        name="middle",
    )(g)


def last_kernel(image_ref, corr_ref, o_ref, *, scale):
    packed = corr_ref[0]
    for m in range(1, 16):
        packed = packed + corr_ref[m]
    inv = inverse_factor(packed, scale)
    upper, lower = lane_halves(inv)
    image = image_ref[...]
    o_ref[:, 0:256] = lax.dot_general(upper, image, NT, precision=HIGH, preferred_element_type=F32)
    o_ref[:, 256:512] = lax.dot_general(lower, image, NT, precision=HIGH, preferred_element_type=F32)


def last(image, corr, scale):
    return pl.pallas_call(
        lambda *refs: last_kernel(*refs, scale=scale),
        out_shape=jax.ShapeDtypeStruct((64, 512), F32),
        in_specs=[VM, VM],
        out_specs=VM,
        name="last",
    )(image, corr).T


def to_all(x, axis):
    size = lax.axis_size(axis)
    return lax.all_to_all(jnp.broadcast_to(x[None], (size, *x.shape)), axis, 0, 0, tiled=True)


def halves_in_lanes(rows, start):
    low = lax.dynamic_slice_in_dim(rows, start, 8, 0)
    high = lax.dynamic_slice_in_dim(rows, start + 256, 8, 0)
    return jnp.concatenate([low, high], axis=1)


def on_device(band_form, interp_coef, screen, coulomb, shift_map, grid_order, energies, initial):
    plane = lax.axis_index("ka")
    col = lax.axis_index("kp")
    cells_x, cells_y = grid_order // GRID_Y, grid_order % GRID_Y
    near_x = lax.dynamic_slice_in_dim(cells_x, 4 * plane, 4)
    near_y = lax.dynamic_slice_in_dim(cells_y, 4 * plane, 4)
    table = (near_x[None, :] - cells_x[:, None]) % GRID_X * GRID_Y + (near_y[None, :] - cells_y[:, None]) % GRID_Y
    table = table.reshape(256)

    columns = screen.transpose(1, 0, 2).reshape(64, 128)
    forms = lax.dynamic_slice_in_dim(band_form, 64 * col, 64, 2).reshape(2, 2, 24, 64).transpose(0, 2, 1, 3).reshape(48, 128)
    coefs = lax.dynamic_slice_in_dim(interp_coef, 4 * col, 4, 1).reshape(16, 128)
    starts = halves_in_lanes(initial, 8 * col)
    diagonal = halves_in_lanes(jnp.broadcast_to(energies[:, None], (512, 64)), 8 * col)
    piece = jnp.concatenate([columns, forms, coefs, starts.astype(BF)], axis=0)
    gathered = lax.all_gather(piece, "ka", axis=0, tiled=False)
    received = lax.all_to_all(pick(gathered, table), "kp", 0, 0, tiled=True)

    own = lax.dynamic_slice_in_dim(table, 8 * col, 8)
    scalars = jnp.concatenate([own, jnp.broadcast_to(col % 2, (8,)).astype(jnp.int32)])
    kernel, sent = pair_blocks(scalars, received, band_form, prepare(band_form), interp_coef, coulomb.reshape(16, 128), shift_map.reshape(64, 16, 128))
    sent = lax.all_to_all(sent, "kp", 0, 0, tiled=True)
    image = jnp.sum(sent[:, 0:16, :].astype(F32).reshape(64, 8, 128), axis=0) + diagonal * starts

    sums = jnp.sum(lax.all_to_all(second_product(sent, to_all(image, "ka")), "kp", 0, 0, tiled=True), axis=0)
    sums = sums + jnp.concatenate([diagonal * image, jnp.zeros((1, 128), F32)], axis=0)
    everyone = to_all(sums, "kp")
    scale = 1.0 / 8192
    image, corr = middle(everyone, scale)
    vectors = last(image, lax.all_to_all(corr, "ka", 0, 0, tiled=True), scale)
    return (kernel, vectors)


def solution(mesh):
    return jax.shard_map(
        on_device,
        mesh=mesh,
        in_specs=(
            P("ka", None, None),
            P("ka", None, None),
            P("ka", "kp", None),
            P(),
            P(),
            P(),
            P("ka"),
            P("ka", None),
        ),
        out_specs=(P("ka", "kp"), P("ka", None)),
        check_vma=False,
    )
```

```python
import jax
import jax.numpy as jnp
from jax import lax
from jax.experimental import pallas as pl
from jax.experimental.pallas import tpu as pltpu
from jax.sharding import PartitionSpec as P

NV, NC = 8, 16
GRID_Y = 8
GRID_X = 8
BF, F32 = jnp.bfloat16, jnp.float32
HIGH = lax.Precision.HIGHEST
VM = pl.BlockSpec(memory_space=pltpu.VMEM)
SM = pl.BlockSpec(memory_space=pltpu.SMEM)


def pick_kernel(t_ref, g_ref, o_ref, rolled):
    def roll_one(h, _):
        x = g_ref[h, 0:64, :].astype(F32)
        rolled[0, h] = x.astype(BF)
        for s in range(1, 4):
            rolled[s, h] = pltpu.roll(x, 32 * s, 1).astype(BF)
        return 0

    lax.fori_loop(0, 16, roll_one, 0, unroll=4)
    lane_block = lax.broadcasted_iota(jnp.int32, (64, 128), 1) // 32

    def dest(d, _):
        for j in range(2):
            acc = None
            for i in range(4):
                q = t_ref[(2 * d + j) * 4 + i]
                tile = rolled[(i - q) & 3, q >> 2].astype(F32)
                acc = tile if acc is None else jnp.where(lane_block == i, tile, acc)
            o_ref[d, 64 * j : 64 * j + 64, :] = acc.astype(BF)
        half = d & 1
        plane = d >> 1
        o_ref[d, 128:152, :] = g_ref[plane, pl.ds(pl.multiple_of(64 + 24 * half, 8), 24), :]
        o_ref[d, 152:160, :] = g_ref[plane, pl.ds(pl.multiple_of(112 + 8 * half, 8), 8), :]
        o_ref[d, 160:168, :] = g_ref[plane, 128:136, :]
        return 0

    lax.fori_loop(0, 32, dest, 0, unroll=4)


def pick(gathered, table):
    return pl.pallas_call(
        pick_kernel,
        out_shape=jax.ShapeDtypeStruct((32, 168, 128), BF),
        in_specs=[pl.BlockSpec(memory_space=pltpu.SMEM), pl.BlockSpec(memory_space=pltpu.VMEM)],
        out_specs=pl.BlockSpec(memory_space=pltpu.VMEM),
        scratch_shapes=[pltpu.VMEM((4, 16, 64, 128), BF)],
        name="pick",
    )(table, gathered)


NT = (((1,), (1,)), ((), ()))
TN = (((0,), (0,)), ((), ()))


def prepare_kernel(form_ref, o_ref):
    for c in range(NC):
        o_ref[0, c] = jnp.broadcast_to(form_ref[0, 8 + c : 9 + c, :].astype(F32), (16, 2048)).astype(BF)


def prepare(near):
    return pl.pallas_call(
        prepare_kernel,
        grid=(4,),
        in_specs=[pl.BlockSpec((1, 24, 2048), lambda i: (i, 0, 0))],
        out_specs=pl.BlockSpec((1, 16, 16, 2048), lambda i: (i, 0, 0, 0)),
        out_shape=jax.ShapeDtypeStruct((4, 16, 16, 2048), BF),
        name="prepare",
    )(near)


def pair_kernel(t_ref, r_ref, near_ref, wide_ref, coef_ref, coul_ref, map_ref, o_ref, send_ref, far, farc, nearc, cols, cond, val, scaled, acc, right, kt):
    lane24 = lax.broadcasted_iota(jnp.int32, (24, 128), 1)
    for m in range(16):
        lo = r_ref[2 * m, 128:152, :].astype(F32)
        hi = r_ref[2 * m + 1, 128:152, :].astype(F32)
        at = (slice(24 * (m // 2), 24 * (m // 2) + 24), slice(128 * (m % 2), 128 * (m % 2) + 128))
        far[(0, *at)] = jnp.where(lane24 < 64, lo, pltpu.roll(hi, 64, 1)).astype(BF)
        far[(1, *at)] = jnp.where(lane24 < 64, pltpu.roll(lo, 64, 1), hi).astype(BF)
    rows = r_ref[:, 152:160, :].reshape(256, 128)
    out_row = lax.broadcasted_iota(jnp.int32, (128, 256), 0)
    in_row = lax.broadcasted_iota(jnp.int32, (128, 256), 1)
    for k in range(2):
        sel = (in_row == (out_row // 4) * 8 + k * 4 + out_row % 4).astype(F32).astype(BF)
        farc[k] = jnp.dot(sel, rows, preferred_element_type=F32).astype(BF)
        cols[k] = r_ref[:, 64 * k : 64 * k + 64, :].reshape(2048, 128).astype(F32).T.astype(BF)
    old = lax.broadcasted_iota(jnp.int32, (128, 128), 1)
    new = lax.broadcasted_iota(jnp.int32, (128, 128), 0)
    order = (old == (new % 8) * 16 + new // 8).astype(F32).astype(BF)
    for i in range(4):
        nearc[i] = lax.dot_general(coef_ref[i], order, (((0,), (1,)), ((), ())), preferred_element_type=F32).astype(BF)

    place = lax.broadcasted_iota(jnp.int32, (256, 128), 0).astype(F32).astype(BF)
    one, zero = jnp.ones((), BF), jnp.zeros((), BF)
    granule = lax.broadcasted_iota(jnp.int32, (8, 128), 1) // 16

    def finish(p):
        j = p // 4
        i = p % 4
        r_hi = right[...].astype(BF)
        r_lo = (right[...] - r_hi.astype(F32)).astype(BF)
        left = acc[64:96, :]
        l_hi = left.astype(BF)
        l_lo = (left - l_hi.astype(F32)).astype(BF)
        low = jnp.dot(r_lo, l_hi, preferred_element_type=F32) + jnp.dot(r_hi, l_lo, preferred_element_type=F32)
        direct = acc[0:64, :] + (jnp.dot(r_hi, l_hi, preferred_element_type=F32) + low)
        tiles = []
        for half in range(2):
            t = [direct[8 * v : 8 * v + 8, 128 * half : 128 * half + 128] for v in range(8)]
            for s in (1, 2, 4):
                upper = (granule & s) != 0
                n = list(t)
                for v in range(8):
                    if not v & s:
                        a, b = t[v], t[v | s]
                        n[v] = jnp.where(upper, pltpu.roll(b, 16 * s, 1), a)
                        n[v | s] = jnp.where(upper, b, pltpu.roll(a, 128 - 16 * s, 1))
                t = n
            tiles += t
        block = jnp.concatenate(tiles, axis=0).astype(BF)
        half = jnp.dot(block, farc[j], preferred_element_type=F32).astype(BF)
        out = jnp.dot(nearc[i], half, preferred_element_type=F32)
        at_i = pl.ds(pl.multiple_of(i * 128, 128), 128)
        at_j = pl.ds(pl.multiple_of(j * 128, 128), 128)
        o_ref[at_i, at_j] = out.astype(BF)
        kt[at_j, at_i] = out.T.astype(BF)

    def pair(p, _):
        finish(jnp.maximum(p - 1, 0))
        j = p // 4
        i = p % 4
        index = map_ref[t_ref[p]]
        scaled[64:96, :] = cols[j, pl.ds(pl.multiple_of(32 * i, 32), 32), :]
        for m in range(16):
            cs = slice(128 * m, 128 * m + 128)
            if m % 2 == 0:
                pick_low = [
                    jnp.where(place == (index[n : n + 1, :] & 255).astype(F32).astype(BF), one, zero) for n in (m, m + 1)
                ]
                both = jnp.dot(far[j], jnp.concatenate(pick_low, axis=1), preferred_element_type=F32)
            high = jnp.broadcast_to(index[m : m + 1, :] >> 8, (24, 128))
            ls = slice(128 * (m % 2), 128 * (m % 2) + 128)
            got = both[0:24, ls]
            for s in range(1, 8):
                got = jnp.where(high == s, both[24 * s : 24 * s + 24, ls], got)
            a = near_ref[i, :, cs].astype(F32)
            m_c = got[8:24, :].astype(BF)
            for c in range(NC):
                cond[16 * c : 16 * c + 16, cs] = wide_ref[i, c, :, cs] * m_c
            a_v = a[0:8, :]
            coul = coul_ref[m : m + 1, :]
            for v in range(0, NV, 2):
                x = jnp.concatenate([a_v * got[v : v + 1, :], a_v * got[v + 1 : v + 2, :]], axis=0).astype(BF)
                val[8 * v : 8 * v + 16, cs] = x
                scaled[8 * v : 8 * v + 16, cs] = (coul * x.astype(F32)).astype(BF)
            if m % 2:
                ks = slice(128 * m - 128, 128 * m + 128)
                part = lax.dot_general(scaled[:, ks], cond[:, ks], NT, preferred_element_type=F32)
                total = part if m == 1 else total + part
        acc[...] = total
        right[...] = lax.dot_general(val[...], scaled[64:96, :], NT, preferred_element_type=F32)
        return 0

    lax.fori_loop(0, 8, pair, 0)
    finish(7)

    odd = t_ref[8] == 1
    both = r_ref[:, 160:168, :].reshape(256, 128).astype(F32)
    lane = lax.broadcasted_iota(jnp.int32, (256, 128), 1)
    other = pltpu.roll(both, 64, 1)
    first = jnp.where(lane < 64, jnp.where(odd, other, both), 0.0).astype(BF)
    second = jnp.where(lane < 64, 0.0, jnp.where(odd, both, other)).astype(BF)
    y = jnp.dot(o_ref[0:256, :], first, preferred_element_type=F32)
    y = y + jnp.dot(o_ref[256:512, :], second, preferred_element_type=F32)
    y_hi = y.astype(BF)
    send_ref[:, 0:8, :] = y_hi.reshape(32, 8, 128)
    send_ref[:, 8:16, :] = (y - y_hi.astype(F32)).astype(BF).reshape(32, 8, 128)
    for b in range(4):
        send_ref[:, 16 + 8 * b : 24 + 8 * b, :] = kt[:, 128 * b : 128 * b + 128].reshape(32, 8, 128)


def pair_blocks(table, received, near, wide, coef, coulomb, shift_map):
    return pl.pallas_call(
        pair_kernel,
        in_specs=[SM, VM, VM, VM, VM, VM, VM],
        out_specs=(VM, VM),
        out_shape=(jax.ShapeDtypeStruct((512, 256), BF), jax.ShapeDtypeStruct((32, 48, 128), BF)),
        scratch_shapes=[
            pltpu.VMEM((2, 192, 256), BF),
            pltpu.VMEM((2, 128, 128), BF),
            pltpu.VMEM((4, 128, 128), BF),
            pltpu.VMEM((2, 128, 2048), BF),
            pltpu.VMEM((256, 2048), BF),
            pltpu.VMEM((64, 2048), BF),
            pltpu.VMEM((96, 2048), BF),
            pltpu.VMEM((96, 256), F32),
            pltpu.VMEM((64, 32), F32),
            pltpu.VMEM((256, 512), BF),
        ],
        name="pairs",
    )(table, received, near, wide, coef, coulomb, shift_map)


def fold_rows(square):
    lane = lax.broadcasted_iota(jnp.int32, (32, 128), 1)
    return jnp.where(lane < 64, square[0:32], pltpu.roll(square[32:64], 64, 1))


def second_kernel(r_ref, x_ref, o_ref):
    lane = lax.broadcasted_iota(jnp.int32, (8, 128), 1)
    parts = []
    for m in range(16):
        x = x_ref[m]
        high = x.astype(BF).astype(F32)
        low = x - high
        parts.append(jnp.where(lane < 64, high, pltpu.roll(low, 64, 1)))
        parts.append(jnp.where(lane < 64, pltpu.roll(high, 64, 1), low))
    x = jnp.concatenate(parts, axis=0)
    xt = x.T.astype(BF)
    sums = []
    for b in range(4):
        g = jnp.dot(xt, r_ref[:, 16 + 8 * b : 24 + 8 * b, :].reshape(256, 128), preferred_element_type=F32)
        sums.append(g[0:64] + g[64:128])
    for b in range(2):
        y = jnp.concatenate([sums[b], sums[b + 2]], axis=0).T
        o_ref[16 * b : 16 * b + 16, 0:8, :] = y.reshape(16, 8, 128)
    corr = jnp.dot(xt, x.astype(BF), preferred_element_type=F32)
    corr = corr + pltpu.roll(corr, 64, 1)
    corr = fold_rows(corr[0:64] + corr[64:128])
    o_ref[:, 8:9, :] = corr.reshape(32, 1, 128)


def second_product(received, x):
    return pl.pallas_call(
        second_kernel,
        out_shape=jax.ShapeDtypeStruct((32, 9, 128), F32),
        in_specs=[VM, VM],
        out_specs=VM,
        name="second",
    )(received, x)


def inverse_factor(packed, scale):
    lane = lax.broadcasted_iota(jnp.int32, (64, 128), 1)
    row = lax.broadcasted_iota(jnp.int32, (64, 128), 0)
    full = jnp.concatenate([packed, pltpu.roll(packed, 64, 1)], axis=0) * scale
    work = jnp.where(lane < 64, full, (lane - 64 == row).astype(F32))
    done = []
    tiles = [work[8 * t : 8 * t + 8] for t in range(8)]
    for t in range(8):
        column = {u: [jnp.broadcast_to(tiles[u][:, 8 * t + k : 8 * t + k + 1], (8, 128)) for k in range(8)] for u in range(t, 8)}
        for k in range(8):
            pivot = column[t][k][k : k + 1, :]
            y = lax.rsqrt(pivot)
            square = y * y
            near_one = pivot * square
            inverse = square * (2.0 - near_one)
            line = tiles[t][k : k + 1, :]
            done.append(line * (y * (1.5 - 0.5 * near_one)))
            line = line * inverse
            ahead = {m: column[t][m][k : k + 1, :] * inverse for m in range(k + 1, 8)}
            for u in range(t, 8):
                factor = column[u][k]
                for m in range(k + 1, 8):
                    column[u][m] = column[u][m] - factor * ahead[m]
                tiles[u] = tiles[u] - factor * line
    return jnp.concatenate(done, axis=0)


def lane_halves(inv):
    lane = lax.broadcasted_iota(jnp.int32, (64, 128), 1)
    return jnp.where(lane < 64, pltpu.roll(inv, 64, 1), 0.0), jnp.where(lane < 64, 0.0, inv)


def apply_inverse(x, inv):
    both = jnp.concatenate(lane_halves(inv), axis=0)
    return lax.dot_general(x, both, NT, precision=HIGH, preferred_element_type=F32)


def middle_kernel(g_ref, image_ref, corr_ref, *, scale):
    packed = g_ref[:, 8:9, :].reshape(32, 128)
    inv = inverse_factor(packed, scale)
    image = apply_inverse(g_ref[:, 0:8, :].reshape(256, 128), inv)
    image_ref[...] = image
    corr = lax.dot_general(image, image, TN, precision=HIGH, preferred_element_type=F32)
    corr = corr[0:64] + pltpu.roll(corr[64:128], 64, 1)
    corr = fold_rows(corr)
    for m in range(16):
        corr_ref[m] = corr


def middle(g, scale):
    return pl.pallas_call(
        lambda *refs: middle_kernel(*refs, scale=scale),
        out_shape=(jax.ShapeDtypeStruct((256, 128), F32), jax.ShapeDtypeStruct((16, 32, 128), F32)),
        in_specs=[VM],
        out_specs=(VM, VM),
        name="middle",
    )(g)


def last_kernel(image_ref, corr_ref, o_ref, *, scale):
    packed = corr_ref[0]
    for m in range(1, 16):
        packed = packed + corr_ref[m]
    inv = inverse_factor(packed, scale)
    upper, lower = lane_halves(inv)
    image = image_ref[...]
    o_ref[:, 0:256] = lax.dot_general(upper, image, NT, precision=HIGH, preferred_element_type=F32)
    o_ref[:, 256:512] = lax.dot_general(lower, image, NT, precision=HIGH, preferred_element_type=F32)


def last(image, corr, scale):
    return pl.pallas_call(
        lambda *refs: last_kernel(*refs, scale=scale),
        out_shape=jax.ShapeDtypeStruct((64, 512), F32),
        in_specs=[VM, VM],
        out_specs=VM,
        name="last",
    )(image, corr).T


def to_all(x, axis):
    size = lax.axis_size(axis)
    return lax.all_to_all(jnp.broadcast_to(x[None], (size, *x.shape)), axis, 0, 0, tiled=True)


def halves_in_lanes(rows, start):
    low = lax.dynamic_slice_in_dim(rows, start, 8, 0)
    high = lax.dynamic_slice_in_dim(rows, start + 256, 8, 0)
    return jnp.concatenate([low, high], axis=1)


def on_device(band_form, interp_coef, screen, coulomb, shift_map, grid_order, energies, initial):
    plane = lax.axis_index("ka")
    col = lax.axis_index("kp")
    cells_x, cells_y = grid_order // GRID_Y, grid_order % GRID_Y
    near_x = lax.dynamic_slice_in_dim(cells_x, 4 * plane, 4)
    near_y = lax.dynamic_slice_in_dim(cells_y, 4 * plane, 4)
    table = (near_x[None, :] - cells_x[:, None]) % GRID_X * GRID_Y + (near_y[None, :] - cells_y[:, None]) % GRID_Y
    table = table.reshape(256)

    columns = screen.transpose(1, 0, 2).reshape(64, 128)
    forms = lax.dynamic_slice_in_dim(band_form, 64 * col, 64, 2).reshape(2, 2, 24, 64).transpose(0, 2, 1, 3).reshape(48, 128)
    coefs = lax.dynamic_slice_in_dim(interp_coef, 4 * col, 4, 1).reshape(16, 128)
    starts = halves_in_lanes(initial, 8 * col)
    diagonal = halves_in_lanes(jnp.broadcast_to(energies[:, None], (512, 64)), 8 * col)
    piece = jnp.concatenate([columns, forms, coefs, starts.astype(BF)], axis=0)
    gathered = lax.all_gather(piece, "ka", axis=0, tiled=False)
    received = lax.all_to_all(pick(gathered, table), "kp", 0, 0, tiled=True)

    received = pltpu.with_memory_space_constraint(received, pltpu.VMEM)
    own = lax.dynamic_slice_in_dim(table, 8 * col, 8)
    scalars = jnp.concatenate([own, jnp.broadcast_to(col % 2, (8,)).astype(jnp.int32)])
    kernel, sent = pair_blocks(scalars, received, band_form, prepare(band_form), interp_coef, coulomb.reshape(16, 128), shift_map.reshape(64, 16, 128))
    sent = lax.all_to_all(sent, "kp", 0, 0, tiled=True)
    image = jnp.sum(sent[:, 0:16, :].astype(F32).reshape(64, 8, 128), axis=0) + diagonal * starts

    sums = jnp.sum(lax.all_to_all(second_product(sent, to_all(image, "ka")), "kp", 0, 0, tiled=True), axis=0)
    sums = sums + jnp.concatenate([diagonal * image, jnp.zeros((1, 128), F32)], axis=0)
    everyone = to_all(sums, "kp")
    scale = 1.0 / 8192
    image, corr = middle(everyone, scale)
    vectors = last(image, lax.all_to_all(corr, "ka", 0, 0, tiled=True), scale)
    return (kernel, vectors)


def solution(mesh):
    return jax.shard_map(
        on_device,
        mesh=mesh,
        in_specs=(
            P("ka", None, None),
            P("ka", None, None),
            P("ka", "kp", None),
            P(),
            P(),
            P(),
            P("ka"),
            P("ka", None),
        ),
        out_specs=(P("ka", "kp"), P("ka", None)),
        check_vma=False,
    )
```

```python
import jax
import jax.numpy as jnp
from jax import lax
from jax.experimental import pallas as pl
from jax.experimental.pallas import tpu as pltpu
from jax.sharding import PartitionSpec as P

NV, NC = 8, 16
GRID_Y = 8
GRID_X = 8
BF, F32 = jnp.bfloat16, jnp.float32
HIGH = lax.Precision.HIGHEST
VM = pl.BlockSpec(memory_space=pltpu.VMEM)
SM = pl.BlockSpec(memory_space=pltpu.SMEM)


def device_at(axis):
    return lax.axis_index(axis)


def vmem(x):
    return pltpu.with_memory_space_constraint(x, pltpu.VMEM)


def share_kernel(form_ref, coef_ref, screen_ref, start_ref, energy_ref, cell_ref, cells_ref, piece_ref, first_ref, diagonal_ref, table_ref, form, coef, sems):
    plane, col = device_at("ka"), device_at("kp")
    odd = (col & 1) == 1
    copies = (
        pltpu.make_async_copy(form_ref.at[:, :, pl.ds(pl.multiple_of(128 * (col // 2), 128), 128)], form, sems.at[0]),
        pltpu.make_async_copy(coef_ref.at[:, pl.ds(pl.multiple_of(8 * (col // 2), 8), 8), :], coef, sems.at[1]),
    )
    for copy in copies:
        copy.start()
    x, y = cells_ref[...] >> 3, cells_ref[...] & 7
    for i in range(4):
        cell = cell_ref[4 * plane + i]
        table_ref[i : i + 1, :] = (((cell >> 3) - x) & 7) * 8 + (((cell & 7) - y) & 7)
    piece_ref[0:64, :] = jnp.concatenate([screen_ref[q].astype(F32) for q in range(4)], axis=1).astype(BF)
    block = col // 16
    back = (128 - 8 * (col % 16)) % 128

    def rows_of(parts):
        both = jnp.concatenate([pltpu.roll(part, back, 1) for part in parts], axis=0)
        return both.T[0:8]

    first = rows_of([start_ref[:, pl.ds(pl.multiple_of(256 * h + 128 * block, 128), 128)] for h in range(2)])
    first_ref[...] = first
    diagonal_ref[...] = rows_of([jnp.broadcast_to(energy_ref[pl.ds(2 * h + block, 1), :], (64, 128)) for h in range(2)])
    piece_ref[128:136, :] = first.astype(BF)
    lane = lax.broadcasted_iota(jnp.int32, (24, 128), 1)
    row = lax.broadcasted_iota(jnp.int32, (8, 128), 0)
    copies[0].wait()
    copies[1].wait()
    for h in range(2):
        a, b = form[2 * h].astype(F32), form[2 * h + 1].astype(F32)
        low = jnp.where(odd, pltpu.roll(a, 64, 1), a)
        high = jnp.where(odd, b, pltpu.roll(b, 64, 1))
        piece_ref[64 + 24 * h : 88 + 24 * h, :] = jnp.where(lane < 64, low, high).astype(BF)
        a, b = coef[2 * h].astype(F32), coef[2 * h + 1].astype(F32)
        low = jnp.where(odd, pltpu.roll(a, 4, 0), a)
        high = jnp.where(odd, b, pltpu.roll(b, 4, 0))
        piece_ref[112 + 8 * h : 120 + 8 * h, :] = jnp.where(row < 4, low, high).astype(BF)


def share(forms, coefs, screen, initial, energies, cells):
    hbm = pl.BlockSpec(memory_space=pl.ANY)
    return pl.pallas_call(
        share_kernel,
        in_specs=[hbm, hbm, VM, VM, VM, SM, VM],
        out_specs=(VM, VM, VM, VM),
        out_shape=(
            jax.ShapeDtypeStruct((136, 128), BF),
            jax.ShapeDtypeStruct((8, 128), F32),
            jax.ShapeDtypeStruct((8, 128), F32),
            jax.ShapeDtypeStruct((4, 64), jnp.int32),
        ),
        scratch_shapes=[pltpu.VMEM((4, 24, 128), BF), pltpu.VMEM((4, 8, 128), BF), pltpu.SemaphoreType.DMA((2,))],
        name="share",
    )(forms, coefs, screen, initial.T, energies.reshape(4, 128), cells, cells.reshape(1, 64))


def pick_kernel(t_ref, g_ref, o_ref, rolled):
    def roll_one(h, _):
        x = g_ref[h, 0:64, :].astype(F32)
        rolled[0, h] = x.astype(BF)
        for s in range(1, 4):
            rolled[s, h] = pltpu.roll(x, 32 * s, 1).astype(BF)
        return 0

    lax.fori_loop(0, 16, roll_one, 0, unroll=4)
    lane_block = lax.broadcasted_iota(jnp.int32, (64, 128), 1) // 32

    def dest(d, _):
        for j in range(2):
            acc = None
            for i in range(4):
                q = t_ref[i, 2 * d + j]
                tile = rolled[(i - q) & 3, q >> 2].astype(F32)
                acc = tile if acc is None else jnp.where(lane_block == i, tile, acc)
            o_ref[d, 64 * j : 64 * j + 64, :] = acc.astype(BF)
        half = d & 1
        plane = d >> 1
        o_ref[d, 128:152, :] = g_ref[plane, pl.ds(pl.multiple_of(64 + 24 * half, 8), 24), :]
        o_ref[d, 152:160, :] = g_ref[plane, pl.ds(pl.multiple_of(112 + 8 * half, 8), 8), :]
        o_ref[d, 160:168, :] = g_ref[plane, 128:136, :]
        return 0

    lax.fori_loop(0, 32, dest, 0, unroll=4)


def pick(gathered, table):
    return pl.pallas_call(
        pick_kernel,
        out_shape=jax.ShapeDtypeStruct((32, 168, 128), BF),
        in_specs=[pl.BlockSpec(memory_space=pltpu.SMEM), pl.BlockSpec(memory_space=pltpu.VMEM)],
        out_specs=pl.BlockSpec(memory_space=pltpu.VMEM),
        scratch_shapes=[pltpu.VMEM((4, 16, 64, 128), BF)],
        name="pick",
    )(table, gathered)


NT = (((1,), (1,)), ((), ()))
TN = (((0,), (0,)), ((), ()))


def prepare_kernel(form_ref, o_ref):
    for c in range(NC):
        o_ref[0, c] = jnp.broadcast_to(form_ref[0, 8 + c : 9 + c, :].astype(F32), (16, 2048)).astype(BF)


def prepare(near):
    return pl.pallas_call(
        prepare_kernel,
        grid=(4,),
        in_specs=[pl.BlockSpec((1, 24, 2048), lambda i: (i, 0, 0))],
        out_specs=pl.BlockSpec((1, 16, 16, 2048), lambda i: (i, 0, 0, 0)),
        out_shape=jax.ShapeDtypeStruct((4, 16, 16, 2048), BF),
        compiler_params=pltpu.CompilerParams(vmem_limit_bytes=32 << 20),
        name="prepare",
    )(near)


def pair_kernel(t_ref, r_ref, near_ref, wide_ref, coef_ref, coul_ref, map_ref, o_ref, send_ref, far, farc, nearc, cols, cond, val, scaled, acc, right, kt):
    col = device_at("kp")
    lane24 = lax.broadcasted_iota(jnp.int32, (24, 128), 1)
    for m in range(16):
        lo = r_ref[2 * m, 128:152, :].astype(F32)
        hi = r_ref[2 * m + 1, 128:152, :].astype(F32)
        at = (slice(24 * (m // 2), 24 * (m // 2) + 24), slice(128 * (m % 2), 128 * (m % 2) + 128))
        far[(0, *at)] = jnp.where(lane24 < 64, lo, pltpu.roll(hi, 64, 1)).astype(BF)
        far[(1, *at)] = jnp.where(lane24 < 64, pltpu.roll(lo, 64, 1), hi).astype(BF)
    rows = r_ref[:, 152:160, :].reshape(256, 128)
    out_row = lax.broadcasted_iota(jnp.int32, (128, 256), 0)
    in_row = lax.broadcasted_iota(jnp.int32, (128, 256), 1)
    for k in range(2):
        sel = (in_row == (out_row // 4) * 8 + k * 4 + out_row % 4).astype(F32).astype(BF)
        farc[k] = jnp.dot(sel, rows, preferred_element_type=F32).astype(BF)
        cols[k] = r_ref[:, 64 * k : 64 * k + 64, :].reshape(2048, 128).astype(F32).T.astype(BF)
    old = lax.broadcasted_iota(jnp.int32, (128, 128), 1)
    new = lax.broadcasted_iota(jnp.int32, (128, 128), 0)
    order = (old == (new % 8) * 16 + new // 8).astype(F32).astype(BF)
    for i in range(4):
        nearc[i] = lax.dot_general(coef_ref[i], order, (((0,), (1,)), ((), ())), preferred_element_type=F32).astype(BF)

    place = lax.broadcasted_iota(jnp.int32, (256, 128), 0).astype(F32).astype(BF)
    one, zero = jnp.ones((), BF), jnp.zeros((), BF)
    granule = lax.broadcasted_iota(jnp.int32, (8, 128), 1) // 16

    def finish(p):
        j = p // 4
        i = p % 4
        r_hi = right[...].astype(BF)
        r_lo = (right[...] - r_hi.astype(F32)).astype(BF)
        left = acc[64:96, :]
        l_hi = left.astype(BF)
        l_lo = (left - l_hi.astype(F32)).astype(BF)
        low = jnp.dot(r_lo, l_hi, preferred_element_type=F32) + jnp.dot(r_hi, l_lo, preferred_element_type=F32)
        direct = acc[0:64, :] + (jnp.dot(r_hi, l_hi, preferred_element_type=F32) + low)
        tiles = []
        for half in range(2):
            t = [direct[8 * v : 8 * v + 8, 128 * half : 128 * half + 128] for v in range(8)]
            for s in (1, 2, 4):
                upper = (granule & s) != 0
                n = list(t)
                for v in range(8):
                    if not v & s:
                        a, b = t[v], t[v | s]
                        n[v] = jnp.where(upper, pltpu.roll(b, 16 * s, 1), a)
                        n[v | s] = jnp.where(upper, b, pltpu.roll(a, 128 - 16 * s, 1))
                t = n
            tiles += t
        block = jnp.concatenate(tiles, axis=0).astype(BF)
        half = jnp.dot(block, farc[j], preferred_element_type=F32).astype(BF)
        out = jnp.dot(nearc[i], half, preferred_element_type=F32)
        at_i = pl.ds(pl.multiple_of(i * 128, 128), 128)
        at_j = pl.ds(pl.multiple_of(j * 128, 128), 128)
        o_ref[at_i, at_j] = out.astype(BF)
        kt[at_j, at_i] = out.T.astype(BF)

    def pair(p, _):
        finish(jnp.maximum(p - 1, 0))
        j = p // 4
        i = p % 4
        index = map_ref[t_ref[i, 2 * col + j]]
        scaled[64:96, :] = cols[j, pl.ds(pl.multiple_of(32 * i, 32), 32), :]
        for m in range(16):
            cs = slice(128 * m, 128 * m + 128)
            if m % 2 == 0:
                pick_low = [
                    jnp.where(place == (index[n : n + 1, :] & 255).astype(F32).astype(BF), one, zero) for n in (m, m + 1)
                ]
                both = jnp.dot(far[j], jnp.concatenate(pick_low, axis=1), preferred_element_type=F32)
            high = jnp.broadcast_to(index[m : m + 1, :] >> 8, (24, 128))
            ls = slice(128 * (m % 2), 128 * (m % 2) + 128)
            got = both[0:24, ls]
            for s in range(1, 8):
                got = jnp.where(high == s, both[24 * s : 24 * s + 24, ls], got)
            a = near_ref[i, :, cs].astype(F32)
            m_c = got[8:24, :].astype(BF)
            for c in range(NC):
                cond[16 * c : 16 * c + 16, cs] = wide_ref[i, c, :, cs] * m_c
            a_v = a[0:8, :]
            coul = coul_ref[m : m + 1, :]
            for v in range(0, NV, 2):
                x = jnp.concatenate([a_v * got[v : v + 1, :], a_v * got[v + 1 : v + 2, :]], axis=0).astype(BF)
                val[8 * v : 8 * v + 16, cs] = x
                scaled[8 * v : 8 * v + 16, cs] = (coul * x.astype(F32)).astype(BF)
            if m % 2:
                ks = slice(128 * m - 128, 128 * m + 128)
                part = lax.dot_general(scaled[:, ks], cond[:, ks], NT, preferred_element_type=F32)
                total = part if m == 1 else total + part
        acc[...] = total
        right[...] = lax.dot_general(val[...], scaled[64:96, :], NT, preferred_element_type=F32)
        return 0

    lax.fori_loop(0, 8, pair, 0)
    finish(7)

    odd = (col & 1) == 1
    both = r_ref[:, 160:168, :].reshape(256, 128).astype(F32)
    lane = lax.broadcasted_iota(jnp.int32, (256, 128), 1)
    other = pltpu.roll(both, 64, 1)
    first = jnp.where(lane < 64, jnp.where(odd, other, both), 0.0).astype(BF)
    second = jnp.where(lane < 64, 0.0, jnp.where(odd, both, other)).astype(BF)
    y = jnp.dot(o_ref[0:256, :], first, preferred_element_type=F32)
    y = y + jnp.dot(o_ref[256:512, :], second, preferred_element_type=F32)
    y_hi = y.astype(BF)
    send_ref[:, 0:8, :] = y_hi.reshape(32, 8, 128)
    send_ref[:, 8:16, :] = (y - y_hi.astype(F32)).astype(BF).reshape(32, 8, 128)
    for b in range(4):
        send_ref[:, 16 + 8 * b : 24 + 8 * b, :] = kt[:, 128 * b : 128 * b + 128].reshape(32, 8, 128)


def pair_blocks(table, received, near, wide, coef, coulomb, shift_map):
    return pl.pallas_call(
        pair_kernel,
        in_specs=[SM, VM, VM, VM, VM, VM, VM],
        out_specs=(VM, VM),
        out_shape=(jax.ShapeDtypeStruct((512, 256), BF), jax.ShapeDtypeStruct((32, 48, 128), BF)),
        scratch_shapes=[
            pltpu.VMEM((2, 192, 256), BF),
            pltpu.VMEM((2, 128, 128), BF),
            pltpu.VMEM((4, 128, 128), BF),
            pltpu.VMEM((2, 128, 2048), BF),
            pltpu.VMEM((256, 2048), BF),
            pltpu.VMEM((64, 2048), BF),
            pltpu.VMEM((96, 2048), BF),
            pltpu.VMEM((96, 256), F32),
            pltpu.VMEM((64, 32), F32),
            pltpu.VMEM((256, 512), BF),
        ],
        compiler_params=pltpu.CompilerParams(vmem_limit_bytes=32 << 20),
        name="pairs",
    )(table, received, near, wide, coef, coulomb, shift_map)


def fold_rows(square):
    lane = lax.broadcasted_iota(jnp.int32, (32, 128), 1)
    return jnp.where(lane < 64, square[0:32], pltpu.roll(square[32:64], 64, 1))


def second_kernel(r_ref, x_ref, o_ref):
    lane = lax.broadcasted_iota(jnp.int32, (8, 128), 1)
    parts = []
    for m in range(16):
        x = x_ref[m]
        high = x.astype(BF).astype(F32)
        low = x - high
        parts.append(jnp.where(lane < 64, high, pltpu.roll(low, 64, 1)))
        parts.append(jnp.where(lane < 64, pltpu.roll(high, 64, 1), low))
    x = jnp.concatenate(parts, axis=0)
    xt = x.T.astype(BF)
    sums = []
    for b in range(4):
        g = jnp.dot(xt, r_ref[:, 16 + 8 * b : 24 + 8 * b, :].reshape(256, 128), preferred_element_type=F32)
        sums.append(g[0:64] + g[64:128])
    for b in range(2):
        y = jnp.concatenate([sums[b], sums[b + 2]], axis=0).T
        o_ref[16 * b : 16 * b + 16, 0:8, :] = y.reshape(16, 8, 128)
    corr = jnp.dot(xt, x.astype(BF), preferred_element_type=F32)
    corr = corr + pltpu.roll(corr, 64, 1)
    corr = fold_rows(corr[0:64] + corr[64:128])
    o_ref[:, 8:9, :] = corr.reshape(32, 1, 128)


def second_product(received, x):
    return pl.pallas_call(
        second_kernel,
        out_shape=jax.ShapeDtypeStruct((32, 9, 128), F32),
        in_specs=[VM, VM],
        out_specs=VM,
        name="second",
    )(received, x)


def pack_symmetric(square):
    lane = lax.broadcasted_iota(jnp.int32, (32, 128), 1)
    row = lax.broadcasted_iota(jnp.int32, (32, 128), 0)
    corner = pltpu.roll(square[32:64], 96, 1)
    values = jnp.where(lane < row, corner, square[0:32])
    diagonal = jnp.sum(jnp.where(lane == row, corner, 0.0), axis=0, keepdims=True)
    values = jnp.where(lane[0:16] < 64, values[0:16], pltpu.roll(values[16:32], 64, 1))
    high = values.astype(BF).astype(F32)
    tail = jnp.broadcast_to(diagonal, (8, 128))
    tail_high = tail.astype(BF).astype(F32)
    tail = jnp.where(row[0:8] == 0, tail_high, jnp.where(row[0:8] == 1, tail - tail_high, 0.0))
    return jnp.concatenate([high, values - high, tail], axis=0).astype(BF)


def unpack_symmetric(parts):
    lane = lax.broadcasted_iota(jnp.int32, (32, 128), 1)
    row = lax.broadcasted_iota(jnp.int32, (32, 128), 0)
    values = parts[0:16] + parts[16:32]
    values = jnp.concatenate([values, pltpu.roll(values, 64, 1)], axis=0)
    diagonal = jnp.broadcast_to(pltpu.roll(parts[32:40], 32, 1)[0:1] + pltpu.roll(parts[32:40], 32, 1)[1:2], (32, 128))
    top = jnp.where(lane < row, 0.0, jnp.where(lane == row, 0.5 * values, values))
    top = jnp.where(lane < 64, top, 0.0)
    low = pltpu.roll(values, 32, 1)
    low = jnp.where(lane - 32 < row, low, jnp.where(lane - 32 == row, 0.5 * diagonal, 0.0))
    low = jnp.where(lane < 32, 0.0, low)
    half = jnp.concatenate([top, low, jnp.zeros((64, 128), F32)], axis=0)
    return half[0:64] + half.T[0:64]


def unfold_rows(packed):
    return jnp.concatenate([packed, pltpu.roll(packed, 64, 1)], axis=0)


def inverse_factor(full, scale):
    lane = lax.broadcasted_iota(jnp.int32, (64, 128), 1)
    row = lax.broadcasted_iota(jnp.int32, (64, 128), 0)
    work = jnp.where(lane < 64, full * scale, (lane - 64 == row).astype(F32))
    done = []
    tiles = [work[8 * t : 8 * t + 8] for t in range(8)]
    for t in range(8):
        column = {u: [jnp.broadcast_to(tiles[u][:, 8 * t + k : 8 * t + k + 1], (8, 128)) for k in range(8)] for u in range(t, 8)}
        for k in range(8):
            pivot = column[t][k][k : k + 1, :]
            y = lax.rsqrt(pivot)
            square = y * y
            near_one = pivot * square
            inverse = square * (2.0 - near_one)
            line = tiles[t][k : k + 1, :]
            done.append(line * (y * (1.5 - 0.5 * near_one)))
            line = line * inverse
            ahead = {m: column[t][m][k : k + 1, :] * inverse for m in range(k + 1, 8)}
            for u in range(t, 8):
                factor = column[u][k]
                for m in range(k + 1, 8):
                    column[u][m] = column[u][m] - factor * ahead[m]
                tiles[u] = tiles[u] - factor * line
    return jnp.concatenate(done, axis=0)


def lane_halves(inv):
    lane = lax.broadcasted_iota(jnp.int32, (64, 128), 1)
    return jnp.where(lane < 64, pltpu.roll(inv, 64, 1), 0.0), jnp.where(lane < 64, 0.0, inv)


def apply_inverse(x, inv):
    both = jnp.concatenate(lane_halves(inv), axis=0)
    return lax.dot_general(x, both, NT, precision=HIGH, preferred_element_type=F32)


def middle_kernel(g_ref, image_ref, corr_ref, *, scale):
    packed = g_ref[:, 8:9, :].reshape(32, 128)
    inv = inverse_factor(unfold_rows(packed), scale)
    image = apply_inverse(g_ref[:, 0:8, :].reshape(256, 128), inv)
    image_ref[...] = image
    corr = lax.dot_general(image, image, TN, precision=HIGH, preferred_element_type=F32)
    corr = corr[0:64] + pltpu.roll(corr[64:128], 64, 1)
    corr = pack_symmetric(corr)
    for m in range(16):
        corr_ref[m] = corr


def middle(g, scale):
    return pl.pallas_call(
        lambda *refs: middle_kernel(*refs, scale=scale),
        out_shape=(jax.ShapeDtypeStruct((256, 128), F32), jax.ShapeDtypeStruct((16, 40, 128), BF)),
        in_specs=[VM],
        out_specs=(VM, VM),
        name="middle",
    )(g)


def last_kernel(image_ref, corr_ref, o_ref, *, scale):
    parts = corr_ref[0].astype(F32)
    for m in range(1, 16):
        parts = parts + corr_ref[m].astype(F32)
    inv = inverse_factor(unpack_symmetric(parts), scale)
    upper, lower = lane_halves(inv)
    image = image_ref[...]
    o_ref[:, 0:256] = lax.dot_general(upper, image, NT, precision=HIGH, preferred_element_type=F32)
    o_ref[:, 256:512] = lax.dot_general(lower, image, NT, precision=HIGH, preferred_element_type=F32)


def last(image, corr, scale):
    return pl.pallas_call(
        lambda *refs: last_kernel(*refs, scale=scale),
        out_shape=jax.ShapeDtypeStruct((64, 512), F32),
        in_specs=[VM, VM],
        out_specs=VM,
        name="last",
    )(image, corr).T


def to_all(x, axis):
    size = lax.axis_size(axis)
    return lax.all_to_all(jnp.broadcast_to(x[None], (size, *x.shape)), axis, 0, 0, tiled=True)


def on_device(band_form, interp_coef, screen, coulomb, shift_map, grid_order, energies, initial):
    piece, starts, diagonal, table = share(band_form, interp_coef, screen, initial, energies, grid_order)
    gathered = lax.all_gather(piece, "ka", axis=0, tiled=False)
    received = lax.all_to_all(pick(vmem(gathered), table), "kp", 0, 0, tiled=True)
    wide = vmem(prepare(band_form))
    kernel, sent = pair_blocks(
        table, vmem(received), band_form, wide, interp_coef, coulomb.reshape(16, 128), vmem(shift_map.reshape(64, 16, 128))
    )
    sent = lax.all_to_all(sent, "kp", 0, 0, tiled=True)
    image = jnp.sum(sent[:, 0:16, :].astype(F32).reshape(64, 8, 128), axis=0) + diagonal * starts

    sums = jnp.sum(lax.all_to_all(second_product(vmem(sent), vmem(to_all(image, "ka"))), "kp", 0, 0, tiled=True), axis=0)
    sums = sums + jnp.concatenate([diagonal * image, jnp.zeros((1, 128), F32)], axis=0)
    everyone = to_all(sums, "kp")
    scale = 1.0 / 8192
    image, corr = middle(vmem(everyone), scale)
    vectors = last(vmem(image), vmem(lax.all_to_all(corr, "ka", 0, 0, tiled=True)), scale)
    return (kernel, vectors)


def solution(mesh):
    return jax.shard_map(
        on_device,
        mesh=mesh,
        in_specs=(
            P("ka", None, None),
            P("ka", None, None),
            P("ka", "kp", None),
            P(),
            P(),
            P(),
            P("ka"),
            P("ka", None),
        ),
        out_specs=(P("ka", "kp"), P("ka", None)),
        check_vma=False,
    )
```

```python
import jax
import jax.numpy as jnp
from jax import lax
from jax.experimental import pallas as pl
from jax.experimental.pallas import tpu as pltpu
from jax.sharding import PartitionSpec as P

NV, NC = 8, 16
GRID_Y = 8
GRID_X = 8
BF, F32 = jnp.bfloat16, jnp.float32
HIGH = lax.Precision.HIGHEST
VM = pl.BlockSpec(memory_space=pltpu.VMEM)
SM = pl.BlockSpec(memory_space=pltpu.SMEM)
SMALL = pltpu.CompilerParams(vmem_limit_bytes=16 << 20)


def device_at(axis):
    return lax.axis_index(axis)


def vmem(x):
    return pltpu.with_memory_space_constraint(x, pltpu.VMEM)


def share_kernel(form_ref, coef_ref, screen_ref, start_ref, energy_ref, cell_ref, cells_ref, piece_ref, first_ref, diagonal_ref, table_ref, form, coef, sems):
    plane, col = device_at("ka"), device_at("kp")
    odd = (col & 1) == 1
    copies = (
        pltpu.make_async_copy(form_ref.at[:, :, pl.ds(pl.multiple_of(128 * (col // 2), 128), 128)], form, sems.at[0]),
        pltpu.make_async_copy(coef_ref.at[:, pl.ds(pl.multiple_of(8 * (col // 2), 8), 8), :], coef, sems.at[1]),
    )
    for copy in copies:
        copy.start()
    x, y = cells_ref[...] >> 3, cells_ref[...] & 7
    for i in range(4):
        cell = cell_ref[4 * plane + i]
        table_ref[i : i + 1, :] = (((cell >> 3) - x) & 7) * 8 + (((cell & 7) - y) & 7)
    piece_ref[0:64, :] = jnp.concatenate([screen_ref[q].astype(F32) for q in range(4)], axis=0).T.astype(BF)
    block = col // 16
    back = (128 - 8 * (col % 16)) % 128

    def rows_of(parts):
        both = jnp.concatenate([pltpu.roll(part, back, 1) for part in parts], axis=0)
        return both.T[0:8]

    first = rows_of([start_ref[:, pl.ds(pl.multiple_of(256 * h + 128 * block, 128), 128)] for h in range(2)])
    first_ref[...] = first
    diagonal_ref[...] = rows_of([jnp.broadcast_to(energy_ref[pl.ds(2 * h + block, 1), :], (64, 128)) for h in range(2)])
    piece_ref[128:136, :] = first.astype(BF)
    lane = lax.broadcasted_iota(jnp.int32, (24, 128), 1)
    row = lax.broadcasted_iota(jnp.int32, (8, 128), 0)
    copies[0].wait()
    copies[1].wait()
    for h in range(2):
        a, b = form[2 * h].astype(F32), form[2 * h + 1].astype(F32)
        low = jnp.where(odd, pltpu.roll(a, 64, 1), a)
        high = jnp.where(odd, b, pltpu.roll(b, 64, 1))
        piece_ref[64 + 24 * h : 88 + 24 * h, :] = jnp.where(lane < 64, low, high).astype(BF)
        a, b = coef[2 * h].astype(F32), coef[2 * h + 1].astype(F32)
        low = jnp.where(odd, pltpu.roll(a, 4, 0), a)
        high = jnp.where(odd, b, pltpu.roll(b, 4, 0))
        piece_ref[112 + 8 * h : 120 + 8 * h, :] = jnp.where(row < 4, low, high).astype(BF)


def share(forms, coefs, screen, initial, energies, cells):
    hbm = pl.BlockSpec(memory_space=pl.ANY)
    return pl.pallas_call(
        share_kernel,
        in_specs=[hbm, hbm, VM, VM, VM, SM, VM],
        out_specs=(VM, VM, VM, VM),
        out_shape=(
            jax.ShapeDtypeStruct((136, 128), BF),
            jax.ShapeDtypeStruct((8, 128), F32),
            jax.ShapeDtypeStruct((8, 128), F32),
            jax.ShapeDtypeStruct((4, 64), jnp.int32),
        ),
        scratch_shapes=[pltpu.VMEM((4, 24, 128), BF), pltpu.VMEM((4, 8, 128), BF), pltpu.SemaphoreType.DMA((2,))],
        compiler_params=SMALL,
        name="share",
    )(forms, coefs, screen.transpose(0, 2, 1), initial.T, energies.reshape(4, 128), cells, cells.reshape(1, 64))


def pick_kernel(t_ref, g_ref, o_ref, rolled):
    def roll_one(h, _):
        x = g_ref[h, 0:64, :].astype(F32)
        rolled[0, h] = x.astype(BF)
        for s in range(1, 4):
            rolled[s, h] = pltpu.roll(x, 32 * s, 1).astype(BF)
        return 0

    lax.fori_loop(0, 16, roll_one, 0, unroll=4)
    lane_block = lax.broadcasted_iota(jnp.int32, (64, 128), 1) // 32

    def dest(d, _):
        for j in range(2):
            acc = None
            for i in range(4):
                q = t_ref[i, 2 * d + j]
                tile = rolled[(i - q) & 3, q >> 2].astype(F32)
                acc = tile if acc is None else jnp.where(lane_block == i, tile, acc)
            o_ref[d, 64 * j : 64 * j + 64, :] = acc.astype(BF)
        half = d & 1
        plane = d >> 1
        o_ref[d, 128:152, :] = g_ref[plane, pl.ds(pl.multiple_of(64 + 24 * half, 8), 24), :]
        o_ref[d, 152:160, :] = g_ref[plane, pl.ds(pl.multiple_of(112 + 8 * half, 8), 8), :]
        o_ref[d, 160:168, :] = g_ref[plane, 128:136, :]
        return 0

    lax.fori_loop(0, 32, dest, 0, unroll=4)


def pick(gathered, table):
    return pl.pallas_call(
        pick_kernel,
        out_shape=jax.ShapeDtypeStruct((32, 168, 128), BF),
        in_specs=[pl.BlockSpec(memory_space=pltpu.SMEM), pl.BlockSpec(memory_space=pltpu.VMEM)],
        out_specs=pl.BlockSpec(memory_space=pltpu.VMEM),
        scratch_shapes=[pltpu.VMEM((4, 16, 64, 128), BF)],
        compiler_params=SMALL,
        name="pick",
    )(table, gathered)


NT = (((1,), (1,)), ((), ()))
TN = (((0,), (0,)), ((), ()))


def prepare_kernel(form_ref, o_ref):
    for c in range(NC):
        o_ref[0, c] = jnp.broadcast_to(form_ref[0, 8 + c : 9 + c, :].astype(F32), (16, 2048)).astype(BF)


def prepare(near):
    return pl.pallas_call(
        prepare_kernel,
        grid=(4,),
        in_specs=[pl.BlockSpec((1, 24, 2048), lambda i: (i, 0, 0))],
        out_specs=pl.BlockSpec((1, 16, 16, 2048), lambda i: (i, 0, 0, 0)),
        out_shape=jax.ShapeDtypeStruct((4, 16, 16, 2048), BF),
        compiler_params=pltpu.CompilerParams(vmem_limit_bytes=32 << 20),
        name="prepare",
    )(near)


def pair_kernel(t_ref, r_ref, near_ref, wide_hbm, coef_ref, coul_ref, map_ref, o_ref, send_ref, far, farc, nearc, cols, cond, val, scaled, acc, right, kt, wide_ref, sems):
    def wide_copy(i):
        return pltpu.make_async_copy(wide_hbm.at[i], wide_ref.at[i], sems.at[i])

    for i in range(4):
        wide_copy(i).start()
    col = device_at("kp")
    lane24 = lax.broadcasted_iota(jnp.int32, (24, 128), 1)
    for m in range(16):
        lo = r_ref[2 * m, 128:152, :].astype(F32)
        hi = r_ref[2 * m + 1, 128:152, :].astype(F32)
        at = (slice(24 * (m // 2), 24 * (m // 2) + 24), slice(128 * (m % 2), 128 * (m % 2) + 128))
        far[(0, *at)] = jnp.where(lane24 < 64, lo, pltpu.roll(hi, 64, 1)).astype(BF)
        far[(1, *at)] = jnp.where(lane24 < 64, pltpu.roll(lo, 64, 1), hi).astype(BF)
    rows = r_ref[:, 152:160, :].reshape(256, 128)
    out_row = lax.broadcasted_iota(jnp.int32, (128, 256), 0)
    in_row = lax.broadcasted_iota(jnp.int32, (128, 256), 1)
    for k in range(2):
        sel = (in_row == (out_row // 4) * 8 + k * 4 + out_row % 4).astype(F32).astype(BF)
        farc[k] = jnp.dot(sel, rows, preferred_element_type=F32).astype(BF)
        cols[k] = r_ref[:, 64 * k : 64 * k + 64, :].reshape(2048, 128).astype(F32).T.astype(BF)
    old = lax.broadcasted_iota(jnp.int32, (128, 128), 1)
    new = lax.broadcasted_iota(jnp.int32, (128, 128), 0)
    order = (old == (new % 8) * 16 + new // 8).astype(F32).astype(BF)
    for i in range(4):
        nearc[i] = lax.dot_general(coef_ref[i], order, (((0,), (1,)), ((), ())), preferred_element_type=F32).astype(BF)

    place = lax.broadcasted_iota(jnp.int32, (256, 128), 0).astype(F32).astype(BF)
    one, zero = jnp.ones((), BF), jnp.zeros((), BF)
    granule = lax.broadcasted_iota(jnp.int32, (8, 128), 1) // 16

    def finish(p):
        j = p // 4
        i = p % 4
        r_hi = right[...].astype(BF)
        r_lo = (right[...] - r_hi.astype(F32)).astype(BF)
        left = acc[64:96, :]
        l_hi = left.astype(BF)
        l_lo = (left - l_hi.astype(F32)).astype(BF)
        low = jnp.dot(r_lo, l_hi, preferred_element_type=F32) + jnp.dot(r_hi, l_lo, preferred_element_type=F32)
        direct = acc[0:64, :] + (jnp.dot(r_hi, l_hi, preferred_element_type=F32) + low)
        tiles = []
        for half in range(2):
            t = [direct[8 * v : 8 * v + 8, 128 * half : 128 * half + 128] for v in range(8)]
            for s in (1, 2, 4):
                upper = (granule & s) != 0
                n = list(t)
                for v in range(8):
                    if not v & s:
                        a, b = t[v], t[v | s]
                        n[v] = jnp.where(upper, pltpu.roll(b, 16 * s, 1), a)
                        n[v | s] = jnp.where(upper, b, pltpu.roll(a, 128 - 16 * s, 1))
                t = n
            tiles += t
        block = jnp.concatenate(tiles, axis=0).astype(BF)
        half = jnp.dot(block, farc[j], preferred_element_type=F32).astype(BF)
        out = jnp.dot(nearc[i], half, preferred_element_type=F32)
        at_i = pl.ds(pl.multiple_of(i * 128, 128), 128)
        at_j = pl.ds(pl.multiple_of(j * 128, 128), 128)
        o_ref[at_i, at_j] = out.astype(BF)
        kt[at_j, at_i] = out.T.astype(BF)

    def pair(p, _):
        @pl.when(p < 4)
        def _():
            wide_copy(p).wait()

        finish(jnp.maximum(p - 1, 0))
        j = p // 4
        i = p % 4
        index = map_ref[t_ref[i, 2 * col + j]]
        scaled[64:96, :] = cols[j, pl.ds(pl.multiple_of(32 * i, 32), 32), :]
        for m in range(16):
            cs = slice(128 * m, 128 * m + 128)
            if m % 2 == 0:
                pick_low = [
                    jnp.where(place == (index[n : n + 1, :] & 255).astype(F32).astype(BF), one, zero) for n in (m, m + 1)
                ]
                both = jnp.dot(far[j], jnp.concatenate(pick_low, axis=1), preferred_element_type=F32)
            high = jnp.broadcast_to(index[m : m + 1, :] >> 8, (24, 128))
            ls = slice(128 * (m % 2), 128 * (m % 2) + 128)
            got = both[0:24, ls]
            for s in range(1, 8):
                got = jnp.where(high == s, both[24 * s : 24 * s + 24, ls], got)
            a = near_ref[i, :, cs].astype(F32)
            m_c = got[8:24, :].astype(BF)
            for c in range(NC):
                cond[16 * c : 16 * c + 16, cs] = wide_ref[i, c, :, cs] * m_c
            a_v = a[0:8, :]
            coul = coul_ref[m : m + 1, :]
            for v in range(0, NV, 2):
                x = jnp.concatenate([a_v * got[v : v + 1, :], a_v * got[v + 1 : v + 2, :]], axis=0).astype(BF)
                val[8 * v : 8 * v + 16, cs] = x
                scaled[8 * v : 8 * v + 16, cs] = (coul * x.astype(F32)).astype(BF)
            if m % 2:
                ks = slice(128 * m - 128, 128 * m + 128)
                part = lax.dot_general(scaled[:, ks], cond[:, ks], NT, preferred_element_type=F32)
                total = part if m == 1 else total + part
        acc[...] = total
        right[...] = lax.dot_general(val[...], scaled[64:96, :], NT, preferred_element_type=F32)
        return 0

    lax.fori_loop(0, 8, pair, 0)
    finish(7)

    odd = (col & 1) == 1
    both = r_ref[:, 160:168, :].reshape(256, 128).astype(F32)
    lane = lax.broadcasted_iota(jnp.int32, (256, 128), 1)
    other = pltpu.roll(both, 64, 1)
    first = jnp.where(lane < 64, jnp.where(odd, other, both), 0.0).astype(BF)
    second = jnp.where(lane < 64, 0.0, jnp.where(odd, both, other)).astype(BF)
    y = jnp.dot(o_ref[0:256, :], first, preferred_element_type=F32)
    y = y + jnp.dot(o_ref[256:512, :], second, preferred_element_type=F32)
    y_hi = y.astype(BF)
    send_ref[:, 0:8, :] = y_hi.reshape(32, 8, 128)
    send_ref[:, 8:16, :] = (y - y_hi.astype(F32)).astype(BF).reshape(32, 8, 128)
    for b in range(4):
        send_ref[:, 16 + 8 * b : 24 + 8 * b, :] = kt[:, 128 * b : 128 * b + 128].reshape(32, 8, 128)


def pair_blocks(table, received, near, wide, coef, coulomb, shift_map):
    return pl.pallas_call(
        pair_kernel,
        in_specs=[SM, VM, VM, pl.BlockSpec(memory_space=pl.ANY), VM, VM, VM],
        out_specs=(VM, VM),
        out_shape=(jax.ShapeDtypeStruct((512, 256), BF), jax.ShapeDtypeStruct((32, 48, 128), BF)),
        scratch_shapes=[
            pltpu.VMEM((2, 192, 256), BF),
            pltpu.VMEM((2, 128, 128), BF),
            pltpu.VMEM((4, 128, 128), BF),
            pltpu.VMEM((2, 128, 2048), BF),
            pltpu.VMEM((256, 2048), BF),
            pltpu.VMEM((64, 2048), BF),
            pltpu.VMEM((96, 2048), BF),
            pltpu.VMEM((96, 256), F32),
            pltpu.VMEM((64, 32), F32),
            pltpu.VMEM((256, 512), BF),
            pltpu.VMEM((4, 16, 16, 2048), BF),
            pltpu.SemaphoreType.DMA((4,)),
        ],
        compiler_params=pltpu.CompilerParams(vmem_limit_bytes=32 << 20),
        name="pairs",
    )(table, received, near, wide, coef, coulomb, shift_map)


def fold_rows(square):
    lane = lax.broadcasted_iota(jnp.int32, (32, 128), 1)
    return jnp.where(lane < 64, square[0:32], pltpu.roll(square[32:64], 64, 1))


def second_kernel(r_ref, x_ref, o_ref):
    lane = lax.broadcasted_iota(jnp.int32, (8, 128), 1)
    parts = []
    for m in range(16):
        x = x_ref[m]
        high = x.astype(BF).astype(F32)
        low = x - high
        parts.append(jnp.where(lane < 64, high, pltpu.roll(low, 64, 1)))
        parts.append(jnp.where(lane < 64, pltpu.roll(high, 64, 1), low))
    x = jnp.concatenate(parts, axis=0)
    xt = x.T.astype(BF)
    sums = []
    for b in range(4):
        g = jnp.dot(xt, r_ref[:, 16 + 8 * b : 24 + 8 * b, :].reshape(256, 128), preferred_element_type=F32)
        sums.append(g[0:64] + g[64:128])
    for b in range(2):
        y = jnp.concatenate([sums[b], sums[b + 2]], axis=0).T
        o_ref[16 * b : 16 * b + 16, 0:8, :] = y.reshape(16, 8, 128)
    corr = jnp.dot(xt, x.astype(BF), preferred_element_type=F32)
    corr = corr + pltpu.roll(corr, 64, 1)
    corr = fold_rows(corr[0:64] + corr[64:128])
    o_ref[:, 8:9, :] = corr.reshape(32, 1, 128)


def second_product(received, x):
    return pl.pallas_call(
        second_kernel,
        out_shape=jax.ShapeDtypeStruct((32, 9, 128), F32),
        in_specs=[VM, VM],
        out_specs=VM,
        compiler_params=SMALL,
        name="second",
    )(received, x)


def pack_symmetric(square):
    lane = lax.broadcasted_iota(jnp.int32, (32, 128), 1)
    row = lax.broadcasted_iota(jnp.int32, (32, 128), 0)
    corner = pltpu.roll(square[32:64], 96, 1)
    values = jnp.where(lane < row, corner, square[0:32])
    diagonal = jnp.sum(jnp.where(lane == row, corner, 0.0), axis=0, keepdims=True)
    values = jnp.where(lane[0:16] < 64, values[0:16], pltpu.roll(values[16:32], 64, 1))
    high = values.astype(BF).astype(F32)
    tail = jnp.broadcast_to(diagonal, (8, 128))
    tail_high = tail.astype(BF).astype(F32)
    tail = jnp.where(row[0:8] == 0, tail_high, jnp.where(row[0:8] == 1, tail - tail_high, 0.0))
    return jnp.concatenate([high, values - high, tail], axis=0).astype(BF)


def unpack_symmetric(parts):
    lane = lax.broadcasted_iota(jnp.int32, (32, 128), 1)
    row = lax.broadcasted_iota(jnp.int32, (32, 128), 0)
    values = parts[0:16] + parts[16:32]
    values = jnp.concatenate([values, pltpu.roll(values, 64, 1)], axis=0)
    diagonal = jnp.broadcast_to(pltpu.roll(parts[32:40], 32, 1)[0:1] + pltpu.roll(parts[32:40], 32, 1)[1:2], (32, 128))
    top = jnp.where(lane < row, 0.0, jnp.where(lane == row, 0.5 * values, values))
    top = jnp.where(lane < 64, top, 0.0)
    low = pltpu.roll(values, 32, 1)
    low = jnp.where(lane - 32 < row, low, jnp.where(lane - 32 == row, 0.5 * diagonal, 0.0))
    low = jnp.where(lane < 32, 0.0, low)
    half = jnp.concatenate([top, low, jnp.zeros((64, 128), F32)], axis=0)
    return half[0:64] + half.T[0:64]


def unfold_rows(packed):
    return jnp.concatenate([packed, pltpu.roll(packed, 64, 1)], axis=0)


def inverse_factor(full, scale):
    lane = lax.broadcasted_iota(jnp.int32, (64, 128), 1)
    row = lax.broadcasted_iota(jnp.int32, (64, 128), 0)
    work = jnp.where(lane < 64, full * scale, (lane - 64 == row).astype(F32))
    done = []
    tiles = [work[8 * t : 8 * t + 8] for t in range(8)]
    for t in range(8):
        column = {u: [jnp.broadcast_to(tiles[u][:, 8 * t + k : 8 * t + k + 1], (8, 128)) for k in range(8)] for u in range(t, 8)}
        for k in range(8):
            pivot = column[t][k][k : k + 1, :]
            y = lax.rsqrt(pivot)
            square = y * y
            near_one = pivot * square
            inverse = square * (2.0 - near_one)
            line = tiles[t][k : k + 1, :]
            done.append(line * (y * (1.5 - 0.5 * near_one)))
            line = line * inverse
            ahead = {m: column[t][m][k : k + 1, :] * inverse for m in range(k + 1, 8)}
            for u in range(t, 8):
                factor = column[u][k]
                for m in range(k + 1, 8):
                    column[u][m] = column[u][m] - factor * ahead[m]
                tiles[u] = tiles[u] - factor * line
    return jnp.concatenate(done, axis=0)


def lane_halves(inv):
    lane = lax.broadcasted_iota(jnp.int32, (64, 128), 1)
    return jnp.where(lane < 64, pltpu.roll(inv, 64, 1), 0.0), jnp.where(lane < 64, 0.0, inv)


def apply_inverse(x, inv):
    both = jnp.concatenate(lane_halves(inv), axis=0)
    return lax.dot_general(x, both, NT, precision=HIGH, preferred_element_type=F32)


def middle_kernel(g_ref, image_ref, corr_ref, *, scale):
    packed = g_ref[:, 8:9, :].reshape(32, 128)
    inv = inverse_factor(unfold_rows(packed), scale)
    image = apply_inverse(g_ref[:, 0:8, :].reshape(256, 128), inv)
    image_ref[...] = image
    corr = lax.dot_general(image, image, TN, precision=HIGH, preferred_element_type=F32)
    corr = corr[0:64] + pltpu.roll(corr[64:128], 64, 1)
    corr = pack_symmetric(corr)
    for m in range(16):
        corr_ref[m] = corr


def middle(g, scale):
    return pl.pallas_call(
        lambda *refs: middle_kernel(*refs, scale=scale),
        out_shape=(jax.ShapeDtypeStruct((256, 128), F32), jax.ShapeDtypeStruct((16, 40, 128), BF)),
        in_specs=[VM],
        out_specs=(VM, VM),
        compiler_params=SMALL,
        name="middle",
    )(g)


def last_kernel(image_ref, corr_ref, o_ref, *, scale):
    parts = corr_ref[0].astype(F32)
    for m in range(1, 16):
        parts = parts + corr_ref[m].astype(F32)
    inv = inverse_factor(unpack_symmetric(parts), scale)
    upper, lower = lane_halves(inv)
    image = image_ref[...]
    o_ref[:, 0:256] = lax.dot_general(upper, image, NT, precision=HIGH, preferred_element_type=F32)
    o_ref[:, 256:512] = lax.dot_general(lower, image, NT, precision=HIGH, preferred_element_type=F32)


def last(image, corr, scale):
    return pl.pallas_call(
        lambda *refs: last_kernel(*refs, scale=scale),
        out_shape=jax.ShapeDtypeStruct((64, 512), F32),
        in_specs=[VM, VM],
        out_specs=VM,
        compiler_params=SMALL,
        name="last",
    )(image, corr).T


def to_all(x, axis):
    size = lax.axis_size(axis)
    return lax.all_to_all(jnp.broadcast_to(x[None], (size, *x.shape)), axis, 0, 0, tiled=True)


def on_device(band_form, interp_coef, screen, coulomb, shift_map, grid_order, energies, initial):
    piece, starts, diagonal, table = share(band_form, interp_coef, screen, initial, energies, grid_order)
    gathered = lax.all_gather(piece, "ka", axis=0, tiled=False)
    received = lax.all_to_all(pick(vmem(gathered), table), "kp", 0, 0, tiled=True)
    wide = pltpu.with_memory_space_constraint(prepare(band_form), pltpu.HBM)
    kernel, sent = pair_blocks(
        table, vmem(received), band_form, wide, interp_coef, coulomb.reshape(16, 128), vmem(shift_map.reshape(64, 16, 128))
    )
    sent = lax.all_to_all(sent, "kp", 0, 0, tiled=True)
    image = jnp.sum(sent[:, 0:16, :].astype(F32).reshape(64, 8, 128), axis=0) + diagonal * starts

    sums = jnp.sum(lax.all_to_all(second_product(vmem(sent), vmem(to_all(image, "ka"))), "kp", 0, 0, tiled=True), axis=0)
    sums = sums + jnp.concatenate([diagonal * image, jnp.zeros((1, 128), F32)], axis=0)
    everyone = to_all(sums, "kp")
    scale = 1.0 / 8192
    image, corr = middle(vmem(everyone), scale)
    vectors = last(image, vmem(lax.all_to_all(corr, "ka", 0, 0, tiled=True)), scale)
    return (kernel, vectors)


def solution(mesh):
    return jax.shard_map(
        on_device,
        mesh=mesh,
        in_specs=(
            P("ka", None, None),
            P("ka", None, None),
            P("ka", "kp", None),
            P(),
            P(),
            P(),
            P("ka"),
            P("ka", None),
        ),
        out_specs=(P("ka", "kp"), P("ka", None)),
        check_vma=False,
    )
```

```python
import jax
import jax.numpy as jnp
from jax import lax
from jax.experimental import pallas as pl
from jax.experimental.pallas import tpu as pltpu
from jax.sharding import PartitionSpec as P

NV, NC = 8, 16
GRID_Y = 8
GRID_X = 8
BF, F32 = jnp.bfloat16, jnp.float32
HIGH = lax.Precision.HIGHEST
VM = pl.BlockSpec(memory_space=pltpu.VMEM)
SM = pl.BlockSpec(memory_space=pltpu.SMEM)
SMALL = pltpu.CompilerParams(vmem_limit_bytes=16 << 20)


def device_at(axis):
    return lax.axis_index(axis)


def vmem(x):
    return pltpu.with_memory_space_constraint(x, pltpu.VMEM)


def share_kernel(form_hbm, coef_hbm, screen_hbm, start_hbm, energy_hbm, cells_hbm, piece_ref, first_ref, diagonal_ref, table_ref, form, coef, screen_ref, start_ref, energy_ref, cells_ref, sems):
    plane, col = device_at("ka"), device_at("kp")
    odd = (col & 1) == 1
    moves = (
        (cells_hbm, cells_ref),
        (screen_hbm, screen_ref),
        (start_hbm, start_ref),
        (energy_hbm, energy_ref),
        (form_hbm.at[:, :, pl.ds(pl.multiple_of(128 * (col // 2), 128), 128)], form),
        (coef_hbm.at[:, pl.ds(pl.multiple_of(8 * (col // 2), 8), 8), :], coef),
    )
    copies = [pltpu.make_async_copy(src, dst, sems.at[n]) for n, (src, dst) in enumerate(moves)]
    for copy in copies:
        copy.start()
    for copy in copies:
        copy.wait()
    x, y = cells_ref[...] >> 3, cells_ref[...] & 7
    for i in range(4):
        own = lax.broadcasted_iota(jnp.int32, (1, 64), 1) == 4 * plane + i
        cell = jnp.sum(jnp.where(own, cells_ref[...], 0).astype(F32), axis=1, keepdims=True).astype(jnp.int32)
        table_ref[i : i + 1, :] = (((cell >> 3) - x) & 7) * 8 + (((cell & 7) - y) & 7)
    piece_ref[0:64, :] = jnp.concatenate([screen_ref[q].astype(F32) for q in range(4)], axis=0).T.astype(BF)
    block = col // 16
    back = (128 - 8 * (col % 16)) % 128

    def rows_of(parts):
        both = jnp.concatenate([pltpu.roll(part, back, 1) for part in parts], axis=0)
        return both.T[0:8]

    first = rows_of([start_ref[:, pl.ds(pl.multiple_of(256 * h + 128 * block, 128), 128)] for h in range(2)])
    first_ref[...] = first
    diagonal_ref[...] = rows_of([jnp.broadcast_to(energy_ref[pl.ds(2 * h + block, 1), :], (64, 128)) for h in range(2)])
    piece_ref[128:136, :] = first.astype(BF)
    lane = lax.broadcasted_iota(jnp.int32, (24, 128), 1)
    row = lax.broadcasted_iota(jnp.int32, (8, 128), 0)
    for h in range(2):
        a, b = form[2 * h].astype(F32), form[2 * h + 1].astype(F32)
        low = jnp.where(odd, pltpu.roll(a, 64, 1), a)
        high = jnp.where(odd, b, pltpu.roll(b, 64, 1))
        piece_ref[64 + 24 * h : 88 + 24 * h, :] = jnp.where(lane < 64, low, high).astype(BF)
        a, b = coef[2 * h].astype(F32), coef[2 * h + 1].astype(F32)
        low = jnp.where(odd, pltpu.roll(a, 4, 0), a)
        high = jnp.where(odd, b, pltpu.roll(b, 4, 0))
        piece_ref[112 + 8 * h : 120 + 8 * h, :] = jnp.where(row < 4, low, high).astype(BF)


def share(forms, coefs, screen, initial, energies, cells):
    hbm = pl.BlockSpec(memory_space=pltpu.HBM)
    return pl.pallas_call(
        share_kernel,
        in_specs=[hbm] * 6,
        out_specs=(VM, VM, VM, VM),
        out_shape=(
            jax.ShapeDtypeStruct((136, 128), BF),
            jax.ShapeDtypeStruct((8, 128), F32),
            jax.ShapeDtypeStruct((8, 128), F32),
            jax.ShapeDtypeStruct((4, 64), jnp.int32),
        ),
        scratch_shapes=[
            pltpu.VMEM((4, 24, 128), BF),
            pltpu.VMEM((4, 8, 128), BF),
            pltpu.VMEM((4, 32, 64), BF),
            pltpu.VMEM((64, 512), F32),
            pltpu.VMEM((4, 128), F32),
            pltpu.VMEM((1, 64), jnp.int32),
            pltpu.SemaphoreType.DMA((6,)),
        ],
        compiler_params=SMALL,
        name="share",
    )(*(pltpu.with_memory_space_constraint(x, pltpu.HBM) for x in (forms, coefs, screen.transpose(0, 2, 1), initial.T, energies.reshape(4, 128), cells.reshape(1, 64))))


def pick_kernel(t_ref, g_ref, o_ref, rolled):
    def roll_one(h, _):
        x = g_ref[h, 0:64, :].astype(F32)
        rolled[0, h] = x.astype(BF)
        for s in range(1, 4):
            rolled[s, h] = pltpu.roll(x, 32 * s, 1).astype(BF)
        return 0

    lax.fori_loop(0, 16, roll_one, 0, unroll=4)
    lane_block = lax.broadcasted_iota(jnp.int32, (64, 128), 1) // 32

    def dest(d, _):
        for j in range(2):
            acc = None
            for i in range(4):
                q = t_ref[i, 2 * d + j]
                tile = rolled[(i - q) & 3, q >> 2].astype(F32)
                acc = tile if acc is None else jnp.where(lane_block == i, tile, acc)
            o_ref[d, 64 * j : 64 * j + 64, :] = acc.astype(BF)
        half = d & 1
        plane = d >> 1
        o_ref[d, 128:152, :] = g_ref[plane, pl.ds(pl.multiple_of(64 + 24 * half, 8), 24), :]
        o_ref[d, 152:160, :] = g_ref[plane, pl.ds(pl.multiple_of(112 + 8 * half, 8), 8), :]
        o_ref[d, 160:168, :] = g_ref[plane, 128:136, :]
        return 0

    lax.fori_loop(0, 32, dest, 0, unroll=4)


def pick(gathered, table):
    return pl.pallas_call(
        pick_kernel,
        out_shape=jax.ShapeDtypeStruct((32, 168, 128), BF),
        in_specs=[pl.BlockSpec(memory_space=pltpu.SMEM), pl.BlockSpec(memory_space=pltpu.VMEM)],
        out_specs=pl.BlockSpec(memory_space=pltpu.VMEM),
        scratch_shapes=[pltpu.VMEM((4, 16, 64, 128), BF)],
        compiler_params=SMALL,
        name="pick",
    )(table, gathered)


NT = (((1,), (1,)), ((), ()))
TN = (((0,), (0,)), ((), ()))


def prepare_kernel(form_ref, o_ref):
    for c in range(NC):
        o_ref[0, c] = jnp.broadcast_to(form_ref[0, 8 + c : 9 + c, :].astype(F32), (16, 2048)).astype(BF)


def prepare(near):
    return pl.pallas_call(
        prepare_kernel,
        grid=(4,),
        in_specs=[pl.BlockSpec((1, 24, 2048), lambda i: (i, 0, 0))],
        out_specs=pl.BlockSpec((1, 16, 16, 2048), lambda i: (i, 0, 0, 0)),
        out_shape=jax.ShapeDtypeStruct((4, 16, 16, 2048), BF),
        compiler_params=pltpu.CompilerParams(vmem_limit_bytes=32 << 20),
        name="prepare",
    )(near)


def pair_kernel(t_ref, r_ref, near_ref, wide_hbm, coef_ref, coul_ref, map_ref, o_ref, send_ref, far, farc, nearc, cols, cond, val, scaled, acc, right, kt, wide_ref, sems):
    def wide_copy(i):
        return pltpu.make_async_copy(wide_hbm.at[i], wide_ref.at[i], sems.at[i])

    for i in range(4):
        wide_copy(i).start()
    col = device_at("kp")
    lane24 = lax.broadcasted_iota(jnp.int32, (24, 128), 1)
    for m in range(16):
        lo = r_ref[2 * m, 128:152, :].astype(F32)
        hi = r_ref[2 * m + 1, 128:152, :].astype(F32)
        at = (slice(24 * (m // 2), 24 * (m // 2) + 24), slice(128 * (m % 2), 128 * (m % 2) + 128))
        far[(0, *at)] = jnp.where(lane24 < 64, lo, pltpu.roll(hi, 64, 1)).astype(BF)
        far[(1, *at)] = jnp.where(lane24 < 64, pltpu.roll(lo, 64, 1), hi).astype(BF)
    rows = r_ref[:, 152:160, :].reshape(256, 128)
    out_row = lax.broadcasted_iota(jnp.int32, (128, 256), 0)
    in_row = lax.broadcasted_iota(jnp.int32, (128, 256), 1)
    for k in range(2):
        sel = (in_row == (out_row // 4) * 8 + k * 4 + out_row % 4).astype(F32).astype(BF)
        farc[k] = jnp.dot(sel, rows, preferred_element_type=F32).astype(BF)
        cols[k] = r_ref[:, 64 * k : 64 * k + 64, :].reshape(2048, 128).astype(F32).T.astype(BF)
    old = lax.broadcasted_iota(jnp.int32, (128, 128), 1)
    new = lax.broadcasted_iota(jnp.int32, (128, 128), 0)
    order = (old == (new % 8) * 16 + new // 8).astype(F32).astype(BF)
    for i in range(4):
        nearc[i] = lax.dot_general(coef_ref[i], order, (((0,), (1,)), ((), ())), preferred_element_type=F32).astype(BF)

    place = lax.broadcasted_iota(jnp.int32, (256, 128), 0).astype(F32).astype(BF)
    one, zero = jnp.ones((), BF), jnp.zeros((), BF)
    granule = lax.broadcasted_iota(jnp.int32, (8, 128), 1) // 16

    def finish(p):
        j = p // 4
        i = p % 4
        r_hi = right[...].astype(BF)
        r_lo = (right[...] - r_hi.astype(F32)).astype(BF)
        left = acc[64:96, :]
        l_hi = left.astype(BF)
        l_lo = (left - l_hi.astype(F32)).astype(BF)
        low = jnp.dot(r_lo, l_hi, preferred_element_type=F32) + jnp.dot(r_hi, l_lo, preferred_element_type=F32)
        direct = acc[0:64, :] + (jnp.dot(r_hi, l_hi, preferred_element_type=F32) + low)
        tiles = []
        for half in range(2):
            t = [direct[8 * v : 8 * v + 8, 128 * half : 128 * half + 128] for v in range(8)]
            for s in (1, 2, 4):
                upper = (granule & s) != 0
                n = list(t)
                for v in range(8):
                    if not v & s:
                        a, b = t[v], t[v | s]
                        n[v] = jnp.where(upper, pltpu.roll(b, 16 * s, 1), a)
                        n[v | s] = jnp.where(upper, b, pltpu.roll(a, 128 - 16 * s, 1))
                t = n
            tiles += t
        block = jnp.concatenate(tiles, axis=0).astype(BF)
        half = jnp.dot(block, farc[j], preferred_element_type=F32).astype(BF)
        out = jnp.dot(nearc[i], half, preferred_element_type=F32)
        at_i = pl.ds(pl.multiple_of(i * 128, 128), 128)
        at_j = pl.ds(pl.multiple_of(j * 128, 128), 128)
        o_ref[at_i, at_j] = out.astype(BF)
        kt[at_j, at_i] = out.T.astype(BF)

    def pair(p, _):
        @pl.when(p < 4)
        def _():
            wide_copy(p).wait()

        finish(jnp.maximum(p - 1, 0))
        j = p // 4
        i = p % 4
        index = map_ref[t_ref[i, 2 * col + j]]
        scaled[64:96, :] = cols[j, pl.ds(pl.multiple_of(32 * i, 32), 32), :]
        for m in range(16):
            cs = slice(128 * m, 128 * m + 128)
            if m % 2 == 0:
                pick_low = [
                    jnp.where(place == (index[n : n + 1, :] & 255).astype(F32).astype(BF), one, zero) for n in (m, m + 1)
                ]
                both = jnp.dot(far[j], jnp.concatenate(pick_low, axis=1), preferred_element_type=F32)
            high = jnp.broadcast_to(index[m : m + 1, :] >> 8, (24, 128))
            ls = slice(128 * (m % 2), 128 * (m % 2) + 128)
            got = both[0:24, ls]
            for s in range(1, 8):
                got = jnp.where(high == s, both[24 * s : 24 * s + 24, ls], got)
            a = near_ref[i, :, cs].astype(F32)
            m_c = got[8:24, :].astype(BF)
            for c in range(NC):
                cond[16 * c : 16 * c + 16, cs] = wide_ref[i, c, :, cs] * m_c
            a_v = a[0:8, :]
            coul = coul_ref[m : m + 1, :]
            for v in range(0, NV, 2):
                x = jnp.concatenate([a_v * got[v : v + 1, :], a_v * got[v + 1 : v + 2, :]], axis=0).astype(BF)
                val[8 * v : 8 * v + 16, cs] = x
                scaled[8 * v : 8 * v + 16, cs] = (coul * x.astype(F32)).astype(BF)
            if m % 2:
                ks = slice(128 * m - 128, 128 * m + 128)
                part = lax.dot_general(scaled[:, ks], cond[:, ks], NT, preferred_element_type=F32)
                total = part if m == 1 else total + part
        acc[...] = total
        right[...] = lax.dot_general(val[...], scaled[64:96, :], NT, preferred_element_type=F32)
        return 0

    lax.fori_loop(0, 8, pair, 0)
    finish(7)

    odd = (col & 1) == 1
    both = r_ref[:, 160:168, :].reshape(256, 128).astype(F32)
    lane = lax.broadcasted_iota(jnp.int32, (256, 128), 1)
    other = pltpu.roll(both, 64, 1)
    first = jnp.where(lane < 64, jnp.where(odd, other, both), 0.0).astype(BF)
    second = jnp.where(lane < 64, 0.0, jnp.where(odd, both, other)).astype(BF)
    y = jnp.dot(o_ref[0:256, :], first, preferred_element_type=F32)
    y = y + jnp.dot(o_ref[256:512, :], second, preferred_element_type=F32)
    y_hi = y.astype(BF)
    send_ref[:, 0:8, :] = y_hi.reshape(32, 8, 128)
    send_ref[:, 8:16, :] = (y - y_hi.astype(F32)).astype(BF).reshape(32, 8, 128)
    for b in range(4):
        send_ref[:, 16 + 8 * b : 24 + 8 * b, :] = kt[:, 128 * b : 128 * b + 128].reshape(32, 8, 128)


def pair_blocks(table, received, near, wide, coef, coulomb, shift_map):
    return pl.pallas_call(
        pair_kernel,
        in_specs=[SM, VM, VM, pl.BlockSpec(memory_space=pl.ANY), VM, VM, VM],
        out_specs=(VM, VM),
        out_shape=(jax.ShapeDtypeStruct((512, 256), BF), jax.ShapeDtypeStruct((32, 48, 128), BF)),
        scratch_shapes=[
            pltpu.VMEM((2, 192, 256), BF),
            pltpu.VMEM((2, 128, 128), BF),
            pltpu.VMEM((4, 128, 128), BF),
            pltpu.VMEM((2, 128, 2048), BF),
            pltpu.VMEM((256, 2048), BF),
            pltpu.VMEM((64, 2048), BF),
            pltpu.VMEM((96, 2048), BF),
            pltpu.VMEM((96, 256), F32),
            pltpu.VMEM((64, 32), F32),
            pltpu.VMEM((256, 512), BF),
            pltpu.VMEM((4, 16, 16, 2048), BF),
            pltpu.SemaphoreType.DMA((4,)),
        ],
        compiler_params=pltpu.CompilerParams(vmem_limit_bytes=32 << 20),
        name="pairs",
    )(table, received, near, wide, coef, coulomb, shift_map)


def fold_rows(square):
    lane = lax.broadcasted_iota(jnp.int32, (32, 128), 1)
    return jnp.where(lane < 64, square[0:32], pltpu.roll(square[32:64], 64, 1))


def second_kernel(r_ref, x_ref, o_ref):
    lane = lax.broadcasted_iota(jnp.int32, (8, 128), 1)
    parts = []
    for m in range(16):
        x = x_ref[m]
        high = x.astype(BF).astype(F32)
        low = x - high
        parts.append(jnp.where(lane < 64, high, pltpu.roll(low, 64, 1)))
        parts.append(jnp.where(lane < 64, pltpu.roll(high, 64, 1), low))
    x = jnp.concatenate(parts, axis=0)
    xt = x.T.astype(BF)
    sums = []
    for b in range(4):
        g = jnp.dot(xt, r_ref[:, 16 + 8 * b : 24 + 8 * b, :].reshape(256, 128), preferred_element_type=F32)
        sums.append(g[0:64] + g[64:128])
    for b in range(2):
        y = jnp.concatenate([sums[b], sums[b + 2]], axis=0).T
        o_ref[16 * b : 16 * b + 16, 0:8, :] = y.reshape(16, 8, 128)
    corr = jnp.dot(xt, x.astype(BF), preferred_element_type=F32)
    corr = corr + pltpu.roll(corr, 64, 1)
    corr = fold_rows(corr[0:64] + corr[64:128])
    o_ref[:, 8:9, :] = corr.reshape(32, 1, 128)


def second_product(received, x):
    return pl.pallas_call(
        second_kernel,
        out_shape=jax.ShapeDtypeStruct((32, 9, 128), F32),
        in_specs=[VM, VM],
        out_specs=VM,
        compiler_params=SMALL,
        name="second",
    )(received, x)


def pack_symmetric(square):
    lane = lax.broadcasted_iota(jnp.int32, (32, 128), 1)
    row = lax.broadcasted_iota(jnp.int32, (32, 128), 0)
    corner = pltpu.roll(square[32:64], 96, 1)
    values = jnp.where(lane < row, corner, square[0:32])
    diagonal = jnp.sum(jnp.where(lane == row, corner, 0.0), axis=0, keepdims=True)
    values = jnp.where(lane[0:16] < 64, values[0:16], pltpu.roll(values[16:32], 64, 1))
    high = values.astype(BF).astype(F32)
    tail = jnp.broadcast_to(diagonal, (8, 128))
    tail_high = tail.astype(BF).astype(F32)
    tail = jnp.where(row[0:8] == 0, tail_high, jnp.where(row[0:8] == 1, tail - tail_high, 0.0))
    return jnp.concatenate([high, values - high, tail], axis=0).astype(BF)


def unpack_symmetric(parts):
    lane = lax.broadcasted_iota(jnp.int32, (32, 128), 1)
    row = lax.broadcasted_iota(jnp.int32, (32, 128), 0)
    values = parts[0:16] + parts[16:32]
    values = jnp.concatenate([values, pltpu.roll(values, 64, 1)], axis=0)
    diagonal = jnp.broadcast_to(pltpu.roll(parts[32:40], 32, 1)[0:1] + pltpu.roll(parts[32:40], 32, 1)[1:2], (32, 128))
    top = jnp.where(lane < row, 0.0, jnp.where(lane == row, 0.5 * values, values))
    top = jnp.where(lane < 64, top, 0.0)
    low = pltpu.roll(values, 32, 1)
    low = jnp.where(lane - 32 < row, low, jnp.where(lane - 32 == row, 0.5 * diagonal, 0.0))
    low = jnp.where(lane < 32, 0.0, low)
    half = jnp.concatenate([top, low, jnp.zeros((64, 128), F32)], axis=0)
    return half[0:64] + half.T[0:64]


def unfold_rows(packed):
    return jnp.concatenate([packed, pltpu.roll(packed, 64, 1)], axis=0)


def inverse_factor(full, scale):
    lane = lax.broadcasted_iota(jnp.int32, (64, 128), 1)
    row = lax.broadcasted_iota(jnp.int32, (64, 128), 0)
    work = jnp.where(lane < 64, full * scale, (lane - 64 == row).astype(F32))
    done = []
    tiles = [work[8 * t : 8 * t + 8] for t in range(8)]
    for t in range(8):
        column = {u: [jnp.broadcast_to(tiles[u][:, 8 * t + k : 8 * t + k + 1], (8, 128)) for k in range(8)] for u in range(t, 8)}
        for k in range(8):
            pivot = column[t][k][k : k + 1, :]
            y = lax.rsqrt(pivot)
            square = y * y
            near_one = pivot * square
            inverse = square * (2.0 - near_one)
            line = tiles[t][k : k + 1, :]
            done.append(line * (y * (1.5 - 0.5 * near_one)))
            line = line * inverse
            ahead = {m: column[t][m][k : k + 1, :] * inverse for m in range(k + 1, 8)}
            for u in range(t, 8):
                factor = column[u][k]
                for m in range(k + 1, 8):
                    column[u][m] = column[u][m] - factor * ahead[m]
                tiles[u] = tiles[u] - factor * line
    return jnp.concatenate(done, axis=0)


def lane_halves(inv):
    lane = lax.broadcasted_iota(jnp.int32, (64, 128), 1)
    return jnp.where(lane < 64, pltpu.roll(inv, 64, 1), 0.0), jnp.where(lane < 64, 0.0, inv)


def apply_inverse(x, inv):
    both = jnp.concatenate(lane_halves(inv), axis=0)
    return lax.dot_general(x, both, NT, precision=HIGH, preferred_element_type=F32)


def middle_kernel(g_ref, image_ref, corr_ref, *, scale):
    packed = g_ref[:, 8:9, :].reshape(32, 128)
    inv = inverse_factor(unfold_rows(packed), scale)
    image = apply_inverse(g_ref[:, 0:8, :].reshape(256, 128), inv)
    image_ref[...] = image
    corr = lax.dot_general(image, image, TN, precision=HIGH, preferred_element_type=F32)
    corr = corr[0:64] + pltpu.roll(corr[64:128], 64, 1)
    corr = pack_symmetric(corr)
    for m in range(16):
        corr_ref[m] = corr


def middle(g, scale):
    return pl.pallas_call(
        lambda *refs: middle_kernel(*refs, scale=scale),
        out_shape=(jax.ShapeDtypeStruct((256, 128), F32), jax.ShapeDtypeStruct((16, 40, 128), BF)),
        in_specs=[VM],
        out_specs=(VM, VM),
        compiler_params=SMALL,
        name="middle",
    )(g)


def last_kernel(image_ref, corr_ref, o_ref, *, scale):
    parts = corr_ref[0].astype(F32)
    for m in range(1, 16):
        parts = parts + corr_ref[m].astype(F32)
    inv = inverse_factor(unpack_symmetric(parts), scale)
    upper, lower = lane_halves(inv)
    image = image_ref[...]
    o_ref[:, 0:256] = lax.dot_general(upper, image, NT, precision=HIGH, preferred_element_type=F32)
    o_ref[:, 256:512] = lax.dot_general(lower, image, NT, precision=HIGH, preferred_element_type=F32)


def last(image, corr, scale):
    return pl.pallas_call(
        lambda *refs: last_kernel(*refs, scale=scale),
        out_shape=jax.ShapeDtypeStruct((64, 512), F32),
        in_specs=[VM, VM],
        out_specs=VM,
        compiler_params=SMALL,
        name="last",
    )(image, corr).T


def to_all(x, axis):
    size = lax.axis_size(axis)
    return lax.all_to_all(jnp.broadcast_to(x[None], (size, *x.shape)), axis, 0, 0, tiled=True)


def on_device(band_form, interp_coef, screen, coulomb, shift_map, grid_order, energies, initial):
    piece, starts, diagonal, table = share(band_form, interp_coef, screen, initial, energies, grid_order)
    gathered = lax.all_gather(piece, "ka", axis=0, tiled=False)
    received = lax.all_to_all(pick(vmem(gathered), table), "kp", 0, 0, tiled=True)
    wide = pltpu.with_memory_space_constraint(prepare(band_form), pltpu.HBM)
    kernel, sent = pair_blocks(
        table, vmem(received), band_form, wide, interp_coef, coulomb.reshape(16, 128), vmem(shift_map.reshape(64, 16, 128))
    )
    sent = lax.all_to_all(sent, "kp", 0, 0, tiled=True)
    image = jnp.sum(sent[:, 0:16, :].astype(F32).reshape(64, 8, 128), axis=0) + diagonal * starts

    sums = jnp.sum(lax.all_to_all(second_product(vmem(sent), vmem(to_all(image, "ka"))), "kp", 0, 0, tiled=True), axis=0)
    sums = sums + jnp.concatenate([diagonal * image, jnp.zeros((1, 128), F32)], axis=0)
    everyone = to_all(sums, "kp")
    scale = 1.0 / 8192
    image, corr = middle(vmem(everyone), scale)
    vectors = last(image, vmem(lax.all_to_all(corr, "ka", 0, 0, tiled=True)), scale)
    return (kernel, vectors)


def solution(mesh):
    return jax.shard_map(
        on_device,
        mesh=mesh,
        in_specs=(
            P("ka", None, None),
            P("ka", None, None),
            P("ka", "kp", None),
            P(),
            P(),
            P(),
            P("ka"),
            P("ka", None),
        ),
        out_specs=(P("ka", "kp"), P("ka", None)),
        check_vma=False,
    )
```

```python
import jax
import jax.numpy as jnp
from jax import lax
from jax.experimental import pallas as pl
from jax.experimental.pallas import tpu as pltpu
from jax.sharding import PartitionSpec as P

NV, NC = 8, 16
GRID_Y = 8
GRID_X = 8
BF, F32 = jnp.bfloat16, jnp.float32
HIGH = lax.Precision.HIGHEST
VM = pl.BlockSpec(memory_space=pltpu.VMEM)
SM = pl.BlockSpec(memory_space=pltpu.SMEM)
SMALL = pltpu.CompilerParams(vmem_limit_bytes=16 << 20)


def device_at(axis):
    return lax.axis_index(axis)


def vmem(x):
    return pltpu.with_memory_space_constraint(x, pltpu.VMEM)


def share_kernel(form_hbm, coef_hbm, screen_hbm, start_hbm, energy_hbm, cells_hbm, piece_ref, first_ref, diagonal_ref, table_ref, form, coef, screen_ref, start_ref, energy_ref, cells_ref, sems):
    plane, col = device_at("ka"), device_at("kp")
    odd = (col & 1) == 1
    moves = (
        (cells_hbm, cells_ref),
        (screen_hbm, screen_ref),
        (start_hbm, start_ref),
        (energy_hbm, energy_ref),
        (form_hbm.at[:, :, pl.ds(pl.multiple_of(128 * (col // 2), 128), 128)], form),
        (coef_hbm.at[:, pl.ds(pl.multiple_of(8 * (col // 2), 8), 8), :], coef),
    )
    copies = [pltpu.make_async_copy(src, dst, sems.at[n]) for n, (src, dst) in enumerate(moves)]
    for copy in copies:
        copy.start()
    for copy in copies:
        copy.wait()
    x, y = cells_ref[...] >> 3, cells_ref[...] & 7
    for i in range(4):
        own = lax.broadcasted_iota(jnp.int32, (1, 64), 1) == 4 * plane + i
        cell = jnp.sum(jnp.where(own, cells_ref[...], 0).astype(F32), axis=1, keepdims=True).astype(jnp.int32)
        table_ref[i : i + 1, :] = (((cell >> 3) - x) & 7) * 8 + (((cell & 7) - y) & 7)
    piece_ref[0:64, :] = jnp.concatenate([screen_ref[q].astype(F32) for q in range(4)], axis=0).T.astype(BF)
    block = col // 16
    back = (128 - 8 * (col % 16)) % 128

    def rows_of(parts):
        both = jnp.concatenate([pltpu.roll(part, back, 1) for part in parts], axis=0)
        return both.T[0:8]

    first = rows_of([start_ref[:, pl.ds(pl.multiple_of(256 * h + 128 * block, 128), 128)] for h in range(2)])
    first_ref[...] = first
    diagonal_ref[...] = rows_of([jnp.broadcast_to(energy_ref[pl.ds(2 * h + block, 1), :], (64, 128)) for h in range(2)])
    piece_ref[128:136, :] = first.astype(BF)
    lane = lax.broadcasted_iota(jnp.int32, (24, 128), 1)
    row = lax.broadcasted_iota(jnp.int32, (8, 128), 0)
    for h in range(2):
        a, b = form[2 * h].astype(F32), form[2 * h + 1].astype(F32)
        low = jnp.where(odd, pltpu.roll(a, 64, 1), a)
        high = jnp.where(odd, b, pltpu.roll(b, 64, 1))
        piece_ref[64 + 24 * h : 88 + 24 * h, :] = jnp.where(lane < 64, low, high).astype(BF)
        a, b = coef[2 * h].astype(F32), coef[2 * h + 1].astype(F32)
        low = jnp.where(odd, pltpu.roll(a, 4, 0), a)
        high = jnp.where(odd, b, pltpu.roll(b, 4, 0))
        piece_ref[112 + 8 * h : 120 + 8 * h, :] = jnp.where(row < 4, low, high).astype(BF)


def share(forms, coefs, screen, initial, energies, cells):
    hbm = pl.BlockSpec(memory_space=pltpu.HBM)
    return pl.pallas_call(
        share_kernel,
        in_specs=[hbm] * 6,
        out_specs=(VM, VM, VM, VM),
        out_shape=(
            jax.ShapeDtypeStruct((136, 128), BF),
            jax.ShapeDtypeStruct((8, 128), F32),
            jax.ShapeDtypeStruct((8, 128), F32),
            jax.ShapeDtypeStruct((4, 64), jnp.int32),
        ),
        scratch_shapes=[
            pltpu.VMEM((4, 24, 128), BF),
            pltpu.VMEM((4, 8, 128), BF),
            pltpu.VMEM((4, 32, 64), BF),
            pltpu.VMEM((64, 512), F32),
            pltpu.VMEM((4, 128), F32),
            pltpu.VMEM((1, 64), jnp.int32),
            pltpu.SemaphoreType.DMA((6,)),
        ],
        compiler_params=SMALL,
        name="share",
    )(*(pltpu.with_memory_space_constraint(x, pltpu.HBM) for x in (forms, coefs, screen.transpose(0, 2, 1), initial.T, energies.reshape(4, 128), cells.reshape(1, 64))))


def slot_of(plane):
    return (plane & 3) * 4 + (plane >> 2)


def pick_kernel(t_ref, g_ref, o_ref, rolled):
    def roll_one(h, _):
        x = g_ref[slot_of(h), 0:64, :].astype(F32)
        rolled[0, h] = x.astype(BF)
        for s in range(1, 4):
            rolled[s, h] = pltpu.roll(x, 32 * s, 1).astype(BF)
        return 0

    lax.fori_loop(0, 16, roll_one, 0, unroll=4)
    lane_block = lax.broadcasted_iota(jnp.int32, (64, 128), 1) // 32

    def dest(d, _):
        for j in range(2):
            acc = None
            for i in range(4):
                q = t_ref[i, 2 * d + j]
                tile = rolled[(i - q) & 3, q >> 2].astype(F32)
                acc = tile if acc is None else jnp.where(lane_block == i, tile, acc)
            o_ref[d, 64 * j : 64 * j + 64, :] = acc.astype(BF)
        half = d & 1
        plane = slot_of(d >> 1)
        o_ref[d, 128:152, :] = g_ref[plane, pl.ds(pl.multiple_of(64 + 24 * half, 8), 24), :]
        o_ref[d, 152:160, :] = g_ref[plane, pl.ds(pl.multiple_of(112 + 8 * half, 8), 8), :]
        o_ref[d, 160:168, :] = g_ref[plane, 128:136, :]
        return 0

    lax.fori_loop(0, 32, dest, 0, unroll=4)


def pick(gathered, table):
    return pl.pallas_call(
        pick_kernel,
        out_shape=jax.ShapeDtypeStruct((32, 168, 128), BF),
        in_specs=[pl.BlockSpec(memory_space=pltpu.SMEM), pl.BlockSpec(memory_space=pltpu.VMEM)],
        out_specs=pl.BlockSpec(memory_space=pltpu.VMEM),
        scratch_shapes=[pltpu.VMEM((4, 16, 64, 128), BF)],
        compiler_params=SMALL,
        name="pick",
    )(table, gathered)


NT = (((1,), (1,)), ((), ()))
TN = (((0,), (0,)), ((), ()))


def prepare_kernel(form_ref, o_ref):
    for c in range(NC):
        o_ref[0, c] = jnp.broadcast_to(form_ref[0, 8 + c : 9 + c, :].astype(F32), (16, 2048)).astype(BF)


def prepare(near):
    return pl.pallas_call(
        prepare_kernel,
        grid=(4,),
        in_specs=[pl.BlockSpec((1, 24, 2048), lambda i: (i, 0, 0))],
        out_specs=pl.BlockSpec((1, 16, 16, 2048), lambda i: (i, 0, 0, 0)),
        out_shape=jax.ShapeDtypeStruct((4, 16, 16, 2048), BF),
        compiler_params=pltpu.CompilerParams(vmem_limit_bytes=32 << 20),
        name="prepare",
    )(near)


def pair_kernel(t_ref, r_ref, near_ref, wide_hbm, coef_ref, coul_ref, map_ref, o_ref, send_ref, far, farc, nearc, cols, cond, val, scaled, acc, right, kt, wide_ref, sems):
    def wide_copy(i):
        return pltpu.make_async_copy(wide_hbm.at[i], wide_ref.at[i], sems.at[i])

    for i in range(4):
        wide_copy(i).start()
    col = device_at("kp")
    lane24 = lax.broadcasted_iota(jnp.int32, (24, 128), 1)
    for m in range(16):
        lo = r_ref[2 * m, 128:152, :].astype(F32)
        hi = r_ref[2 * m + 1, 128:152, :].astype(F32)
        at = (slice(24 * (m // 2), 24 * (m // 2) + 24), slice(128 * (m % 2), 128 * (m % 2) + 128))
        far[(0, *at)] = jnp.where(lane24 < 64, lo, pltpu.roll(hi, 64, 1)).astype(BF)
        far[(1, *at)] = jnp.where(lane24 < 64, pltpu.roll(lo, 64, 1), hi).astype(BF)
    rows = r_ref[:, 152:160, :].reshape(256, 128)
    out_row = lax.broadcasted_iota(jnp.int32, (128, 256), 0)
    in_row = lax.broadcasted_iota(jnp.int32, (128, 256), 1)
    for k in range(2):
        sel = (in_row == (out_row // 4) * 8 + k * 4 + out_row % 4).astype(F32).astype(BF)
        farc[k] = jnp.dot(sel, rows, preferred_element_type=F32).astype(BF)
        cols[k] = r_ref[:, 64 * k : 64 * k + 64, :].reshape(2048, 128).astype(F32).T.astype(BF)
    old = lax.broadcasted_iota(jnp.int32, (128, 128), 1)
    new = lax.broadcasted_iota(jnp.int32, (128, 128), 0)
    order = (old == (new % 8) * 16 + new // 8).astype(F32).astype(BF)
    for i in range(4):
        nearc[i] = lax.dot_general(coef_ref[i], order, (((0,), (1,)), ((), ())), preferred_element_type=F32).astype(BF)

    place = lax.broadcasted_iota(jnp.int32, (256, 128), 0).astype(F32).astype(BF)
    one, zero = jnp.ones((), BF), jnp.zeros((), BF)
    granule = lax.broadcasted_iota(jnp.int32, (8, 128), 1) // 16

    def finish(p):
        j = p // 4
        i = p % 4
        r_hi = right[...].astype(BF)
        r_lo = (right[...] - r_hi.astype(F32)).astype(BF)
        left = acc[64:96, :]
        l_hi = left.astype(BF)
        l_lo = (left - l_hi.astype(F32)).astype(BF)
        low = jnp.dot(r_lo, l_hi, preferred_element_type=F32) + jnp.dot(r_hi, l_lo, preferred_element_type=F32)
        direct = acc[0:64, :] + (jnp.dot(r_hi, l_hi, preferred_element_type=F32) + low)
        tiles = []
        for half in range(2):
            t = [direct[8 * v : 8 * v + 8, 128 * half : 128 * half + 128] for v in range(8)]
            for s in (1, 2, 4):
                upper = (granule & s) != 0
                n = list(t)
                for v in range(8):
                    if not v & s:
                        a, b = t[v], t[v | s]
                        n[v] = jnp.where(upper, pltpu.roll(b, 16 * s, 1), a)
                        n[v | s] = jnp.where(upper, b, pltpu.roll(a, 128 - 16 * s, 1))
                t = n
            tiles += t
        block = jnp.concatenate(tiles, axis=0).astype(BF)
        half = jnp.dot(block, farc[j], preferred_element_type=F32).astype(BF)
        out = jnp.dot(nearc[i], half, preferred_element_type=F32)
        at_i = pl.ds(pl.multiple_of(i * 128, 128), 128)
        at_j = pl.ds(pl.multiple_of(j * 128, 128), 128)
        o_ref[at_i, at_j] = out.astype(BF)
        kt[at_j, at_i] = out.T.astype(BF)

    def pair(p, _):
        @pl.when(p < 4)
        def _():
            wide_copy(p).wait()

        finish(jnp.maximum(p - 1, 0))
        j = p // 4
        i = p % 4
        index = map_ref[t_ref[i, 2 * col + j]]
        scaled[64:96, :] = cols[j, pl.ds(pl.multiple_of(32 * i, 32), 32), :]
        for m in range(16):
            cs = slice(128 * m, 128 * m + 128)
            if m % 2 == 0:
                pick_low = [
                    jnp.where(place == (index[n : n + 1, :] & 255).astype(F32).astype(BF), one, zero) for n in (m, m + 1)
                ]
                both = jnp.dot(far[j], jnp.concatenate(pick_low, axis=1), preferred_element_type=F32)
            high = jnp.broadcast_to(index[m : m + 1, :] >> 8, (24, 128))
            ls = slice(128 * (m % 2), 128 * (m % 2) + 128)
            got = both[0:24, ls]
            for s in range(1, 8):
                got = jnp.where(high == s, both[24 * s : 24 * s + 24, ls], got)
            a = near_ref[i, :, cs].astype(F32)
            m_c = got[8:24, :].astype(BF)
            for c in range(NC):
                cond[16 * c : 16 * c + 16, cs] = wide_ref[i, c, :, cs] * m_c
            a_v = a[0:8, :]
            coul = coul_ref[m : m + 1, :]
            for v in range(0, NV, 2):
                x = jnp.concatenate([a_v * got[v : v + 1, :], a_v * got[v + 1 : v + 2, :]], axis=0).astype(BF)
                val[8 * v : 8 * v + 16, cs] = x
                scaled[8 * v : 8 * v + 16, cs] = (coul * x.astype(F32)).astype(BF)
            if m % 2:
                ks = slice(128 * m - 128, 128 * m + 128)
                part = lax.dot_general(scaled[:, ks], cond[:, ks], NT, preferred_element_type=F32)
                total = part if m == 1 else total + part
        acc[...] = total
        right[...] = lax.dot_general(val[...], scaled[64:96, :], NT, preferred_element_type=F32)
        return 0

    lax.fori_loop(0, 8, pair, 0)
    finish(7)

    odd = (col & 1) == 1
    both = r_ref[:, 160:168, :].reshape(256, 128).astype(F32)
    lane = lax.broadcasted_iota(jnp.int32, (256, 128), 1)
    other = pltpu.roll(both, 64, 1)
    first = jnp.where(lane < 64, jnp.where(odd, other, both), 0.0).astype(BF)
    second = jnp.where(lane < 64, 0.0, jnp.where(odd, both, other)).astype(BF)
    y = jnp.dot(o_ref[0:256, :], first, preferred_element_type=F32)
    y = y + jnp.dot(o_ref[256:512, :], second, preferred_element_type=F32)
    y_hi = y.astype(BF)
    send_ref[:, 0:8, :] = y_hi.reshape(32, 8, 128)
    send_ref[:, 8:16, :] = (y - y_hi.astype(F32)).astype(BF).reshape(32, 8, 128)
    for b in range(4):
        send_ref[:, 16 + 8 * b : 24 + 8 * b, :] = kt[:, 128 * b : 128 * b + 128].reshape(32, 8, 128)


def pair_blocks(table, received, near, wide, coef, coulomb, shift_map):
    return pl.pallas_call(
        pair_kernel,
        in_specs=[SM, VM, VM, pl.BlockSpec(memory_space=pl.ANY), VM, VM, VM],
        out_specs=(VM, VM),
        out_shape=(jax.ShapeDtypeStruct((512, 256), BF), jax.ShapeDtypeStruct((32, 48, 128), BF)),
        scratch_shapes=[
            pltpu.VMEM((2, 192, 256), BF),
            pltpu.VMEM((2, 128, 128), BF),
            pltpu.VMEM((4, 128, 128), BF),
            pltpu.VMEM((2, 128, 2048), BF),
            pltpu.VMEM((256, 2048), BF),
            pltpu.VMEM((64, 2048), BF),
            pltpu.VMEM((96, 2048), BF),
            pltpu.VMEM((96, 256), F32),
            pltpu.VMEM((64, 32), F32),
            pltpu.VMEM((256, 512), BF),
            pltpu.VMEM((4, 16, 16, 2048), BF),
            pltpu.SemaphoreType.DMA((4,)),
        ],
        compiler_params=pltpu.CompilerParams(vmem_limit_bytes=32 << 20),
        name="pairs",
    )(table, received, near, wide, coef, coulomb, shift_map)


def fold_rows(square):
    lane = lax.broadcasted_iota(jnp.int32, (32, 128), 1)
    return jnp.where(lane < 64, square[0:32], pltpu.roll(square[32:64], 64, 1))


def second_kernel(r_ref, x_ref, o_ref):
    lane = lax.broadcasted_iota(jnp.int32, (8, 128), 1)
    parts = []
    for m in range(16):
        x = x_ref[m]
        high = x.astype(BF).astype(F32)
        low = x - high
        parts.append(jnp.where(lane < 64, high, pltpu.roll(low, 64, 1)))
        parts.append(jnp.where(lane < 64, pltpu.roll(high, 64, 1), low))
    x = jnp.concatenate(parts, axis=0)
    xt = x.T.astype(BF)
    sums = []
    for b in range(4):
        g = jnp.dot(xt, r_ref[:, 16 + 8 * b : 24 + 8 * b, :].reshape(256, 128), preferred_element_type=F32)
        sums.append(g[0:64] + g[64:128])
    for b in range(2):
        y = jnp.concatenate([sums[b], sums[b + 2]], axis=0).T
        o_ref[16 * b : 16 * b + 16, 0:8, :] = y.reshape(16, 8, 128)
    corr = jnp.dot(xt, x.astype(BF), preferred_element_type=F32)
    corr = corr + pltpu.roll(corr, 64, 1)
    corr = fold_rows(corr[0:64] + corr[64:128])
    o_ref[:, 8:9, :] = corr.reshape(32, 1, 128)


def second_product(received, x):
    return pl.pallas_call(
        second_kernel,
        out_shape=jax.ShapeDtypeStruct((32, 9, 128), F32),
        in_specs=[VM, VM],
        out_specs=VM,
        compiler_params=SMALL,
        name="second",
    )(received, x)


def pack_symmetric(square):
    lane = lax.broadcasted_iota(jnp.int32, (32, 128), 1)
    row = lax.broadcasted_iota(jnp.int32, (32, 128), 0)
    corner = pltpu.roll(square[32:64], 96, 1)
    values = jnp.where(lane < row, corner, square[0:32])
    diagonal = jnp.sum(jnp.where(lane == row, corner, 0.0), axis=0, keepdims=True)
    values = jnp.where(lane[0:16] < 64, values[0:16], pltpu.roll(values[16:32], 64, 1))
    high = values.astype(BF).astype(F32)
    tail = jnp.broadcast_to(diagonal, (8, 128))
    tail_high = tail.astype(BF).astype(F32)
    tail = jnp.where(row[0:8] == 0, tail_high, jnp.where(row[0:8] == 1, tail - tail_high, 0.0))
    return jnp.concatenate([high, values - high, tail], axis=0).astype(BF)


def unpack_symmetric(parts):
    lane = lax.broadcasted_iota(jnp.int32, (32, 128), 1)
    row = lax.broadcasted_iota(jnp.int32, (32, 128), 0)
    values = parts[0:16] + parts[16:32]
    values = jnp.concatenate([values, pltpu.roll(values, 64, 1)], axis=0)
    diagonal = jnp.broadcast_to(pltpu.roll(parts[32:40], 32, 1)[0:1] + pltpu.roll(parts[32:40], 32, 1)[1:2], (32, 128))
    top = jnp.where(lane < row, 0.0, jnp.where(lane == row, 0.5 * values, values))
    top = jnp.where(lane < 64, top, 0.0)
    low = pltpu.roll(values, 32, 1)
    low = jnp.where(lane - 32 < row, low, jnp.where(lane - 32 == row, 0.5 * diagonal, 0.0))
    low = jnp.where(lane < 32, 0.0, low)
    half = jnp.concatenate([top, low, jnp.zeros((64, 128), F32)], axis=0)
    return half[0:64] + half.T[0:64]


def unfold_rows(packed):
    return jnp.concatenate([packed, pltpu.roll(packed, 64, 1)], axis=0)


def inverse_factor(full, scale):
    lane = lax.broadcasted_iota(jnp.int32, (64, 128), 1)
    row = lax.broadcasted_iota(jnp.int32, (64, 128), 0)
    work = jnp.where(lane < 64, full * scale, (lane - 64 == row).astype(F32))
    done = []
    tiles = [work[8 * t : 8 * t + 8] for t in range(8)]
    for t in range(8):
        column = {u: [jnp.broadcast_to(tiles[u][:, 8 * t + k : 8 * t + k + 1], (8, 128)) for k in range(8)] for u in range(t, 8)}
        for k in range(8):
            pivot = column[t][k][k : k + 1, :]
            y = lax.rsqrt(pivot)
            square = y * y
            near_one = pivot * square
            inverse = square * (2.0 - near_one)
            line = tiles[t][k : k + 1, :]
            done.append(line * (y * (1.5 - 0.5 * near_one)))
            line = line * inverse
            ahead = {m: column[t][m][k : k + 1, :] * inverse for m in range(k + 1, 8)}
            for u in range(t, 8):
                factor = column[u][k]
                for m in range(k + 1, 8):
                    column[u][m] = column[u][m] - factor * ahead[m]
                tiles[u] = tiles[u] - factor * line
    return jnp.concatenate(done, axis=0)


def lane_halves(inv):
    lane = lax.broadcasted_iota(jnp.int32, (64, 128), 1)
    return jnp.where(lane < 64, pltpu.roll(inv, 64, 1), 0.0), jnp.where(lane < 64, 0.0, inv)


def apply_inverse(x, inv):
    both = jnp.concatenate(lane_halves(inv), axis=0)
    return lax.dot_general(x, both, NT, precision=HIGH, preferred_element_type=F32)


def middle_kernel(g_ref, image_ref, corr_ref, *, scale):
    packed = g_ref[:, 8:9, :].reshape(32, 128)
    inv = inverse_factor(unfold_rows(packed), scale)
    image = apply_inverse(g_ref[:, 0:8, :].reshape(256, 128), inv)
    image_ref[...] = image
    corr = lax.dot_general(image, image, TN, precision=HIGH, preferred_element_type=F32)
    corr = corr[0:64] + pltpu.roll(corr[64:128], 64, 1)
    corr = pack_symmetric(corr)
    for m in range(16):
        corr_ref[m] = corr


def middle(g, scale):
    return pl.pallas_call(
        lambda *refs: middle_kernel(*refs, scale=scale),
        out_shape=(jax.ShapeDtypeStruct((256, 128), F32), jax.ShapeDtypeStruct((16, 40, 128), BF)),
        in_specs=[VM],
        out_specs=(VM, VM),
        compiler_params=SMALL,
        name="middle",
    )(g)


def last_kernel(image_ref, corr_ref, o_ref, *, scale):
    parts = corr_ref[0].astype(F32)
    for m in range(1, 16):
        parts = parts + corr_ref[m].astype(F32)
    inv = inverse_factor(unpack_symmetric(parts), scale)
    upper, lower = lane_halves(inv)
    image = image_ref[...]
    o_ref[:, 0:256] = lax.dot_general(upper, image, NT, precision=HIGH, preferred_element_type=F32)
    o_ref[:, 256:512] = lax.dot_general(lower, image, NT, precision=HIGH, preferred_element_type=F32)


def last(image, corr, scale):
    return pl.pallas_call(
        lambda *refs: last_kernel(*refs, scale=scale),
        out_shape=jax.ShapeDtypeStruct((64, 512), F32),
        in_specs=[VM, VM],
        out_specs=VM,
        compiler_params=SMALL,
        name="last",
    )(image, corr).T


def to_all(x, axis):
    size = lax.axis_size(axis)
    return lax.all_to_all(jnp.broadcast_to(x[None], (size, *x.shape)), axis, 0, 0, tiled=True)


def gather_planes(x):
    for groups in ([[i + 4 * j for j in range(4)] for i in range(4)], [[4 * i + j for j in range(4)] for i in range(4)]):
        x = jnp.broadcast_to(x[None], (4, *x.shape)).reshape(-1, 136, 128)
        x = lax.all_to_all(x, "ka", 0, 0, tiled=True, axis_index_groups=groups)
    return x


def on_device(band_form, interp_coef, screen, coulomb, shift_map, grid_order, energies, initial):
    piece, starts, diagonal, table = share(band_form, interp_coef, screen, initial, energies, grid_order)
    gathered = gather_planes(piece)
    received = lax.all_to_all(pick(vmem(gathered), table), "kp", 0, 0, tiled=True)
    wide = pltpu.with_memory_space_constraint(prepare(band_form), pltpu.HBM)
    kernel, sent = pair_blocks(
        table, vmem(received), band_form, wide, interp_coef, coulomb.reshape(16, 128), vmem(shift_map.reshape(64, 16, 128))
    )
    sent = lax.all_to_all(sent, "kp", 0, 0, tiled=True)
    image = jnp.sum(sent[:, 0:16, :].astype(F32).reshape(64, 8, 128), axis=0) + diagonal * starts

    sums = jnp.sum(lax.all_to_all(second_product(vmem(sent), vmem(to_all(image, "ka"))), "kp", 0, 0, tiled=True), axis=0)
    sums = sums + jnp.concatenate([diagonal * image, jnp.zeros((1, 128), F32)], axis=0)
    everyone = to_all(sums, "kp")
    scale = 1.0 / 8192
    image, corr = middle(vmem(everyone), scale)
    vectors = last(image, vmem(lax.all_to_all(corr, "ka", 0, 0, tiled=True)), scale)
    return (kernel, vectors)


def solution(mesh):
    return jax.shard_map(
        on_device,
        mesh=mesh,
        in_specs=(
            P("ka", None, None),
            P("ka", None, None),
            P("ka", "kp", None),
            P(),
            P(),
            P(),
            P("ka"),
            P("ka", None),
        ),
        out_specs=(P("ka", "kp"), P("ka", None)),
        check_vma=False,
    )
```

```python
import jax
import jax.numpy as jnp
from jax import lax
from jax.experimental import pallas as pl
from jax.experimental.pallas import tpu as pltpu
from jax.sharding import PartitionSpec as P

NV, NC = 8, 16
GRID_Y = 8
GRID_X = 8
BF, F32 = jnp.bfloat16, jnp.float32
HIGH = lax.Precision.HIGHEST
VM = pl.BlockSpec(memory_space=pltpu.VMEM)
SM = pl.BlockSpec(memory_space=pltpu.SMEM)
SMALL = pltpu.CompilerParams(vmem_limit_bytes=16 << 20)


def device_at(axis):
    return lax.axis_index(axis)


def vmem(x):
    return pltpu.with_memory_space_constraint(x, pltpu.VMEM)


def share_kernel(form_hbm, coef_hbm, screen_hbm, start_hbm, energy_hbm, cells_hbm, piece_ref, first_ref, diagonal_ref, table_ref, form, coef, screen_ref, start_ref, energy_ref, cells_ref, sems):
    plane, col = device_at("ka"), device_at("kp")
    odd = (col & 1) == 1
    moves = (
        (cells_hbm, cells_ref),
        (screen_hbm, screen_ref),
        (start_hbm, start_ref),
        (energy_hbm, energy_ref),
        (form_hbm.at[:, :, pl.ds(pl.multiple_of(128 * (col // 2), 128), 128)], form),
        (coef_hbm.at[:, pl.ds(pl.multiple_of(8 * (col // 2), 8), 8), :], coef),
    )
    copies = [pltpu.make_async_copy(src, dst, sems.at[n]) for n, (src, dst) in enumerate(moves)]
    for copy in copies:
        copy.start()
    for copy in copies:
        copy.wait()
    x, y = cells_ref[...] >> 3, cells_ref[...] & 7
    for i in range(4):
        own = lax.broadcasted_iota(jnp.int32, (1, 64), 1) == 4 * plane + i
        cell = jnp.sum(jnp.where(own, cells_ref[...], 0).astype(F32), axis=1, keepdims=True).astype(jnp.int32)
        table_ref[i : i + 1, :] = (((cell >> 3) - x) & 7) * 8 + (((cell & 7) - y) & 7)
    piece_ref[0:64, :] = jnp.concatenate([screen_ref[q].astype(F32) for q in range(4)], axis=0).T.astype(BF)
    block = col // 16
    back = (128 - 8 * (col % 16)) % 128

    def rows_of(parts):
        both = jnp.concatenate([pltpu.roll(part, back, 1) for part in parts], axis=0)
        return both.T[0:8]

    first = rows_of([start_ref[:, pl.ds(pl.multiple_of(256 * h + 128 * block, 128), 128)] for h in range(2)])
    first_ref[...] = first
    diagonal_ref[...] = rows_of([jnp.broadcast_to(energy_ref[pl.ds(2 * h + block, 1), :], (64, 128)) for h in range(2)])
    piece_ref[128:136, :] = first.astype(BF)
    lane = lax.broadcasted_iota(jnp.int32, (24, 128), 1)
    row = lax.broadcasted_iota(jnp.int32, (8, 128), 0)
    for h in range(2):
        a, b = form[2 * h].astype(F32), form[2 * h + 1].astype(F32)
        low = jnp.where(odd, pltpu.roll(a, 64, 1), a)
        high = jnp.where(odd, b, pltpu.roll(b, 64, 1))
        piece_ref[64 + 24 * h : 88 + 24 * h, :] = jnp.where(lane < 64, low, high).astype(BF)
        a, b = coef[2 * h].astype(F32), coef[2 * h + 1].astype(F32)
        low = jnp.where(odd, pltpu.roll(a, 4, 0), a)
        high = jnp.where(odd, b, pltpu.roll(b, 4, 0))
        piece_ref[112 + 8 * h : 120 + 8 * h, :] = jnp.where(row < 4, low, high).astype(BF)


def share(forms, coefs, screen, initial, energies, cells):
    hbm = pl.BlockSpec(memory_space=pltpu.HBM)
    return pl.pallas_call(
        share_kernel,
        in_specs=[hbm] * 6,
        out_specs=(VM, VM, VM, VM),
        out_shape=(
            jax.ShapeDtypeStruct((136, 128), BF),
            jax.ShapeDtypeStruct((8, 128), F32),
            jax.ShapeDtypeStruct((8, 128), F32),
            jax.ShapeDtypeStruct((4, 64), jnp.int32),
        ),
        scratch_shapes=[
            pltpu.VMEM((4, 24, 128), BF),
            pltpu.VMEM((4, 8, 128), BF),
            pltpu.VMEM((4, 32, 64), BF),
            pltpu.VMEM((64, 512), F32),
            pltpu.VMEM((4, 128), F32),
            pltpu.VMEM((1, 64), jnp.int32),
            pltpu.SemaphoreType.DMA((6,)),
        ],
        compiler_params=SMALL,
        name="share",
    )(*(pltpu.with_memory_space_constraint(x, pltpu.HBM) for x in (forms, coefs, screen.transpose(0, 2, 1), initial.T, energies.reshape(4, 128), cells.reshape(1, 64))))


def pick_kernel(t_ref, g_ref, o_ref, rolled):
    def roll_one(h, _):
        x = g_ref[h, 0:64, :].astype(F32)
        rolled[0, h] = x.astype(BF)
        for s in range(1, 4):
            rolled[s, h] = pltpu.roll(x, 32 * s, 1).astype(BF)
        return 0

    lax.fori_loop(0, 16, roll_one, 0, unroll=8)
    lane_block = lax.broadcasted_iota(jnp.int32, (64, 128), 1) // 32

    def dest(d, _):
        for j in range(2):
            acc = None
            for i in range(4):
                q = t_ref[i, 2 * d + j]
                tile = rolled[(i - q) & 3, q >> 2].astype(F32)
                acc = tile if acc is None else jnp.where(lane_block == i, tile, acc)
            o_ref[d, 64 * j : 64 * j + 64, :] = acc.astype(BF)
        half = d & 1
        plane = d >> 1
        o_ref[d, 128:152, :] = g_ref[plane, pl.ds(pl.multiple_of(64 + 24 * half, 8), 24), :]
        o_ref[d, 152:160, :] = g_ref[plane, pl.ds(pl.multiple_of(112 + 8 * half, 8), 8), :]
        o_ref[d, 160:168, :] = g_ref[plane, 128:136, :]
        return 0

    lax.fori_loop(0, 32, dest, 0, unroll=8)


def pick(gathered, table):
    return pl.pallas_call(
        pick_kernel,
        out_shape=jax.ShapeDtypeStruct((32, 168, 128), BF),
        in_specs=[pl.BlockSpec(memory_space=pltpu.SMEM), pl.BlockSpec(memory_space=pltpu.VMEM)],
        out_specs=pl.BlockSpec(memory_space=pltpu.VMEM),
        scratch_shapes=[pltpu.VMEM((4, 16, 64, 128), BF)],
        compiler_params=SMALL,
        name="pick",
    )(table, gathered)


NT = (((1,), (1,)), ((), ()))
TN = (((0,), (0,)), ((), ()))


def prepare_kernel(form_ref, o_ref):
    for c in range(NC):
        o_ref[0, c] = jnp.broadcast_to(form_ref[0, 8 + c : 9 + c, :].astype(F32), (16, 2048)).astype(BF)


def prepare(near):
    return pl.pallas_call(
        prepare_kernel,
        grid=(4,),
        in_specs=[pl.BlockSpec((1, 24, 2048), lambda i: (i, 0, 0))],
        out_specs=pl.BlockSpec((1, 16, 16, 2048), lambda i: (i, 0, 0, 0)),
        out_shape=jax.ShapeDtypeStruct((4, 16, 16, 2048), BF),
        compiler_params=pltpu.CompilerParams(vmem_limit_bytes=32 << 20),
        name="prepare",
    )(near)


def pair_kernel(t_ref, r_ref, near_ref, wide_hbm, coef_ref, coul_ref, map_ref, o_ref, send_ref, far, farc, nearc, cols, cond, val, scaled, acc, right, kt, wide_ref, sems):
    def wide_copy(i):
        return pltpu.make_async_copy(wide_hbm.at[i], wide_ref.at[i], sems.at[i])

    for i in range(4):
        wide_copy(i).start()
    col = device_at("kp")
    lane24 = lax.broadcasted_iota(jnp.int32, (24, 128), 1)
    for m in range(16):
        lo = r_ref[2 * m, 128:152, :].astype(F32)
        hi = r_ref[2 * m + 1, 128:152, :].astype(F32)
        at = (slice(24 * (m // 2), 24 * (m // 2) + 24), slice(128 * (m % 2), 128 * (m % 2) + 128))
        far[(0, *at)] = jnp.where(lane24 < 64, lo, pltpu.roll(hi, 64, 1)).astype(BF)
        far[(1, *at)] = jnp.where(lane24 < 64, pltpu.roll(lo, 64, 1), hi).astype(BF)
    rows = r_ref[:, 152:160, :].reshape(256, 128)
    out_row = lax.broadcasted_iota(jnp.int32, (128, 256), 0)
    in_row = lax.broadcasted_iota(jnp.int32, (128, 256), 1)
    for k in range(2):
        sel = (in_row == (out_row // 4) * 8 + k * 4 + out_row % 4).astype(F32).astype(BF)
        farc[k] = jnp.dot(sel, rows, preferred_element_type=F32).astype(BF)
        cols[k] = r_ref[:, 64 * k : 64 * k + 64, :].reshape(2048, 128).astype(F32).T.astype(BF)
    old = lax.broadcasted_iota(jnp.int32, (128, 128), 1)
    new = lax.broadcasted_iota(jnp.int32, (128, 128), 0)
    order = (old == (new % 8) * 16 + new // 8).astype(F32).astype(BF)
    for i in range(4):
        nearc[i] = lax.dot_general(coef_ref[i], order, (((0,), (1,)), ((), ())), preferred_element_type=F32).astype(BF)

    place = lax.broadcasted_iota(jnp.int32, (256, 128), 0).astype(F32).astype(BF)
    one, zero = jnp.ones((), BF), jnp.zeros((), BF)
    granule = lax.broadcasted_iota(jnp.int32, (8, 128), 1) // 16

    def finish(p):
        j = p // 4
        i = p % 4
        r_hi = right[...].astype(BF)
        r_lo = (right[...] - r_hi.astype(F32)).astype(BF)
        left = acc[64:96, :]
        l_hi = left.astype(BF)
        l_lo = (left - l_hi.astype(F32)).astype(BF)
        low = jnp.dot(r_lo, l_hi, preferred_element_type=F32) + jnp.dot(r_hi, l_lo, preferred_element_type=F32)
        direct = acc[0:64, :] + (jnp.dot(r_hi, l_hi, preferred_element_type=F32) + low)
        tiles = []
        for half in range(2):
            t = [direct[8 * v : 8 * v + 8, 128 * half : 128 * half + 128] for v in range(8)]
            for s in (1, 2, 4):
                upper = (granule & s) != 0
                n = list(t)
                for v in range(8):
                    if not v & s:
                        a, b = t[v], t[v | s]
                        n[v] = jnp.where(upper, pltpu.roll(b, 16 * s, 1), a)
                        n[v | s] = jnp.where(upper, b, pltpu.roll(a, 128 - 16 * s, 1))
                t = n
            tiles += t
        block = jnp.concatenate(tiles, axis=0).astype(BF)
        half = jnp.dot(block, farc[j], preferred_element_type=F32).astype(BF)
        out = jnp.dot(nearc[i], half, preferred_element_type=F32)
        at_i = pl.ds(pl.multiple_of(i * 128, 128), 128)
        at_j = pl.ds(pl.multiple_of(j * 128, 128), 128)
        o_ref[at_i, at_j] = out.astype(BF)
        kt[at_j, at_i] = out.T.astype(BF)

    def pair(p, _):
        @pl.when(p < 4)
        def _():
            wide_copy(p).wait()

        finish(jnp.maximum(p - 1, 0))
        j = p // 4
        i = p % 4
        index = map_ref[t_ref[i, 2 * col + j]]
        scaled[64:96, :] = cols[j, pl.ds(pl.multiple_of(32 * i, 32), 32), :]
        for m in range(16):
            cs = slice(128 * m, 128 * m + 128)
            if m % 2 == 0:
                pick_low = [
                    jnp.where(place == (index[n : n + 1, :] & 255).astype(F32).astype(BF), one, zero) for n in (m, m + 1)
                ]
                both = jnp.dot(far[j], jnp.concatenate(pick_low, axis=1), preferred_element_type=F32)
            high = jnp.broadcast_to(index[m : m + 1, :] >> 8, (24, 128))
            ls = slice(128 * (m % 2), 128 * (m % 2) + 128)
            got = both[0:24, ls]
            for s in range(1, 8):
                got = jnp.where(high == s, both[24 * s : 24 * s + 24, ls], got)
            a = near_ref[i, :, cs].astype(F32)
            m_c = got[8:24, :].astype(BF)
            for c in range(NC):
                cond[16 * c : 16 * c + 16, cs] = wide_ref[i, c, :, cs] * m_c
            a_v = a[0:8, :]
            coul = coul_ref[m : m + 1, :]
            for v in range(0, NV, 2):
                x = jnp.concatenate([a_v * got[v : v + 1, :], a_v * got[v + 1 : v + 2, :]], axis=0).astype(BF)
                val[8 * v : 8 * v + 16, cs] = x
                scaled[8 * v : 8 * v + 16, cs] = (coul * x.astype(F32)).astype(BF)
            if m % 2:
                ks = slice(128 * m - 128, 128 * m + 128)
                part = lax.dot_general(scaled[:, ks], cond[:, ks], NT, preferred_element_type=F32)
                total = part if m == 1 else total + part
        acc[...] = total
        right[...] = lax.dot_general(val[...], scaled[64:96, :], NT, preferred_element_type=F32)
        return 0

    lax.fori_loop(0, 8, pair, 0)
    finish(7)

    odd = (col & 1) == 1
    both = r_ref[:, 160:168, :].reshape(256, 128).astype(F32)
    lane = lax.broadcasted_iota(jnp.int32, (256, 128), 1)
    other = pltpu.roll(both, 64, 1)
    first = jnp.where(lane < 64, jnp.where(odd, other, both), 0.0).astype(BF)
    second = jnp.where(lane < 64, 0.0, jnp.where(odd, both, other)).astype(BF)
    y = jnp.dot(o_ref[0:256, :], first, preferred_element_type=F32)
    y = y + jnp.dot(o_ref[256:512, :], second, preferred_element_type=F32)
    y_hi = y.astype(BF)
    send_ref[:, 0:8, :] = y_hi.reshape(32, 8, 128)
    send_ref[:, 8:16, :] = (y - y_hi.astype(F32)).astype(BF).reshape(32, 8, 128)
    for b in range(4):
        send_ref[:, 16 + 8 * b : 24 + 8 * b, :] = kt[:, 128 * b : 128 * b + 128].reshape(32, 8, 128)


def pair_blocks(table, received, near, wide, coef, coulomb, shift_map):
    return pl.pallas_call(
        pair_kernel,
        in_specs=[SM, VM, VM, pl.BlockSpec(memory_space=pl.ANY), VM, VM, VM],
        out_specs=(VM, VM),
        out_shape=(jax.ShapeDtypeStruct((512, 256), BF), jax.ShapeDtypeStruct((32, 48, 128), BF)),
        scratch_shapes=[
            pltpu.VMEM((2, 192, 256), BF),
            pltpu.VMEM((2, 128, 128), BF),
            pltpu.VMEM((4, 128, 128), BF),
            pltpu.VMEM((2, 128, 2048), BF),
            pltpu.VMEM((256, 2048), BF),
            pltpu.VMEM((64, 2048), BF),
            pltpu.VMEM((96, 2048), BF),
            pltpu.VMEM((96, 256), F32),
            pltpu.VMEM((64, 32), F32),
            pltpu.VMEM((256, 512), BF),
            pltpu.VMEM((4, 16, 16, 2048), BF),
            pltpu.SemaphoreType.DMA((4,)),
        ],
        compiler_params=pltpu.CompilerParams(vmem_limit_bytes=32 << 20),
        name="pairs",
    )(table, received, near, wide, coef, coulomb, shift_map)


def fold_rows(square):
    lane = lax.broadcasted_iota(jnp.int32, (32, 128), 1)
    return jnp.where(lane < 64, square[0:32], pltpu.roll(square[32:64], 64, 1))


def second_kernel(r_ref, x_ref, o_ref):
    lane = lax.broadcasted_iota(jnp.int32, (8, 128), 1)
    parts = []
    for m in range(16):
        x = x_ref[m]
        high = x.astype(BF).astype(F32)
        low = x - high
        parts.append(jnp.where(lane < 64, high, pltpu.roll(low, 64, 1)))
        parts.append(jnp.where(lane < 64, pltpu.roll(high, 64, 1), low))
    x = jnp.concatenate(parts, axis=0)
    xt = x.T.astype(BF)
    sums = []
    for b in range(4):
        g = jnp.dot(xt, r_ref[:, 16 + 8 * b : 24 + 8 * b, :].reshape(256, 128), preferred_element_type=F32)
        sums.append(g[0:64] + g[64:128])
    for b in range(2):
        y = jnp.concatenate([sums[b], sums[b + 2]], axis=0).T
        o_ref[16 * b : 16 * b + 16, 0:8, :] = y.reshape(16, 8, 128)
    corr = jnp.dot(xt, x.astype(BF), preferred_element_type=F32)
    corr = corr + pltpu.roll(corr, 64, 1)
    corr = fold_rows(corr[0:64] + corr[64:128])
    o_ref[:, 8:9, :] = corr.reshape(32, 1, 128)


def second_product(received, x):
    return pl.pallas_call(
        second_kernel,
        out_shape=jax.ShapeDtypeStruct((32, 9, 128), F32),
        in_specs=[VM, VM],
        out_specs=VM,
        compiler_params=SMALL,
        name="second",
    )(received, x)


def pack_symmetric(square):
    lane = lax.broadcasted_iota(jnp.int32, (32, 128), 1)
    row = lax.broadcasted_iota(jnp.int32, (32, 128), 0)
    corner = pltpu.roll(square[32:64], 96, 1)
    values = jnp.where(lane < row, corner, square[0:32])
    diagonal = jnp.sum(jnp.where(lane == row, corner, 0.0), axis=0, keepdims=True)
    values = jnp.where(lane[0:16] < 64, values[0:16], pltpu.roll(values[16:32], 64, 1))
    high = values.astype(BF).astype(F32)
    tail = jnp.broadcast_to(diagonal, (8, 128))
    tail_high = tail.astype(BF).astype(F32)
    tail = jnp.where(row[0:8] == 0, tail_high, jnp.where(row[0:8] == 1, tail - tail_high, 0.0))
    return jnp.concatenate([high, values - high, tail], axis=0).astype(BF)


def unpack_symmetric(parts):
    lane = lax.broadcasted_iota(jnp.int32, (32, 128), 1)
    row = lax.broadcasted_iota(jnp.int32, (32, 128), 0)
    values = parts[0:16] + parts[16:32]
    values = jnp.concatenate([values, pltpu.roll(values, 64, 1)], axis=0)
    diagonal = jnp.broadcast_to(pltpu.roll(parts[32:40], 32, 1)[0:1] + pltpu.roll(parts[32:40], 32, 1)[1:2], (32, 128))
    top = jnp.where(lane < row, 0.0, jnp.where(lane == row, 0.5 * values, values))
    top = jnp.where(lane < 64, top, 0.0)
    low = pltpu.roll(values, 32, 1)
    low = jnp.where(lane - 32 < row, low, jnp.where(lane - 32 == row, 0.5 * diagonal, 0.0))
    low = jnp.where(lane < 32, 0.0, low)
    half = jnp.concatenate([top, low, jnp.zeros((64, 128), F32)], axis=0)
    return half[0:64] + half.T[0:64]


def unfold_rows(packed):
    return jnp.concatenate([packed, pltpu.roll(packed, 64, 1)], axis=0)


def inverse_factor(full, scale):
    lane = lax.broadcasted_iota(jnp.int32, (64, 128), 1)
    row = lax.broadcasted_iota(jnp.int32, (64, 128), 0)
    work = jnp.where(lane < 64, full * scale, (lane - 64 == row).astype(F32))
    done = []
    tiles = [work[8 * t : 8 * t + 8] for t in range(8)]
    for t in range(8):
        column = {u: [jnp.broadcast_to(tiles[u][:, 8 * t + k : 8 * t + k + 1], (8, 128)) for k in range(8)] for u in range(t, 8)}
        for k in range(8):
            pivot = column[t][k][k : k + 1, :]
            y = lax.rsqrt(pivot)
            square = y * y
            near_one = pivot * square
            inverse = square * (2.0 - near_one)
            line = tiles[t][k : k + 1, :]
            done.append(line * (y * (1.5 - 0.5 * near_one)))
            line = line * inverse
            ahead = {m: column[t][m][k : k + 1, :] * inverse for m in range(k + 1, 8)}
            for u in range(t, 8):
                factor = column[u][k]
                for m in range(k + 1, 8):
                    column[u][m] = column[u][m] - factor * ahead[m]
                tiles[u] = tiles[u] - factor * line
    return jnp.concatenate(done, axis=0)


def lane_halves(inv):
    lane = lax.broadcasted_iota(jnp.int32, (64, 128), 1)
    return jnp.where(lane < 64, pltpu.roll(inv, 64, 1), 0.0), jnp.where(lane < 64, 0.0, inv)


def apply_inverse(x, inv):
    both = jnp.concatenate(lane_halves(inv), axis=0)
    return lax.dot_general(x, both, NT, precision=HIGH, preferred_element_type=F32)


def middle_kernel(g_ref, image_ref, corr_ref, *, scale):
    packed = g_ref[:, 8:9, :].reshape(32, 128)
    inv = inverse_factor(unfold_rows(packed), scale)
    image = apply_inverse(g_ref[:, 0:8, :].reshape(256, 128), inv)
    image_ref[...] = image
    corr = lax.dot_general(image, image, TN, precision=HIGH, preferred_element_type=F32)
    corr = corr[0:64] + pltpu.roll(corr[64:128], 64, 1)
    corr = pack_symmetric(corr)
    for m in range(16):
        corr_ref[m] = corr


def middle(g, scale):
    return pl.pallas_call(
        lambda *refs: middle_kernel(*refs, scale=scale),
        out_shape=(jax.ShapeDtypeStruct((256, 128), F32), jax.ShapeDtypeStruct((16, 40, 128), BF)),
        in_specs=[VM],
        out_specs=(VM, VM),
        compiler_params=SMALL,
        name="middle",
    )(g)


def last_kernel(image_ref, corr_ref, o_ref, *, scale):
    parts = corr_ref[0].astype(F32)
    for m in range(1, 16):
        parts = parts + corr_ref[m].astype(F32)
    inv = inverse_factor(unpack_symmetric(parts), scale)
    upper, lower = lane_halves(inv)
    image = image_ref[...]
    o_ref[:, 0:256] = lax.dot_general(upper, image, NT, precision=HIGH, preferred_element_type=F32)
    o_ref[:, 256:512] = lax.dot_general(lower, image, NT, precision=HIGH, preferred_element_type=F32)


def last(image, corr, scale):
    return pl.pallas_call(
        lambda *refs: last_kernel(*refs, scale=scale),
        out_shape=jax.ShapeDtypeStruct((64, 512), F32),
        in_specs=[VM, VM],
        out_specs=VM,
        compiler_params=SMALL,
        name="last",
    )(image, corr).T


def to_all(x, axis):
    size = lax.axis_size(axis)
    return lax.all_to_all(jnp.broadcast_to(x[None], (size, *x.shape)), axis, 0, 0, tiled=True)


def on_device(band_form, interp_coef, screen, coulomb, shift_map, grid_order, energies, initial):
    piece, starts, diagonal, table = share(band_form, interp_coef, screen, initial, energies, grid_order)
    gathered = lax.all_gather(piece, "ka", axis=0, tiled=False)
    received = lax.all_to_all(pick(vmem(gathered), table), "kp", 0, 0, tiled=True)
    wide = pltpu.with_memory_space_constraint(prepare(band_form), pltpu.HBM)
    kernel, sent = pair_blocks(
        table, vmem(received), band_form, wide, interp_coef, coulomb.reshape(16, 128), vmem(shift_map.reshape(64, 16, 128))
    )
    sent = lax.all_to_all(sent, "kp", 0, 0, tiled=True)
    image = jnp.sum(sent[:, 0:16, :].astype(F32).reshape(64, 8, 128), axis=0) + diagonal * starts

    sums = jnp.sum(lax.all_to_all(second_product(vmem(sent), vmem(to_all(image, "ka"))), "kp", 0, 0, tiled=True), axis=0)
    sums = sums + jnp.concatenate([diagonal * image, jnp.zeros((1, 128), F32)], axis=0)
    everyone = to_all(sums, "kp")
    scale = 1.0 / 8192
    image, corr = middle(vmem(everyone), scale)
    vectors = last(image, vmem(lax.all_to_all(corr, "ka", 0, 0, tiled=True)), scale)
    return (kernel, vectors)


def solution(mesh):
    return jax.shard_map(
        on_device,
        mesh=mesh,
        in_specs=(
            P("ka", None, None),
            P("ka", None, None),
            P("ka", "kp", None),
            P(),
            P(),
            P(),
            P("ka"),
            P("ka", None),
        ),
        out_specs=(P("ka", "kp"), P("ka", None)),
        check_vma=False,
    )
```
